32 devices in a mesh: parts: 2 (over y), row: 4 (over z), col: 2 (over x), cores: 2 (over core).
Axes of the slice: x: 2, y: 2, z: 4, core: 2. Of those that a mesh axis runs over, the one named last changes fastest.
Arguments:
- latent: float32 [128, 256, 128], P(('parts', 'row', 'cores'), 'col'), parts along dimension 0, may hold values from -6 to 6
- moment_one: float32 [128, 256, 128], P(('parts', 'row', 'cores'), 'col'), parts along dimension 0, may hold values from -0.3 to 0.3
- moment_two: float32 [128, 256, 128], P(('parts', 'row', 'cores'), 'col'), parts along dimension 0, may hold values from 0.001 to 0.01
- hole_mask: int32 [128, 256], P(('parts', 'row', 'cores'), 'col'), parts along dimension 0, may hold values 0 or 1
- target_rgb: float32 [3, 128, 256], P(None, ('parts', 'row', 'cores'), 'col'), parts along dimension 1, may hold values from -4 to 4
- kernel_one: bfloat16 [3, 3, 128, 128], replicated, may hold values from -0.1875 to 0.1875
- bias_one: float32 [128], replicated, may hold values from -3 to 3
- kernel_two: bfloat16 [3, 3, 128, 128], replicated, may hold values from -0.1875 to 0.1875
- bias_two: float32 [128], replicated, may hold values from -3 to 3
- rgb_weight: bfloat16 [3, 128], replicated, may hold values from -0.5 to 0.5
Outputs:
- latent_out: float32 [128, 256, 128], P(('parts', 'row', 'cores'), 'col'), parts along dimension 0
- moment_one_out: float32 [128, 256, 128], P(('parts', 'row', 'cores'), 'col'), parts along dimension 0
- moment_two_out: float32 [128, 256, 128], P(('parts', 'row', 'cores'), 'col'), parts along dimension 0
The draws below stay inside these ranges and needn't reach their ends.
There are 2 independent parts, one for each index of `parts`. The reference program is written for one: setup_inputs(seed, part) draws one part's arguments, and reference() takes and returns one part's arrays. A program takes and returns all parts, laid end to end along the dimension named above; an argument that names none is the same for every part. Nothing has to cross between parts.
All inputs are finite; a program needn't handle non-finite values. No bound on the sum of `hole_mask` on one device may be relied on, other than what follows from the above.
Results may differ from the reference program's by a relative error of at most 0.0045.
Values may be sent and summed in bfloat16 or wider, within the bound.
No kernel may reach another device: no remote copies, remote signals or barrier semaphores. Data moves between devices by JAX's collectives and lax.ppermute only.
A program may use at most 64 MiB of HBM per device.

```python
import math
import jax
import jax.numpy as jnp
from jax import lax

C = 128
STEPS = 2
H = 64
W = 256


def touch_ends(array, key, least, largest):
    longest = array.shape.index(max(array.shape))
    spots = []
    for shift in (0, 1):
        where = [jax.random.randint(jax.random.fold_in(key, axis), (), 0, length) for axis, length in enumerate(array.shape)]
        where[longest] = (where[longest] + shift) % array.shape[longest]
        spots.append(tuple(where))
    return array.at[spots[0]].set(least).at[spots[1]].set(largest)


def shard_levels(rng, extent, cuts, least, top_value):
    factor_of, own = 1.0, jax.random.fold_in(rng, 6)
    for position, shards_of in cuts:
        heights = jnp.exp(jax.random.uniform(jax.random.fold_in(own, position), (shards_of,), jnp.float32, least / len(cuts), top_value / len(cuts)))
        factor_of = factor_of * jnp.repeat(heights, extent[position] // shards_of).reshape([-1 if axis == position else 1 for axis in range(len(extent))])
    return factor_of


def noise(key, shape, width, limit, split=(), kind=jnp.bfloat16):
    values = width * jax.random.normal(key, shape, jnp.float32)
    if split:
        values = values * shard_levels(key, shape, split, -0.22, 0.18)
    return jnp.clip(values, -limit, limit).astype(kind)


def setup_inputs(seed: int = 0, part: int = 0) -> dict:
    key_list = jax.random.split(jax.random.key(seed), 11)
    own_keys = jax.random.split(jax.random.fold_in(key_list[10], part), 11)
    return {
        "latent": noise(own_keys[0], (H, W, C), 1.0, 6.0, ((0, 8), (1, 2)), jnp.float32),
        "moment_one": noise(own_keys[1], (H, W, C), 0.05, 0.3, ((0, 8), (1, 2)), jnp.float32),
        "moment_two": jnp.clip(jnp.exp(math.log(0.01) - 2.30258502 * jax.random.uniform(own_keys[2], (H, W, C), jnp.float32) ** shard_levels(own_keys[2], (H, W, C), ((0, 8), (1, 2)), -0.2, 0.2)), 0.001, 0.01),
        "hole_mask": touch_ends((jax.random.randint(own_keys[3], (H, W), 0, 2) < 1).astype(jnp.int32), jax.random.fold_in(own_keys[3], 1), 0, 1),
        "target_rgb": noise(own_keys[4], (3, H, W), 1.0, 4.0, ((1, 8), (2, 2)), jnp.float32),
        "kernel_one": noise(key_list[5], (3, 3, C, C), (9 * C) ** -0.5, 0.1875),
        "bias_one": noise(key_list[6], (C,), 0.5, 3.0, (), jnp.float32),
        "kernel_two": noise(key_list[7], (3, 3, C, C), (9 * C) ** -0.5, 0.1875),
        "bias_two": noise(key_list[8], (C,), 0.5, 3.0, (), jnp.float32),
        "rgb_weight": noise(key_list[9], (3, C), C ** -0.5, 0.5),
    }


BETA_ONE = 0.6
BETA_TWO = 0.9
LEARN_RATE = 0.4
EPSILON = 1e-08

def convolve(padded, kernel, height, breadth, transposed):
    channels = padded.shape[2]
    weights = kernel.astype(jnp.float32)
    summed = None
    for tap_row in range(3):
        for tap_col in range(3):
            if transposed:
                section = padded[2 - tap_row:2 - tap_row + height, 2 - tap_col:2 - tap_col + breadth]
                matrix = weights[tap_row, tap_col].T
            else:
                section = padded[tap_row:tap_row + height, tap_col:tap_col + breadth]
                matrix = weights[tap_row, tap_col]
            product = jnp.dot(section.reshape(height * breadth, channels).astype(jnp.float32), matrix, precision=lax.Precision.HIGHEST, preferred_element_type=jnp.float32)
            summed = product if summed is None else summed + product
    return summed.reshape(height, breadth, -1)

def padding(field):
    return jnp.pad(field, ((1, 1), (1, 1), (0, 0)))

def silu_slope(value):
    sigma = jax.nn.sigmoid(value)
    return sigma * (1.0 + value * (1.0 - sigma))

def reference(latent, moment_one, moment_two, hole_mask, target_rgb, kernel_one, bias_one, kernel_two, bias_two, rgb_weight):
    height, breadth = (latent.shape[0], latent.shape[1])
    current, first, second = (latent, moment_one, moment_two)
    known = hole_mask.astype(jnp.float32)
    projection = rgb_weight.astype(jnp.float32)
    for iteration in range(STEPS):
        rounded = current.astype(jnp.bfloat16)
        pre_one = convolve(padding(rounded), kernel_one, height, breadth, False) + bias_one
        hidden_one = jax.nn.silu(pre_one).astype(jnp.bfloat16)
        pre_two = convolve(padding(hidden_one), kernel_two, height, breadth, False) + bias_two
        hidden_two = jax.nn.silu(pre_two).astype(jnp.bfloat16)
        color = jnp.einsum('yxc,kc->kyx', hidden_two.astype(jnp.float32), projection, precision=lax.Precision.HIGHEST)
        residual = known[None] * (color - target_rgb)
        grad_hidden = jnp.einsum('kyx,kc->yxc', residual, projection, precision=lax.Precision.HIGHEST)
        grad_two = (grad_hidden * silu_slope(pre_two)).astype(jnp.bfloat16)
        grad_inner = convolve(padding(grad_two), kernel_two, height, breadth, True)
        grad_one = (grad_inner * silu_slope(pre_one)).astype(jnp.bfloat16)
        gradient = convolve(padding(grad_one), kernel_one, height, breadth, True)
        first = BETA_ONE * first + (1.0 - BETA_ONE) * gradient
        second = BETA_TWO * second + (1.0 - BETA_TWO) * gradient * gradient
        current = current - LEARN_RATE * first / (jnp.sqrt(second) + EPSILON)
    return (current, first, second)
```

```python
import functools
import math

import jax
import jax.numpy as jnp
from jax import lax
from jax.experimental import pallas as pl
from jax.experimental.pallas import tpu as pltpu
from jax.sharding import PartitionSpec as P

STEPS = 2

BETA_ONE = 0.6
BETA_TWO = 0.9
LEARN_RATE = 0.4
EPSILON = 1e-08

ROWS = ("row", "cores")
STRIPS = 16
SIDE = 8
EDGE = 4
PLANES = 7
VMEM = pl.BlockSpec(memory_space=pltpu.VMEM)
ANY = pl.BlockSpec(memory_space=pl.ANY)
F32 = jnp.float32
BF16 = jnp.bfloat16


def row_place():
    cores = lax.axis_size("cores")
    return lax.axis_index("row") * cores + lax.axis_index("cores")


def pairs(count, parity):
    chosen = []
    for low in range(parity, count - 1, 2):
        chosen += [(low, low + 1), (low + 1, low)]
    return chosen


def swap(block, axes, parity):
    return lax.ppermute(block, axes, pairs(lax.axis_size(axes), parity))


def call(kernel, out_shape, in_specs, out_specs, scratch, cost, name):
    return pl.pallas_call(
        kernel,
        out_shape=out_shape,
        in_specs=in_specs,
        out_specs=out_specs,
        scratch_shapes=scratch,
        compiler_params=pltpu.CompilerParams(vmem_limit_bytes=24 << 20),
        cost_estimate=pl.CostEstimate(flops=cost[0], bytes_accessed=cost[1], transcendentals=0),
        name=name,
    )


def shape(dims, dtype):
    return jax.ShapeDtypeStruct(dims, dtype)


def pack_rows(latent, target, mask, near, far, turned, held, planes, sem):
    height = latent.shape[0]
    copy = pltpu.make_async_copy(latent, held, sem)
    copy.start()
    known = mask[...].astype(F32)
    planes[...] = jnp.zeros_like(planes)
    for color in range(3):
        wanted = known * target[color]
        high = wanted.astype(BF16).astype(F32)
        planes[pl.ds(color, height, stride=PLANES), :] = high
        planes[pl.ds(color + 3, height, stride=PLANES), :] = wanted - high
    planes[pl.ds(6, height, stride=PLANES), :] = known
    flat = planes[...].T.astype(BF16)
    turned[...] = flat
    near[EDGE] = flat
    far[EDGE] = flat
    copy.wait()
    even = lax.rem(row_place(), 2) == 0
    last = height - EDGE
    near[:EDGE] = held[pl.ds(jnp.where(even, last, 0), EDGE)].astype(BF16)
    far[:EDGE] = held[pl.ds(jnp.where(even, 0, last), EDGE)].astype(BF16)


def pack_columns(sides, latent, first, second, near, far, turned, *rest):
    outs, (held, flat, sem) = rest[:sides], rest[sides:]
    height, breadth = latent.shape[0], latent.shape[1]
    copies = []
    for number, source in enumerate((latent, first, second)):
        for end, start in enumerate((0, breadth - SIDE)):
            copy = pltpu.make_async_copy(
                source.at[:, pl.ds(start, SIDE)], held.at[number, end], sem.at[number, end]
            )
            copy.start()
            copies.append(copy)
    row_even = lax.rem(row_place(), 2) == 0
    col_even = lax.rem(lax.axis_index("col"), 2) == 0
    starts = (0, breadth - SIDE)
    near_ends = [near[:, s : s + SIDE].astype(F32) for s in starts]
    far_ends = [far[:, s : s + SIDE].astype(F32) for s in starts]
    own_ends = [turned[s : s + SIDE].astype(F32) for s in starts]
    for copy in copies:
        copy.wait()
    full = height + 2 * EDGE
    for side, out in enumerate(outs):
        right = col_even if side == 0 else jnp.logical_not(col_even)
        pick = lambda ends: jnp.where(right, ends[1], ends[0])
        close, away = pick(near_ends), pick(far_ends)
        above = jnp.where(row_even, away, close)
        below = jnp.where(row_even, close, away)
        middle = pick([held[0, end] for end in range(2)])
        flat[: EDGE * SIDE] = above[:EDGE].reshape(EDGE * SIDE, -1)
        flat[EDGE * SIDE : (EDGE + height) * SIDE] = middle.reshape(height * SIDE, -1)
        flat[(EDGE + height) * SIDE : full * SIDE] = below[:EDGE].reshape(EDGE * SIDE, -1)
        at = full * SIDE
        for piece in (above[EDGE], pick(own_ends), below[EDGE]):
            flat[at : at + SIDE] = piece
            at += SIDE
        flat[at : at + SIDE] = jnp.zeros_like(own_ends[0])
        at += SIDE
        low = middle - middle.astype(BF16).astype(F32)
        for piece in (low, pick([held[1, e] for e in range(2)]), pick([held[2, e] for e in range(2)])):
            for row in range(height):
                nearest = jnp.where(right, piece[row, SIDE - EDGE :], piece[row, :EDGE])
                flat[at : at + EDGE] = nearest
                at += EDGE
        out[...] = flat[...].astype(BF16)


def packed_length(height):
    return (height + 2 * EDGE) * SIDE + 4 * SIDE + 3 * height * EDGE


def pack_weights(one, two, rgb, ahead_one, ahead_two, back_one, back_two, colors, held):
    size = one.shape[2]
    for kernel, ahead, back in ((one, ahead_one, back_one), (two, ahead_two, back_two)):
        for row in range(4):
            for col in range(3):
                at = (row * 3 + col) * size
                for out in range(2):
                    tap = row - out
                    if 0 <= tap <= 2:
                        front = kernel[tap, col]
                        rear = kernel[2 - tap, 2 - col].astype(F32).T.astype(BF16)
                    else:
                        front = rear = jnp.zeros((size, size), BF16)
                    ahead[at : at + size, out * size : (out + 1) * size] = front
                    back[at : at + size, out * size : (out + 1) * size] = rear
    held[...] = jnp.zeros_like(held)
    held[0:3] = rgb[...].astype(F32)
    held[3:6] = rgb[...].astype(F32)
    colors[...] = held[...].astype(BF16)


def put(dest, row, value, strip):
    dest[row, 1 : strip + 1] = value.astype(BF16).reshape(strip, STRIPS, -1)
    dest[row, 0] = pltpu.roll(value[(strip - 1) * STRIPS :], 1, 0).astype(BF16)
    dest[row, strip + 1] = pltpu.roll(value[:STRIPS], STRIPS - 1, 0).astype(BF16)


def conv_pair(source, row, weights, strip):
    taps = [
        source[row + down, across : across + strip].reshape(strip * STRIPS, -1)
        for down in range(4)
        for across in range(3)
    ]
    return jnp.dot(jnp.concatenate(taps, axis=1), weights[...], preferred_element_type=F32)


def strips_of(source, row, strip):
    return jnp.concatenate(
        [source[row, pl.ds(j, STRIPS, stride=strip), :] for j in range(strip)], axis=0
    )


def sigma_of(value):
    return 0.5 * jnp.tanh(0.5 * value) + 0.5


def gradient(height, strip, refs, weights, aims, known, inside, emit):
    wide, hidden, slope, grad_two, grad_one = refs
    ahead_one, ahead_two, back_one, back_two, colors, bias_one, bias_two = weights
    size = wide.shape[-1]
    place, count = row_place(), lax.axis_size("row") * lax.axis_size("cores")
    top = (place > 0).astype(F32)
    bottom = (place < count - 1).astype(F32)
    columns = inside[...]
    halves = lambda both: (both[:, :size], both[:, size:])
    pixels = strip * STRIPS

    for pair in range((height + 6) // 2):
        for half, summed in enumerate(halves(conv_pair(wide, 2 * pair, ahead_one, strip))):
            row = 2 * pair + half
            value = summed + bias_one[...]
            sigma = sigma_of(value)
            hid = value * sigma
            keep = columns
            if row < 3:
                keep = columns * top
            elif row >= height + 3:
                keep = columns * bottom
            put(hidden, row, hid * keep, strip)
            if 2 <= row < height + 4:
                slope[row - 2] = (sigma + hid * (1.0 - sigma)) * keep

    lane = lax.broadcasted_iota(jnp.int32, (2 * pixels, size), 1)
    for pair in range((height + 4) // 2):
        both = conv_pair(hidden, 2 * pair, ahead_two, strip)
        value = jnp.concatenate(halves(both), axis=0) + bias_two[...]
        sigma = sigma_of(value)
        hid = value * sigma
        color = lax.dot_general(
            hid.astype(BF16), colors[...], (((1,), (1,)), ((), ())), preferred_element_type=F32
        )
        spot = slice(2 * pair, 2 * pair + 2)
        residual = known[spot].reshape(2 * pixels, -1) * color - aims[spot].reshape(2 * pixels, -1)
        rest = residual - residual.astype(BF16).astype(F32)
        split = jnp.where(lane < 3, residual, rest).astype(BF16)
        spread = jnp.dot(split, colors[...], preferred_element_type=F32)
        result = spread * (sigma + hid * (1.0 - sigma))
        for half in range(2):
            put(grad_two, 2 * pair + half, result[half * pixels : (half + 1) * pixels], strip)

    for pair in range((height + 2) // 2):
        for half, summed in enumerate(halves(conv_pair(grad_two, 2 * pair, back_two, strip))):
            row = 2 * pair + half
            put(grad_one, row, summed * slope[row], strip)

    for pair in range(height // 2):
        for half, summed in enumerate(halves(conv_pair(grad_one, 2 * pair, back_one, strip))):
            emit(2 * pair + half, summed)


def adam(current, first, second, grad):
    first = BETA_ONE * first + (1.0 - BETA_ONE) * grad
    second = BETA_TWO * second + (1.0 - BETA_TWO) * grad * grad
    return current - LEARN_RATE * first / (jnp.sqrt(second) + EPSILON), first, second


def first_step(sides, *refs):
    latent, moment_one, moment_two, near, far, turned = refs[:6]
    columns = refs[6 : 6 + sides]
    refs = refs[6 + sides :]
    weights, refs = refs[:7], refs[7:]
    (own, near_out, far_out, z_out, m_out, v_out, aims, known, inside), refs = refs[:9], refs[9:]
    z_held, m_held, v_held, flat, turn, wide, hidden, slope, grad_two, grad_one, sem = refs
    height, breadth, size = latent.shape
    strip = (breadth + 2 * SIDE) // STRIPS
    pixels = strip * STRIPS
    full = height + 2 * EDGE

    copies = []
    for number, (source, dest) in enumerate(
        (
            (latent, z_held.at[pl.ds(EDGE, height), pl.ds(SIDE, breadth)]),
            (moment_one, m_held.at[:, pl.ds(SIDE, breadth)]),
            (moment_two, v_held.at[:, pl.ds(SIDE, breadth)]),
        )
    ):
        copy = pltpu.make_async_copy(source, dest, sem.at[number])
        copy.start()
        copies.append(copy)

    place, col = row_place(), lax.axis_index("col")
    row_even, col_even = lax.rem(place, 2) == 0, lax.rem(col, 2) == 0

    base = col * breadth - SIDE
    total = lax.axis_size("col") * breadth
    for j in range(strip):
        at = lax.broadcasted_iota(jnp.int32, (STRIPS, size), 0) * strip + (j + base)
        inside[j * STRIPS : (j + 1) * STRIPS] = ((at >= 0) & (at < total)).astype(F32)

    for source, low in ((near, row_even), (far, jnp.logical_not(row_even))):
        start = jnp.where(low, height + EDGE, 0)
        z_held[pl.ds(start, EDGE), SIDE : SIDE + breadth] = source[:EDGE].astype(F32)
        turn[jnp.where(low, 2, 0), SIDE : SIDE + breadth] = source[EDGE].astype(F32)
    turn[1, SIDE : SIDE + breadth] = turned[...].astype(F32)

    for side in range(2):
        right = col_even if side == 0 else jnp.logical_not(col_even)
        start = pl.multiple_of(jnp.where(right, SIDE + breadth, 0), SIDE)
        spot = pl.ds(start, SIDE)
        if side >= sides:
            for held in (z_held, m_held, v_held, turn):
                held[:, spot] = jnp.zeros((held.shape[0], SIDE, size), F32)
            continue
        flat[...] = columns[side][...].astype(F32)
        z_held[:, spot] = flat[: full * SIDE].reshape(full, SIDE, size)
        at = full * SIDE
        turn[:, spot] = flat[at : at + 3 * SIDE].reshape(3, SIDE, size)
        at += 4 * SIDE
        blank = jnp.zeros((SIDE - EDGE, size), F32)
        for number, held in enumerate((z_held, m_held, v_held)):
            for row in range(height):
                piece = flat[at : at + EDGE]
                at += EDGE
                piece = jnp.where(
                    right,
                    jnp.concatenate([piece, blank], axis=0),
                    jnp.concatenate([blank, piece], axis=0),
                )
                if number == 0:
                    held[EDGE + row, spot] += piece
                else:
                    held[row, spot] = piece

    lane_in = lax.broadcasted_iota(jnp.int32, (size, 2 * size), 0)
    lane_out = lax.broadcasted_iota(jnp.int32, (size, 2 * size), 1)
    color = lax.rem(lane_out, 3)
    aimed = (lane_out < 6) & ((lane_in == color) | (lane_in == color + 3))
    masked = (lane_out >= size) & (lane_out < size + 6) & (lane_in == 6)
    chosen = (aimed | masked).astype(F32).astype(BF16)
    turned_strips = [strips_of(turn, slot, strip) for slot in range(3)]
    for row in range(height + 4):
        slot, source = (0, height - 2 + row) if row < 2 else (1, row - 2)
        if row >= height + 2:
            slot, source = 2, row - height - 2
        value = turned_strips[slot]
        if source:
            value = pltpu.roll(value, size - PLANES * source, 1)
        both = jnp.dot(value.astype(BF16), chosen, preferred_element_type=F32)
        aims[row] = both[:, :size]
        known[row] = both[:, size:]

    copies[0].wait()
    for row in range(full):
        put(wide, row, strips_of(z_held, row, strip), strip)
    copies[1].wait()
    copies[2].wait()

    def emit(row, grad):
        current, first, second = adam(
            strips_of(z_held, EDGE + row, strip),
            strips_of(m_held, row, strip),
            strips_of(v_held, row, strip),
            grad,
        )
        current = current * inside[...]
        z_out[row] = current
        m_out[row] = first
        v_out[row] = second
        put(own, row, current, strip)

    gradient(
        height, strip, (wide, hidden, slope, grad_two, grad_one), weights, aims, known, inside, emit
    )
    last = height - EDGE
    near_out[...] = own[pl.ds(jnp.where(row_even, last, 0), EDGE)]
    far_out[...] = own[pl.ds(jnp.where(row_even, 0, last), EDGE)]


def last_step(*refs):
    own, near, far, z_in, m_in, v_in, aims, known, inside = refs[:9]
    weights, refs = refs[9:16], refs[16:]
    (z_out, m_out, v_out), refs = refs[:3], refs[3:]
    z_held, m_held, v_held, wide, hidden, slope, grad_two, grad_one, sem = refs
    height, breadth, size = z_out.shape
    strip = (breadth + 2 * SIDE) // STRIPS
    row_even = lax.rem(row_place(), 2) == 0
    wide[EDGE : EDGE + height] = own[...]
    wide[pl.ds(jnp.where(row_even, height + EDGE, 0), EDGE)] = near[...]
    wide[pl.ds(jnp.where(row_even, 0, height + EDGE), EDGE)] = far[...]
    copies = []

    def emit(row, grad):
        results = adam(z_in[row], m_in[row], v_in[row], grad)
        for number, (held, out, value) in enumerate(
            zip((z_held, m_held, v_held), (z_out, m_out, v_out), results)
        ):
            for j in range(strip):
                held[row, pl.ds(j, STRIPS, stride=strip), :] = value[
                    j * STRIPS : (j + 1) * STRIPS
                ]
            copy = pltpu.make_async_copy(
                held.at[row, pl.ds(SIDE, breadth)], out.at[row], sem.at[number, row]
            )
            copy.start()
            copies.append(copy)

    gradient(
        height, strip, (wide, hidden, slope, grad_two, grad_one), weights, aims, known, inside, emit
    )
    for copy in copies:
        copy.wait()


def body(
    latent,
    moment_one,
    moment_two,
    hole_mask,
    target_rgb,
    kernel_one,
    bias_one,
    kernel_two,
    bias_two,
    rgb_weight,
):
    height, breadth, size = latent.shape
    strip = (breadth + 2 * SIDE) // STRIPS
    assert strip * STRIPS == breadth + 2 * SIDE and height % 2 == 0
    assert height * PLANES <= size and breadth == size
    pixels = strip * STRIPS
    full = height + 2 * EDGE
    sides = 1 if lax.axis_size("col") == 2 else 2
    length = packed_length(height)
    dma = pltpu.SemaphoreType.DMA

    near, far, turned = call(
        pack_rows,
        [shape((EDGE + 1, breadth, size), BF16)] * 2 + [shape((breadth, size), BF16)],
        [ANY, VMEM, VMEM],
        [VMEM] * 3,
        [pltpu.VMEM((height, breadth, size), F32), pltpu.VMEM((size, breadth), F32), dma],
        (10**6, 10**6),
        "pack_rows",
    )(latent, target_rgb, hole_mask)
    near = swap(near, ROWS, 0)
    far = swap(far, ROWS, 1)

    matrix = shape((12 * size, 2 * size), BF16)
    packed = call(
        pack_weights,
        [matrix] * 4 + [shape((size, size), BF16)],
        [VMEM] * 3,
        [VMEM] * 5,
        [pltpu.VMEM((size, size), F32)],
        (10**6, 4 * 10**6),
        "pack_weights",
    )(kernel_one, kernel_two, rgb_weight)
    weights = (*packed, bias_one[None], bias_two[None])

    columns = call(
        functools.partial(pack_columns, sides),
        [shape((length, size), BF16)] * sides,
        [ANY] * 3 + [VMEM] * 3,
        [VMEM] * sides,
        [pltpu.VMEM((3, 2, height, SIDE, size), F32), pltpu.VMEM((length, size), F32), dma((3, 2))],
        (10**5, 10**5),
        "pack_columns",
    )(latent, moment_one, moment_two, near, far, turned)
    columns = [swap(block, "col", side) for side, block in enumerate(columns)]

    work = 4 * 2 * 12 * 11 * pixels * size * size
    tall = lambda rows: pltpu.VMEM((rows, strip + 2, STRIPS, size), BF16)
    scratch = [
        tall(full),
        tall(height + 6),
        pltpu.VMEM((height + 2, pixels, size), F32),
        tall(height + 4),
        tall(height + 2),
    ]
    held = pltpu.VMEM((height, pixels, size), F32)
    half = shape((EDGE, strip + 2, STRIPS, size), BF16)
    lines = shape((height, pixels, size), F32)
    aims = shape((height + 4, pixels, size), F32)
    own, near, far, z, m, v, aims, known, inside = call(
        functools.partial(first_step, sides),
        [shape((height, strip + 2, STRIPS, size), BF16), half, half, lines, lines, lines]
        + [aims, aims, shape((pixels, size), F32)],
        [ANY] * 3 + [VMEM] * (3 + sides + 7),
        [VMEM] * 9,
        [pltpu.VMEM((full, pixels, size), F32), held, held, pltpu.VMEM((length, size), F32)]
        + [pltpu.VMEM((3, pixels, size), F32)]
        + scratch
        + [dma((3,))],
        (work, 10**7),
        "first_step",
    )(latent, moment_one, moment_two, near, far, turned, *columns, *weights)
    near = swap(near, ROWS, 0)
    far = swap(far, ROWS, 1)

    out = shape(latent.shape, F32)
    return call(
        last_step,
        [out] * 3,
        [VMEM] * 16,
        [ANY] * 3,
        [held] * 3 + scratch + [dma((3, height))],
        (work, 10**7),
        "last_step",
    )(own, near, far, z, m, v, aims, known, inside, *weights)


def solution(mesh):
    tile = P(("parts", "row", "cores"), "col", None)
    return jax.shard_map(
        body,
        mesh=mesh,
        in_specs=(
            tile,
            tile,
            tile,
            P(("parts", "row", "cores"), "col"),
            P(None, ("parts", "row", "cores"), "col"),
            P(),
            P(),
            P(),
            P(),
            P(),
        ),
        out_specs=(tile, tile, tile),
        check_vma=False,
    )
```

```python
import functools
import math

import jax
import jax.numpy as jnp
from jax import lax
from jax.experimental import pallas as pl
from jax.experimental.pallas import tpu as pltpu
from jax.sharding import PartitionSpec as P

STEPS = 2

BETA_ONE = 0.6
BETA_TWO = 0.9
LEARN_RATE = 0.4
EPSILON = 1e-08

ROWS = ("row", "cores")
STRIPS = 16
SIDE = 8
EDGE = 4
PLANES = 7
VMEM = pl.BlockSpec(memory_space=pltpu.VMEM)
HBM = pl.BlockSpec(memory_space=pltpu.HBM)
F32 = jnp.float32
BF16 = jnp.bfloat16


def row_place():
    cores = lax.axis_size("cores")
    return lax.axis_index("row") * cores + lax.axis_index("cores")


def pairs(count, parity):
    chosen = []
    for low in range(parity, count - 1, 2):
        chosen += [(low, low + 1), (low + 1, low)]
    return chosen


def swap(block, axes, parity):
    return lax.ppermute(block, axes, pairs(lax.axis_size(axes), parity))


def call(kernel, out_shape, in_specs, out_specs, scratch, cost, name, aliases=None):
    return pl.pallas_call(
        kernel,
        out_shape=out_shape,
        in_specs=in_specs,
        out_specs=out_specs,
        scratch_shapes=scratch,
        compiler_params=pltpu.CompilerParams(vmem_limit_bytes=24 << 20),
        cost_estimate=pl.CostEstimate(flops=cost[0], bytes_accessed=cost[1], transcendentals=0),
        input_output_aliases=aliases or {},
        name=name,
    )


def shape(dims, dtype):
    return jax.ShapeDtypeStruct(dims, dtype)


def pick_row(index, height):
    odd = lax.rem(row_place(), 2) == 1
    return jnp.where(odd, height - 1 - index, index)


def pick_partner_row(index, height):
    odd = lax.rem(row_place(), 2) == 1
    return jnp.where(odd, index, height - 1 - index)


def piece_counts(height):
    return height, height + 2, height * EDGE // SIDE


def pack_columns(sides, latent, first, second, target, mask, *rest):
    outs, rest = rest[:sides], rest[sides:]
    turned, ends, aim, known, planes, flat, sem = rest
    height, breadth = latent.shape[0], latent.shape[1]
    copies = []
    for number, source in enumerate((latent, first, second)):
        for end, start in enumerate((0, breadth - SIDE)):
            copy = pltpu.make_async_copy(
                source.at[:, pl.ds(start, SIDE)], ends.at[number, end], sem.at[number, end]
            )
            copy.start()
            copies.append(copy)
    early = [
        pltpu.make_async_copy(target, aim, sem.at[3, 0]),
        pltpu.make_async_copy(mask, known, sem.at[3, 1]),
    ]
    for copy in early:
        copy.start()
    planes[...] = jnp.zeros_like(planes)
    for copy in early:
        copy.wait()
    keep = known[...].astype(F32)
    for color in range(3):
        wanted = keep * aim[color]
        high = wanted.astype(BF16).astype(F32)
        planes[pl.ds(color, height, stride=PLANES), :] = high
        planes[pl.ds(color + 3, height, stride=PLANES), :] = wanted - high
    planes[pl.ds(6, height, stride=PLANES), :] = keep
    swapped = planes[...].T
    turned[...] = swapped.astype(BF16)
    for copy in copies:
        copy.wait()
    col_even = lax.rem(lax.axis_index("col"), 2) == 0
    _, at_low, step = piece_counts(height)
    for side, out in enumerate(outs):
        right = col_even if side == 0 else jnp.logical_not(col_even)
        flat[height] = jnp.where(right, swapped[breadth - SIDE :], swapped[:SIDE])
        flat[height + 1] = jnp.zeros(flat.shape[1:], F32)
        for row in range(height):
            source = pick_row(row, height)
            own = [jnp.where(right, ends[n, 1, source], ends[n, 0, source]) for n in range(3)]
            flat[row] = own[0]
            own[0] = own[0] - own[0].astype(BF16).astype(F32)
            for number, piece in enumerate(own):
                near = jnp.where(right, piece[SIDE - EDGE :], piece[:EDGE])
                at = EDGE * row
                flat[at_low + number * step + at // SIDE, at % SIDE : at % SIDE + EDGE] = near
        out[...] = flat[...].astype(BF16)


def pack_weights(one, two, rgb, bias_one, bias_two, *refs):
    ahead_one, ahead_two, back_one, back_two, colors, bias, held = refs
    size = one.shape[2]
    odd = lax.rem(row_place(), 2) == 1
    for kernel, ahead, back in ((one, ahead_one, back_one), (two, ahead_two, back_two)):
        for row in range(4):
            for col in range(3):
                at = (row * 3 + col) * size
                for out in range(2):
                    tap = row - out
                    if 0 <= tap <= 2:
                        front = kernel[jnp.where(odd, 2 - tap, tap), col]
                        rear = kernel[jnp.where(odd, tap, 2 - tap), 2 - col]
                        rear = rear.astype(F32).T.astype(BF16)
                    else:
                        front = rear = jnp.zeros((size, size), BF16)
                    ahead[at : at + size, out * size : (out + 1) * size] = front
                    back[at : at + size, out * size : (out + 1) * size] = rear
    held[...] = jnp.zeros_like(held)
    held[0:3] = rgb[...].astype(F32)
    held[3:6] = rgb[...].astype(F32)
    colors[...] = held[...].astype(BF16)
    bias[0] = jnp.broadcast_to(bias_one[...], bias.shape[1:])
    bias[1] = jnp.broadcast_to(bias_two[...], bias.shape[1:])


def put(dest, row, value, strip):
    dest[row, 1 : strip + 1] = value.astype(BF16).reshape(strip, STRIPS, -1)
    dest[row, 0] = pltpu.roll(value[(strip - 1) * STRIPS :], 1, 0).astype(BF16)
    dest[row, strip + 1] = pltpu.roll(value[:STRIPS], STRIPS - 1, 0).astype(BF16)


def widen(dest, source, strip):
    for row in range(EDGE):
        dest[row, 1 : strip + 1] = source[row]
        dest[row, 0] = pltpu.roll(source[row, strip - 1].astype(F32), 1, 0).astype(BF16)
        dest[row, strip + 1] = pltpu.roll(source[row, 0].astype(F32), STRIPS - 1, 0).astype(BF16)


def strips_of(source, row, strip):
    return jnp.concatenate(
        [source[row, pl.ds(j, STRIPS, stride=strip), :] for j in range(strip)], axis=0
    )


def fill_sides(sides, held, pieces, spread, rows):
    breadth = held.shape[1] - 2 * SIDE
    col_even = lax.rem(lax.axis_index("col"), 2) == 0
    for side in range(2):
        right = col_even if side == 0 else jnp.logical_not(col_even)
        spot = pl.ds(pl.multiple_of(jnp.where(right, SIDE + breadth, 0), SIDE), SIDE)
        for row in range(rows):
            if side < sides:
                held[row, spot] = spread(pieces[side], row, right)
            else:
                held[row, spot] = jnp.zeros((SIDE, held.shape[2]), F32)


def nearest(pieces, number, height, row, right):
    _, at_low, step = piece_counts(height)
    at = EDGE * row
    piece = pieces[at_low + number * step + at // SIDE].astype(F32)
    piece = piece[at % SIDE : at % SIDE + EDGE]
    blank = jnp.zeros((SIDE - EDGE, piece.shape[1]), F32)
    return jnp.where(
        right,
        jnp.concatenate([piece, blank], axis=0),
        jnp.concatenate([blank, piece], axis=0),
    )


def pack_rows(sides, latent, turned, *rest):
    pieces, rest = rest[:sides], rest[sides:]
    own, lines, near, far, spots, inside, held, turn = rest
    height, breadth, size = latent.shape
    strip = own.shape[1] - 2
    for row in range(height):
        held[row, SIDE : SIDE + breadth] = latent[pick_row(row, height)]
    fill_sides(
        sides,
        held,
        pieces,
        lambda piece, row, right: piece[row].astype(F32) + nearest(piece, 0, height, row, right),
        height,
    )
    turn[0, SIDE : SIDE + breadth] = turned[...].astype(F32)
    fill_sides(sides, turn, pieces, lambda piece, row, right: piece[height].astype(F32), 1)
    spot = strips_of(turn, 0, strip).astype(BF16).reshape(strip, STRIPS, size)
    spots[...] = spot
    near[EDGE] = spot
    far[EDGE] = spot
    for row in range(height):
        line = strips_of(held, row, strip)
        lines[row] = line
        put(own, row, line, strip)
        short = line.astype(BF16).reshape(strip, STRIPS, size)
        if row < EDGE:
            far[EDGE - 1 - row] = short
        if row >= height - EDGE:
            near[height - 1 - row] = short
    col = lax.axis_index("col")
    base = col * breadth - SIDE
    total = lax.axis_size("col") * breadth
    for j in range(strip):
        at = lax.broadcasted_iota(jnp.int32, (STRIPS, size), 0) * strip + (j + base)
        inside[j * STRIPS : (j + 1) * STRIPS] = ((at >= 0) & (at < total)).astype(F32)


def aim_rows(aims, known, spots):
    size = aims.shape[2]
    lane_in = lax.broadcasted_iota(jnp.int32, (size, 2 * size), 0)
    lane_out = lax.broadcasted_iota(jnp.int32, (size, 2 * size), 1)
    color = lax.rem(lane_out, 3)
    aimed = (lane_out < 6) & ((lane_in == color) | (lane_in == color + 3))
    masked = (lane_out >= size) & (lane_out < size + 6) & (lane_in == 6)
    chosen = (aimed | masked).astype(F32).astype(BF16)
    for row, (spot, source) in enumerate(spots):
        value = pltpu.roll(spot, lax.rem(size - PLANES * source, size), 1)
        both = jnp.dot(value.astype(BF16), chosen, preferred_element_type=F32)
        aims[row] = both[:, :size]
        known[row] = both[:, size:]


def conv_pair(rows, first, weights, strip):
    taps = []
    for down in range(4):
        source, at = rows[first + down]
        for across in range(3):
            taps.append(source[at, across : across + strip].reshape(strip * STRIPS, -1))
    return jnp.dot(jnp.concatenate(taps, axis=1), weights[...], preferred_element_type=F32)


def sigma_of(value):
    return 0.5 * jnp.tanh(0.5 * value) + 0.5


def gradient(firsts, rows, weights, aims, known, inside, emit):
    wide, hidden, slope, grad_two, grad_one = rows
    ahead_one, ahead_two, back_one, back_two, colors, bias = weights
    pixels, size = inside.shape
    strip = pixels // STRIPS
    place, count = row_place(), lax.axis_size("row") * lax.axis_size("cores")
    odd = lax.rem(place, 2) == 1
    there = jnp.where(odd, place < count - 1, place > 0).astype(F32)
    columns = inside[...]
    halves = lambda both: (both[:, :size], both[:, size:])

    for first in firsts[0]:
        for half, summed in enumerate(halves(conv_pair(wide, first - 1, ahead_one, strip))):
            row = first + half
            value = summed + bias[0, :1]
            sigma = sigma_of(value)
            hid = value * sigma
            keep = columns * there if row < EDGE else columns
            put(*hidden[row], hid * keep, strip)
            if row in slope:
                held, at = slope[row]
                held[at] = (sigma + hid * (1.0 - sigma)) * keep

    lane = lax.broadcasted_iota(jnp.int32, (2 * pixels, size), 1)
    for number, first in enumerate(firsts[1]):
        both = conv_pair(hidden, first - 1, ahead_two, strip)
        value = jnp.concatenate(halves(both), axis=0) + bias[1, :1]
        sigma = sigma_of(value)
        hid = value * sigma
        color = lax.dot_general(
            hid.astype(BF16), colors[...], (((1,), (1,)), ((), ())), preferred_element_type=F32
        )
        spot = slice(2 * number, 2 * number + 2)
        residual = known[spot].reshape(2 * pixels, -1) * color - aims[spot].reshape(2 * pixels, -1)
        rest = residual - residual.astype(BF16).astype(F32)
        split = jnp.where(lane < 3, residual, rest).astype(BF16)
        spread = jnp.dot(split, colors[...], preferred_element_type=F32)
        result = spread * (sigma + hid * (1.0 - sigma))
        for half in range(2):
            put(*grad_two[first + half], result[half * pixels : (half + 1) * pixels], strip)

    for first in firsts[2]:
        for half, summed in enumerate(halves(conv_pair(grad_two, first - 1, back_two, strip))):
            held, at = slope[first + half]
            put(*grad_one[first + half], summed * held[at], strip)

    for first in firsts[3]:
        for half, summed in enumerate(halves(conv_pair(grad_one, first - 1, back_one, strip))):
            emit(first + half - EDGE, summed)


def adam(current, first, second, grad):
    first = BETA_ONE * first + (1.0 - BETA_ONE) * grad
    second = BETA_TWO * second + (1.0 - BETA_TWO) * grad * grad
    return current - LEARN_RATE * first / (jnp.sqrt(second) + EPSILON), first, second


def place_rows(*parts):
    rows = {}
    for first, last, held, at in parts:
        for row in range(first, last):
            rows[row] = (held, at + row - first)
    return rows


def near_firsts(height):
    return [range(5 + n, height + 7 - n, 2) for n in range(4)]


def far_firsts():
    return [range(1 + n, 5 + n, 2) for n in range(4)]


def near_rows(height, own, halo, passed, scratch):
    hidden, slope, grad_two, grad_one = scratch
    hidden_out, slope_out, two_out, one_out = passed
    return (
        {**own, **place_rows((height + 4, height + 8, halo, 0))},
        place_rows((5, 7, hidden_out, 0), (7, height + 7, hidden, 0)),
        place_rows((5, 7, slope_out, 0), (7, height + 5, slope, 0)),
        place_rows((6, 8, two_out, 0), (8, height + 6, grad_two, 0)),
        place_rows((7, 9, one_out, 0), (9, height + 5, grad_one, 0)),
    )


def far_rows(own, halo, passed, scratch):
    hidden, slope, grad_two, grad_one = scratch
    hidden_in, slope_in, two_in, one_in = passed
    return (
        {**own, **place_rows((0, 4, halo, 0))},
        place_rows((1, 5, hidden, 0), (5, 7, hidden_in, 0)),
        place_rows((3, 5, slope, 0), (5, 7, slope_in, 0)),
        place_rows((2, 6, grad_two, 0), (6, 8, two_in, 0)),
        place_rows((3, 7, grad_one, 0), (7, 9, one_in, 0)),
    )


def flat_spot(spots):
    return spots[...].reshape(-1, spots.shape[-1]).astype(F32)


def first_near(sides, own, lines, moment_one, moment_two, near, spots, inside, *refs):
    pieces, refs = refs[:sides], refs[sides:]
    weights, refs = refs[:6], refs[6:]
    passed, refs = refs[:4], refs[4:]
    (new, near_out, z_out, m_out, v_out, m_rest, v_rest, aims, known), refs = refs[:9], refs[9:]
    halo, m_held, v_held, *scratch = refs
    height, breadth = moment_one.shape[:2]
    strip = own.shape[1] - 2
    widen(halo, near, strip)
    mine, theirs = flat_spot(spots), flat_spot(near.at[EDGE])
    aim_rows(
        aims,
        known,
        [(mine, pick_row(row, height)) for row in range(2, height)]
        + [(theirs, pick_partner_row(row, height)) for row in (height - 1, height - 2)],
    )
    for number, (held, moment) in enumerate(((m_held, moment_one), (v_held, moment_two))):
        for row in range(height):
            held[row, SIDE : SIDE + breadth] = moment[pick_row(row, height)]
        fill_sides(
            sides,
            held,
            pieces,
            lambda piece, row, right: nearest(piece, number + 1, height, row, right),
            height,
        )
    for row in range(EDGE):
        m_rest[row] = strips_of(m_held, row, strip)
        v_rest[row] = strips_of(v_held, row, strip)

    def emit(row, grad):
        current, first, second = adam(
            lines[row], strips_of(m_held, row, strip), strips_of(v_held, row, strip), grad
        )
        current = current * inside[...]
        at = row - EDGE
        z_out[at] = current
        m_out[at] = first
        v_out[at] = second
        put(new, at, current, strip)
        if row >= height - EDGE:
            near_out[height - 1 - row] = current.astype(BF16).reshape(near_out.shape[1:])

    rows = near_rows(height, place_rows((4, height + 4, own, 0)), halo, passed, scratch)
    gradient(near_firsts(height), rows, weights, aims, known, inside, emit)


def first_far(own, lines, m_rest, v_rest, far, spots, inside, *refs):
    passed, refs = refs[:4], refs[4:]
    weights, refs = refs[:6], refs[6:]
    (new, far_out, z_out, m_out, v_out, aims, known), refs = refs[:7], refs[7:]
    halo, *scratch = refs
    height = own.shape[0]
    strip = own.shape[1] - 2
    widen(halo, far, strip)
    mine, theirs = flat_spot(spots), flat_spot(far.at[EDGE])
    aim_rows(
        aims,
        known,
        [(theirs, pick_partner_row(row, height)) for row in (1, 0)]
        + [(mine, pick_row(row, height)) for row in range(2)],
    )

    def emit(row, grad):
        current, first, second = adam(lines[row], m_rest[row], v_rest[row], grad)
        current = current * inside[...]
        z_out[row] = current
        m_out[row] = first
        v_out[row] = second
        put(new, row, current, strip)
        far_out[EDGE - 1 - row] = current.astype(BF16).reshape(far_out.shape[1:])

    rows = far_rows(place_rows((4, 8, own, 0)), halo, passed, scratch)
    gradient(far_firsts(), rows, weights, aims, known, inside, emit)


def send_rows(outs, helds, sem, height, strip):
    copies = []
    breadth = outs[0].shape[1]

    def send(row, at, values):
        for number, (held, out, value) in enumerate(zip(helds, outs, values)):
            for j in range(strip):
                held[at, pl.ds(j, STRIPS, stride=strip), :] = value[j * STRIPS : (j + 1) * STRIPS]
            copy = pltpu.make_async_copy(
                held.at[at, pl.ds(SIDE, breadth)],
                out.at[pick_row(row, height)],
                sem.at[number, at],
            )
            copy.start()
            copies.append(copy)

    return send, copies


def last_near(low, high, near, z_in, m_in, v_in, aims, known, inside, *refs):
    weights, refs = refs[:6], refs[6:]
    passed, refs = refs[:4], refs[4:]
    outs, refs = refs[:3], refs[3:]
    helds, refs = refs[:3], refs[3:]
    halo, *scratch, sem = refs
    height = EDGE + high.shape[0]
    strip = low.shape[1] - 2
    widen(halo, near, strip)
    send, copies = send_rows(outs, helds, sem, height, strip)

    def emit(row, grad):
        at = row - EDGE
        send(row, at, adam(z_in[at], m_in[at], v_in[at], grad))

    own = place_rows((4, 8, low, 0), (8, height + 4, high, 0))
    rows = near_rows(height, own, halo, passed, scratch)
    gradient(near_firsts(height), rows, weights, aims, known, inside, emit)
    for copy in copies:
        copy.wait()


def last_far(low, far, z_in, m_in, v_in, aims, known, inside, *refs):
    passed, refs = refs[:4], refs[4:]
    weights, refs = refs[:6], refs[6:]
    outs, refs = refs[3:6], refs[6:]
    helds, refs = refs[:3], refs[3:]
    halo, *scratch, sem = refs
    height = outs[0].shape[0]
    strip = low.shape[1] - 2
    widen(halo, far, strip)
    send, copies = send_rows(outs, helds, sem, height, strip)

    def emit(row, grad):
        send(row, row, adam(z_in[row], m_in[row], v_in[row], grad))

    rows = far_rows(place_rows((4, 8, low, 0)), halo, passed, scratch)
    gradient(far_firsts(), rows, weights, aims, known, inside, emit)
    for copy in copies:
        copy.wait()


def body(
    latent,
    moment_one,
    moment_two,
    hole_mask,
    target_rgb,
    kernel_one,
    bias_one,
    kernel_two,
    bias_two,
    rgb_weight,
):
    height, breadth, size = latent.shape
    strip = (breadth + 2 * SIDE) // STRIPS
    assert strip * STRIPS == breadth + 2 * SIDE and height % 2 == 0 and height >= 8
    assert height * PLANES <= size and breadth == size and lax.axis_size("cores") == 2
    pixels = strip * STRIPS
    sides = 1 if lax.axis_size("col") == 2 else 2
    dma = pltpu.SemaphoreType.DMA
    _, at_low, step = piece_counts(height)
    block = (at_low + 3 * step, SIDE, size)
    tall = lambda rows: shape((rows, strip + 2, STRIPS, size), BF16)
    short = lambda rows: shape((rows, strip, STRIPS, size), BF16)
    lines_of = lambda rows: shape((rows, pixels, size), F32)
    vmem = lambda like: pltpu.VMEM(like.shape, like.dtype)
    work = 2 * 12 * 2 * pixels * size * size

    *columns, turned = call(
        functools.partial(pack_columns, sides),
        [shape(block, BF16)] * sides + [shape((breadth, size), BF16)],
        [HBM] * 5,
        [VMEM] * (sides + 1),
        [
            pltpu.VMEM((3, 2, height, SIDE, size), F32),
            pltpu.VMEM(target_rgb.shape, F32),
            pltpu.VMEM(hole_mask.shape, jnp.int32),
            pltpu.VMEM((size, breadth), F32),
            pltpu.VMEM(block, F32),
            dma((4, 2)),
        ],
        (10**6, 10**6),
        "pack_columns",
    )(latent, moment_one, moment_two, target_rgb, hole_mask)
    columns = [swap(piece, "col", side) for side, piece in enumerate(columns)]

    matrix = shape((12 * size, 2 * size), BF16)
    weights = call(
        pack_weights,
        [matrix] * 4 + [shape((size, size), BF16), shape((2, 8, size), F32)],
        [VMEM] * 5,
        [VMEM] * 6,
        [pltpu.VMEM((size, size), F32)],
        (10**6, 4 * 10**6),
        "pack_weights",
    )(kernel_one, kernel_two, rgb_weight, bias_one[None], bias_two[None])

    own, lines, near, far, spots, inside = call(
        functools.partial(pack_rows, sides),
        [tall(height), lines_of(height), short(EDGE + 1), short(EDGE + 1)]
        + [shape((strip, STRIPS, size), BF16), shape((pixels, size), F32)],
        [VMEM] * (2 + sides),
        [VMEM] * 6,
        [vmem(lines_of(height)), vmem(lines_of(1))],
        (10**6, 4 * 10**6),
        "pack_rows",
    )(latent, turned, *columns)
    near = swap(near, ROWS, 0)
    far = swap(far, ROWS, 1)

    passed = [tall(2), lines_of(2), tall(2), tall(2)]
    near_scratch = [
        vmem(tall(height)),
        vmem(lines_of(height - 2)),
        vmem(tall(height - 2)),
        vmem(tall(height - 4)),
    ]
    far_scratch = [vmem(tall(4)), vmem(lines_of(2)), vmem(tall(4)), vmem(tall(4))]
    near_work = (2 * (height - 1) + 0) * work, 10**7
    far_work = 8 * work, 10**7
    rest, some = height - EDGE, EDGE

    *results, near_next, z_high, m_high, v_high, m_rest, v_rest, aims_near, known_near = call(
        functools.partial(first_near, sides),
        passed
        + [tall(rest), short(EDGE), lines_of(rest), lines_of(rest), lines_of(rest)]
        + [lines_of(some), lines_of(some), lines_of(height), lines_of(height)],
        [VMEM] * (7 + sides + 6),
        [VMEM] * 13,
        [vmem(tall(EDGE)), vmem(lines_of(height)), vmem(lines_of(height))] + near_scratch,
        near_work,
        "first_near",
    )(own, lines, moment_one, moment_two, near, spots, inside, *columns, *weights)
    *handed, high = results
    near_next = swap(near_next, ROWS, 0)

    low, far_next, z_low, m_low, v_low, aims_far, known_far = call(
        first_far,
        [tall(some), short(EDGE), lines_of(some), lines_of(some), lines_of(some)]
        + [lines_of(4), lines_of(4)],
        [VMEM] * (7 + 4 + 6),
        [VMEM] * 7,
        [vmem(tall(EDGE))] + far_scratch,
        far_work,
        "first_far",
    )(own, lines, m_rest, v_rest, far, spots, inside, *handed, *weights)
    far_next = swap(far_next, ROWS, 1)

    out = shape(latent.shape, F32)
    results = call(
        last_near,
        passed + [out] * 3,
        [VMEM] * (9 + 6),
        [VMEM] * 4 + [HBM] * 3,
        [vmem(lines_of(rest))] * 3 + [vmem(tall(EDGE))] + near_scratch + [dma((3, rest))],
        near_work,
        "last_near",
    )(low, high, near_next, z_high, m_high, v_high, aims_near, known_near, inside, *weights)
    handed, outs = results[:4], results[4:]
    return call(
        last_far,
        [out] * 3,
        [VMEM] * (8 + 4 + 6) + [HBM] * 3,
        [HBM] * 3,
        [vmem(lines_of(some))] * 3 + [vmem(tall(EDGE))] + far_scratch + [dma((3, some))],
        far_work,
        "last_far",
        {18: 0, 19: 1, 20: 2},
    )(low, far_next, z_low, m_low, v_low, aims_far, known_far, inside, *handed, *weights, *outs)


def solution(mesh):
    tile = P(("parts", "row", "cores"), "col", None)
    return jax.shard_map(
        body,
        mesh=mesh,
        in_specs=(
            tile,
            tile,
            tile,
            P(("parts", "row", "cores"), "col"),
            P(None, ("parts", "row", "cores"), "col"),
            P(),
            P(),
            P(),
            P(),
            P(),
        ),
        out_specs=(tile, tile, tile),
        check_vma=False,
    )
```

```python
import functools
import math

import jax
import jax.numpy as jnp
from jax import lax
from jax.experimental import pallas as pl
from jax.experimental.pallas import tpu as pltpu
from jax.sharding import PartitionSpec as P

STEPS = 2

BETA_ONE = 0.6
BETA_TWO = 0.9
LEARN_RATE = 0.4
EPSILON = 1e-08

ROWS = ("row", "cores")
STRIPS = 16
SIDE = 8
EDGE = 4
PLANES = 7
VMEM = pl.BlockSpec(memory_space=pltpu.VMEM)
HBM = pl.BlockSpec(memory_space=pltpu.HBM)
F32 = jnp.float32
BF16 = jnp.bfloat16


def row_place():
    cores = lax.axis_size("cores")
    return lax.axis_index("row") * cores + lax.axis_index("cores")


def pairs(count, parity):
    chosen = []
    for low in range(parity, count - 1, 2):
        chosen += [(low, low + 1), (low + 1, low)]
    return chosen


def swap(block, axes, parity):
    return lax.ppermute(block, axes, pairs(lax.axis_size(axes), parity))


def call(kernel, out_shape, in_specs, out_specs, scratch, cost, name, aliases=None, limit=24 << 20):
    return pl.pallas_call(
        kernel,
        out_shape=out_shape,
        in_specs=in_specs,
        out_specs=out_specs,
        scratch_shapes=scratch,
        compiler_params=pltpu.CompilerParams(vmem_limit_bytes=limit),
        cost_estimate=pl.CostEstimate(flops=cost[0], bytes_accessed=cost[1], transcendentals=0),
        input_output_aliases=aliases or {},
        name=name,
    )


def in_hbm(array):
    return pltpu.with_memory_space_constraint(array, pltpu.HBM)


def shape(dims, dtype):
    return jax.ShapeDtypeStruct(dims, dtype)


def pick_row(index, height):
    odd = lax.rem(row_place(), 2) == 1
    return jnp.where(odd, height - 1 - index, index)


def pick_partner_row(index, height):
    odd = lax.rem(row_place(), 2) == 1
    return jnp.where(odd, index, height - 1 - index)


def piece_counts(height):
    return height, height + 2, height * EDGE // SIDE


def pack_columns(sides, latent, first, second, target, mask, *rest):
    outs, rest = rest[:sides], rest[sides:]
    turned, *inner, aim, known, planes, flat, sem = rest
    height, breadth = latent.shape[0], latent.shape[1]
    early = [
        pltpu.make_async_copy(target, aim, sem.at[3]),
        pltpu.make_async_copy(mask, known, sem.at[4]),
    ]
    copies = [
        pltpu.make_async_copy(source, dest, sem.at[number])
        for number, (source, dest) in enumerate(zip((latent, first, second), inner))
    ]
    for copy in early + copies:
        copy.start()
    planes[...] = jnp.zeros_like(planes)
    for copy in early:
        copy.wait()
    keep = known[...].astype(F32)
    for color in range(3):
        wanted = keep * aim[color]
        high = wanted.astype(BF16).astype(F32)
        planes[pl.ds(color, height, stride=PLANES), :] = high
        planes[pl.ds(color + 3, height, stride=PLANES), :] = wanted - high
    planes[pl.ds(6, height, stride=PLANES), :] = keep
    swapped = planes[...].T
    turned[...] = swapped.astype(BF16)
    for copy in copies:
        copy.wait()
    col_even = lax.rem(lax.axis_index("col"), 2) == 0
    _, at_low, step = piece_counts(height)
    for side, out in enumerate(outs):
        right = col_even if side == 0 else jnp.logical_not(col_even)
        flat[height] = jnp.where(right, swapped[breadth - SIDE :], swapped[:SIDE])
        flat[height + 1] = jnp.zeros(flat.shape[1:], F32)
        for row in range(height):
            source = pick_row(row, height)
            own = [
                jnp.where(right, block[source, breadth - SIDE :], block[source, :SIDE])
                for block in inner
            ]
            flat[row] = own[0]
            own[0] = own[0] - own[0].astype(BF16).astype(F32)
            for number, piece in enumerate(own):
                near = jnp.where(right, piece[SIDE - EDGE :], piece[:EDGE])
                at = EDGE * row
                flat[at_low + number * step + at // SIDE, at % SIDE : at % SIDE + EDGE] = near
        out[...] = flat[...].astype(BF16)


def pack_weights(one, two, rgb, bias_one, bias_two, *refs):
    ahead_one, ahead_two, back_one, back_two, colors, bias, held = refs
    size = one.shape[2]
    odd = lax.rem(row_place(), 2) == 1
    for kernel, ahead, back in ((one, ahead_one, back_one), (two, ahead_two, back_two)):
        for row in range(4):
            for col in range(3):
                at = (row * 3 + col) * size
                for out in range(2):
                    tap = row - out
                    if 0 <= tap <= 2:
                        front = kernel[jnp.where(odd, 2 - tap, tap), col]
                        rear = kernel[jnp.where(odd, tap, 2 - tap), 2 - col]
                        rear = rear.astype(F32).T.astype(BF16)
                    else:
                        front = rear = jnp.zeros((size, size), BF16)
                    ahead[at : at + size, out * size : (out + 1) * size] = front
                    back[at : at + size, out * size : (out + 1) * size] = rear
    held[...] = jnp.zeros_like(held)
    held[0:3] = rgb[...].astype(F32)
    held[3:6] = rgb[...].astype(F32)
    colors[...] = held[...].astype(BF16)
    bias[0] = jnp.broadcast_to(bias_one[...], bias.shape[1:])
    bias[1] = jnp.broadcast_to(bias_two[...], bias.shape[1:])


def put(dest, row, value, strip):
    dest[row, 1 : strip + 1] = value.astype(BF16).reshape(strip, STRIPS, -1)
    dest[row, 0] = pltpu.roll(value[(strip - 1) * STRIPS :], 1, 0).astype(BF16)
    dest[row, strip + 1] = pltpu.roll(value[:STRIPS], STRIPS - 1, 0).astype(BF16)


def widen(dest, source, strip):
    for row in range(EDGE):
        dest[row, 1 : strip + 1] = source[row]
        dest[row, 0] = pltpu.roll(source[row, strip - 1].astype(F32), 1, 0).astype(BF16)
        dest[row, strip + 1] = pltpu.roll(source[row, 0].astype(F32), STRIPS - 1, 0).astype(BF16)


def strips_of(source, row, strip):
    return jnp.concatenate(
        [source[row, pl.ds(j, STRIPS, stride=strip), :] for j in range(strip)], axis=0
    )


def fill_sides(sides, held, pieces, spread, rows):
    breadth = held.shape[1] - 2 * SIDE
    col_even = lax.rem(lax.axis_index("col"), 2) == 0
    for side in range(2):
        right = col_even if side == 0 else jnp.logical_not(col_even)
        spot = pl.ds(pl.multiple_of(jnp.where(right, SIDE + breadth, 0), SIDE), SIDE)
        for row in range(rows):
            if side < sides:
                held[row, spot] = spread(pieces[side], row, right)
            else:
                held[row, spot] = jnp.zeros((SIDE, held.shape[2]), F32)


def nearest(pieces, number, height, row, right):
    _, at_low, step = piece_counts(height)
    at = EDGE * row
    piece = pieces[at_low + number * step + at // SIDE].astype(F32)
    piece = piece[at % SIDE : at % SIDE + EDGE]
    blank = jnp.zeros((SIDE - EDGE, piece.shape[1]), F32)
    return jnp.where(
        right,
        jnp.concatenate([piece, blank], axis=0),
        jnp.concatenate([blank, piece], axis=0),
    )


def pack_rows(sides, latent, turned, *rest):
    pieces, rest = rest[:sides], rest[sides:]
    own, lines, near, far, spots, inside, held, turn = rest
    height, breadth, size = latent.shape
    strip = own.shape[1] - 2
    for row in range(height):
        held[row, SIDE : SIDE + breadth] = latent[pick_row(row, height)]
    fill_sides(
        sides,
        held,
        pieces,
        lambda piece, row, right: piece[row].astype(F32) + nearest(piece, 0, height, row, right),
        height,
    )
    turn[0, SIDE : SIDE + breadth] = turned[...].astype(F32)
    fill_sides(sides, turn, pieces, lambda piece, row, right: piece[height].astype(F32), 1)
    spot = strips_of(turn, 0, strip).astype(BF16).reshape(strip, STRIPS, size)
    spots[...] = spot
    near[EDGE] = spot
    far[EDGE] = spot
    for row in range(height):
        line = strips_of(held, row, strip)
        lines[row] = line
        put(own, row, line, strip)
        short = line.astype(BF16).reshape(strip, STRIPS, size)
        if row < EDGE:
            far[EDGE - 1 - row] = short
        if row >= height - EDGE:
            near[height - 1 - row] = short
    col = lax.axis_index("col")
    base = col * breadth - SIDE
    total = lax.axis_size("col") * breadth
    for j in range(strip):
        at = lax.broadcasted_iota(jnp.int32, (STRIPS, size), 0) * strip + (j + base)
        inside[j * STRIPS : (j + 1) * STRIPS] = ((at >= 0) & (at < total)).astype(F32)


def aim_rows(aims, known, spots):
    size = aims.shape[2]
    lane_in = lax.broadcasted_iota(jnp.int32, (size, 2 * size), 0)
    lane_out = lax.broadcasted_iota(jnp.int32, (size, 2 * size), 1)
    color = lax.rem(lane_out, 3)
    aimed = (lane_out < 6) & ((lane_in == color) | (lane_in == color + 3))
    masked = (lane_out >= size) & (lane_out < size + 6) & (lane_in == 6)
    chosen = (aimed | masked).astype(F32).astype(BF16)
    for row, (spot, source) in enumerate(spots):
        value = pltpu.roll(spot, lax.rem(size - PLANES * source, size), 1)
        both = jnp.dot(value.astype(BF16), chosen, preferred_element_type=F32)
        aims[row] = both[:, :size]
        known[row] = both[:, size:]


def conv_pair(rows, first, weights, strip):
    taps = []
    for down in range(4):
        source, at = rows[first + down]
        for across in range(3):
            taps.append(source[at, across : across + strip].reshape(strip * STRIPS, -1))
    return jnp.dot(jnp.concatenate(taps, axis=1), weights[...], preferred_element_type=F32)


def sigma_of(value):
    return 0.5 * jnp.tanh(0.5 * value) + 0.5


def gradient(firsts, rows, weights, aims, known, inside, emit):
    wide, hidden, slope, grad_two, grad_one = rows
    ahead_one, ahead_two, back_one, back_two, colors, bias = weights
    pixels, size = inside.shape
    strip = pixels // STRIPS
    place, count = row_place(), lax.axis_size("row") * lax.axis_size("cores")
    odd = lax.rem(place, 2) == 1
    there = jnp.where(odd, place < count - 1, place > 0).astype(F32)
    columns = inside[...]
    halves = lambda both: (both[:, :size], both[:, size:])

    for first in firsts[0]:
        for half, summed in enumerate(halves(conv_pair(wide, first - 1, ahead_one, strip))):
            row = first + half
            value = summed + bias[0, :1]
            sigma = sigma_of(value)
            hid = value * sigma
            keep = columns * there if row < EDGE else columns
            put(*hidden[row], hid * keep, strip)
            if row in slope:
                held, at = slope[row]
                held[at] = (sigma + hid * (1.0 - sigma)) * keep

    lane = lax.broadcasted_iota(jnp.int32, (2 * pixels, size), 1)
    for number, first in enumerate(firsts[1]):
        both = conv_pair(hidden, first - 1, ahead_two, strip)
        value = jnp.concatenate(halves(both), axis=0) + bias[1, :1]
        sigma = sigma_of(value)
        hid = value * sigma
        color = lax.dot_general(
            hid.astype(BF16), colors[...], (((1,), (1,)), ((), ())), preferred_element_type=F32
        )
        spot = slice(2 * number, 2 * number + 2)
        residual = known[spot].reshape(2 * pixels, -1) * color - aims[spot].reshape(2 * pixels, -1)
        rest = residual - residual.astype(BF16).astype(F32)
        split = jnp.where(lane < 3, residual, rest).astype(BF16)
        spread = jnp.dot(split, colors[...], preferred_element_type=F32)
        result = spread * (sigma + hid * (1.0 - sigma))
        for half in range(2):
            put(*grad_two[first + half], result[half * pixels : (half + 1) * pixels], strip)

    for first in firsts[2]:
        for half, summed in enumerate(halves(conv_pair(grad_two, first - 1, back_two, strip))):
            held, at = slope[first + half]
            put(*grad_one[first + half], summed * held[at], strip)

    for first in firsts[3]:
        for half, summed in enumerate(halves(conv_pair(grad_one, first - 1, back_one, strip))):
            emit(first + half - EDGE, summed)


def adam(current, first, second, grad):
    first = BETA_ONE * first + (1.0 - BETA_ONE) * grad
    second = BETA_TWO * second + (1.0 - BETA_TWO) * grad * grad
    return current - LEARN_RATE * first / (jnp.sqrt(second) + EPSILON), first, second


def place_rows(*parts):
    rows = {}
    for first, last, held, at in parts:
        for row in range(first, last):
            rows[row] = (held, at + row - first)
    return rows


def near_firsts(height):
    return [range(5 + n, height + 7 - n, 2) for n in range(4)]


def far_firsts():
    return [range(1 + n, 5 + n, 2) for n in range(4)]


def near_rows(height, own, halo, passed, scratch):
    hidden, slope, grad_two, grad_one = scratch
    hidden_out, slope_out, two_out, one_out = passed
    return (
        {**own, **place_rows((height + 4, height + 8, halo, 0))},
        place_rows((5, 7, hidden_out, 0), (7, height + 7, hidden, 0)),
        place_rows((5, 7, slope_out, 0), (7, height + 5, slope, 0)),
        place_rows((6, 8, two_out, 0), (8, height + 6, grad_two, 0)),
        place_rows((7, 9, one_out, 0), (9, height + 5, grad_one, 0)),
    )


def far_rows(own, halo, passed, scratch):
    hidden, slope, grad_two, grad_one = scratch
    hidden_in, slope_in, two_in, one_in = passed
    return (
        {**own, **place_rows((0, 4, halo, 0))},
        place_rows((1, 5, hidden, 0), (5, 7, hidden_in, 0)),
        place_rows((3, 5, slope, 0), (5, 7, slope_in, 0)),
        place_rows((2, 6, grad_two, 0), (6, 8, two_in, 0)),
        place_rows((3, 7, grad_one, 0), (7, 9, one_in, 0)),
    )


def flat_spot(spots):
    return spots[...].reshape(-1, spots.shape[-1]).astype(F32)


def first_near(sides, own, lines, moment_one, moment_two, near, spots, inside, *refs):
    pieces, refs = refs[:sides], refs[sides:]
    weights, refs = refs[:6], refs[6:]
    passed, refs = refs[:4], refs[4:]
    (new, near_out, z_out, m_out, v_out, m_rest, v_rest, aims, known), refs = refs[:9], refs[9:]
    halo, m_held, v_held, *scratch = refs
    height, breadth = moment_one.shape[:2]
    strip = own.shape[1] - 2
    widen(halo, near, strip)
    mine, theirs = flat_spot(spots), flat_spot(near.at[EDGE])
    aim_rows(
        aims,
        known,
        [(mine, pick_row(row, height)) for row in range(2, height)]
        + [(theirs, pick_partner_row(row, height)) for row in (height - 1, height - 2)],
    )
    for number, (held, moment) in enumerate(((m_held, moment_one), (v_held, moment_two))):
        for row in range(height):
            held[row, SIDE : SIDE + breadth] = moment[pick_row(row, height)]
        fill_sides(
            sides,
            held,
            pieces,
            lambda piece, row, right: nearest(piece, number + 1, height, row, right),
            height,
        )
    for row in range(EDGE):
        m_rest[row] = strips_of(m_held, row, strip)
        v_rest[row] = strips_of(v_held, row, strip)

    def emit(row, grad):
        current, first, second = adam(
            lines[row], strips_of(m_held, row, strip), strips_of(v_held, row, strip), grad
        )
        current = current * inside[...]
        at = row - EDGE
        z_out[at] = current
        m_out[at] = first
        v_out[at] = second
        put(new, at, current, strip)
        if row >= height - EDGE:
            near_out[height - 1 - row] = current.astype(BF16).reshape(near_out.shape[1:])

    rows = near_rows(height, place_rows((4, height + 4, own, 0)), halo, passed, scratch)
    gradient(near_firsts(height), rows, weights, aims, known, inside, emit)


def first_far(own, lines, m_rest, v_rest, far, spots, inside, *refs):
    passed, refs = refs[:4], refs[4:]
    weights, refs = refs[:6], refs[6:]
    (new, far_out, z_out, m_out, v_out, aims, known), refs = refs[:7], refs[7:]
    halo, *scratch = refs
    height = own.shape[0]
    strip = own.shape[1] - 2
    widen(halo, far, strip)
    mine, theirs = flat_spot(spots), flat_spot(far.at[EDGE])
    aim_rows(
        aims,
        known,
        [(theirs, pick_partner_row(row, height)) for row in (1, 0)]
        + [(mine, pick_row(row, height)) for row in range(2)],
    )

    def emit(row, grad):
        current, first, second = adam(lines[row], m_rest[row], v_rest[row], grad)
        current = current * inside[...]
        z_out[row] = current
        m_out[row] = first
        v_out[row] = second
        put(new, row, current, strip)
        far_out[EDGE - 1 - row] = current.astype(BF16).reshape(far_out.shape[1:])

    rows = far_rows(place_rows((4, 8, own, 0)), halo, passed, scratch)
    gradient(far_firsts(), rows, weights, aims, known, inside, emit)


def keep_row(held, at, value, strip):
    for j in range(strip):
        held[at, pl.ds(j, STRIPS, stride=strip), :] = value[j * STRIPS : (j + 1) * STRIPS]


def last_near(low, high, near, z_in, m_in, v_in, aims, known, inside, *refs):
    weights, refs = refs[:6], refs[6:]
    passed, refs = refs[:4], refs[4:]
    helds, refs = refs[:3], refs[3:]
    halo, *scratch = refs
    height = EDGE + high.shape[0]
    strip = low.shape[1] - 2
    widen(halo, near, strip)

    def emit(row, grad):
        at = row - EDGE
        for held, value in zip(helds, adam(z_in[at], m_in[at], v_in[at], grad)):
            keep_row(held, at, value, strip)

    own = place_rows((4, 8, low, 0), (8, height + 4, high, 0))
    rows = near_rows(height, own, halo, passed, scratch)
    gradient(near_firsts(height), rows, weights, aims, known, inside, emit)


def last_far(low, far, z_in, m_in, v_in, aims, known, inside, *refs):
    passed, refs = refs[:4], refs[4:]
    weights, refs = refs[:6], refs[6:]
    ready, outs, helds, refs = refs[:3], refs[3:6], refs[6:9], refs[9:]
    halo, *scratch, sem = refs
    height, breadth = outs[0].shape[:2]
    strip = low.shape[1] - 2
    copies = []

    def send(row, number, held, at):
        copy = pltpu.make_async_copy(
            held.at[at, pl.ds(SIDE, breadth)],
            outs[number].at[pick_row(row, height)],
            sem.at[number, row],
        )
        copy.start()
        copies.append(copy)

    for row in range(EDGE, height):
        for number in range(3):
            send(row, number, ready[number], row - EDGE)
    widen(halo, far, strip)

    def emit(row, grad):
        for number, value in enumerate(adam(z_in[row], m_in[row], v_in[row], grad)):
            keep_row(helds[number], row, value, strip)
            send(row, number, helds[number], row)

    rows = far_rows(place_rows((4, 8, low, 0)), halo, passed, scratch)
    gradient(far_firsts(), rows, weights, aims, known, inside, emit)
    for copy in copies:
        copy.wait()


def body(
    latent,
    moment_one,
    moment_two,
    hole_mask,
    target_rgb,
    kernel_one,
    bias_one,
    kernel_two,
    bias_two,
    rgb_weight,
):
    height, breadth, size = latent.shape
    strip = (breadth + 2 * SIDE) // STRIPS
    assert strip * STRIPS == breadth + 2 * SIDE and height % 2 == 0 and height >= 8
    assert height * PLANES <= size and breadth == size and lax.axis_size("cores") == 2
    pixels = strip * STRIPS
    sides = 1 if lax.axis_size("col") == 2 else 2
    dma = pltpu.SemaphoreType.DMA
    _, at_low, step = piece_counts(height)
    block = (at_low + 3 * step, SIDE, size)
    tall = lambda rows: shape((rows, strip + 2, STRIPS, size), BF16)
    short = lambda rows: shape((rows, strip, STRIPS, size), BF16)
    lines_of = lambda rows: shape((rows, pixels, size), F32)
    vmem = lambda like: pltpu.VMEM(like.shape, like.dtype)
    work = 2 * 12 * 2 * pixels * size * size

    *columns, turned, latent, moment_one, moment_two = call(
        functools.partial(pack_columns, sides),
        [shape(block, BF16)] * sides
        + [shape((breadth, size), BF16)]
        + [shape(latent.shape, F32)] * 3,
        [HBM] * 5,
        [VMEM] * (sides + 4),
        [
            pltpu.VMEM(target_rgb.shape, F32),
            pltpu.VMEM(hole_mask.shape, jnp.int32),
            pltpu.VMEM((size, breadth), F32),
            pltpu.VMEM(block, F32),
            dma((5,)),
        ],
        (10**6, 10**6),
        "pack_columns",
    )(*map(in_hbm, (latent, moment_one, moment_two, target_rgb, hole_mask)))
    columns = [swap(piece, "col", side) for side, piece in enumerate(columns)]

    matrix = shape((12 * size, 2 * size), BF16)
    weights = call(
        pack_weights,
        [matrix] * 4 + [shape((size, size), BF16), shape((2, 8, size), F32)],
        [VMEM] * 5,
        [VMEM] * 6,
        [pltpu.VMEM((size, size), F32)],
        (10**6, 4 * 10**6),
        "pack_weights",
    )(kernel_one, kernel_two, rgb_weight, bias_one[None], bias_two[None])

    columns, weights = lax.optimization_barrier((columns, weights))
    own, lines, near, far, spots, inside = call(
        functools.partial(pack_rows, sides),
        [tall(height), lines_of(height), short(EDGE + 1), short(EDGE + 1)]
        + [shape((strip, STRIPS, size), BF16), shape((pixels, size), F32)],
        [VMEM] * (2 + sides),
        [VMEM] * 6,
        [vmem(lines_of(height)), vmem(lines_of(1))],
        (10**6, 4 * 10**6),
        "pack_rows",
    )(latent, turned, *columns)
    near = swap(near, ROWS, 0)
    far = swap(far, ROWS, 1)

    passed = [tall(2), lines_of(2), tall(2), tall(2)]
    near_scratch = [
        vmem(tall(height)),
        vmem(lines_of(height - 2)),
        vmem(tall(height - 2)),
        vmem(tall(height - 4)),
    ]
    far_scratch = [vmem(tall(4)), vmem(lines_of(2)), vmem(tall(4)), vmem(tall(4))]
    near_work = (2 * (height - 1) + 0) * work, 10**7
    far_work = 8 * work, 10**7
    rest, some = height - EDGE, EDGE

    *results, near_next, z_high, m_high, v_high, m_rest, v_rest, aims_near, known_near = call(
        functools.partial(first_near, sides),
        passed
        + [tall(rest), short(EDGE), lines_of(rest), lines_of(rest), lines_of(rest)]
        + [lines_of(some), lines_of(some), lines_of(height), lines_of(height)],
        [VMEM] * (7 + sides + 6),
        [VMEM] * 13,
        [vmem(tall(EDGE)), vmem(lines_of(height)), vmem(lines_of(height))] + near_scratch,
        near_work,
        "first_near",
    )(own, lines, moment_one, moment_two, near, spots, inside, *columns, *weights)
    *handed, high = results
    near_next = swap(near_next, ROWS, 0)

    low, far_next, z_low, m_low, v_low, aims_far, known_far = call(
        first_far,
        [tall(some), short(EDGE), lines_of(some), lines_of(some), lines_of(some)]
        + [lines_of(4), lines_of(4)],
        [VMEM] * (7 + 4 + 6),
        [VMEM] * 7,
        [vmem(tall(EDGE))] + far_scratch,
        far_work,
        "first_far",
    )(own, lines, m_rest, v_rest, far, spots, inside, *handed, *weights)
    far_next = swap(far_next, ROWS, 1)

    out = shape(latent.shape, F32)
    results = call(
        last_near,
        passed + [lines_of(rest)] * 3,
        [VMEM] * (9 + 6),
        [VMEM] * 7,
        [vmem(tall(EDGE))] + near_scratch,
        near_work,
        "last_near",
    )(low, high, near_next, z_high, m_high, v_high, aims_near, known_near, inside, *weights)
    handed, ready = results[:4], results[4:]
    return call(
        last_far,
        [out] * 3,
        [VMEM] * (8 + 4 + 6 + 3),
        [HBM] * 3,
        [vmem(lines_of(some))] * 3 + [vmem(tall(EDGE))] + far_scratch + [dma((3, height))],
        far_work,
        "last_far",
    )(low, far_next, z_low, m_low, v_low, aims_far, known_far, inside, *handed, *weights, *ready)


def solution(mesh):
    tile = P(("parts", "row", "cores"), "col", None)
    return jax.shard_map(
        body,
        mesh=mesh,
        in_specs=(
            tile,
            tile,
            tile,
            P(("parts", "row", "cores"), "col"),
            P(None, ("parts", "row", "cores"), "col"),
            P(),
            P(),
            P(),
            P(),
            P(),
        ),
        out_specs=(tile, tile, tile),
        check_vma=False,
    )
```

```python
import functools
import math

import jax
import jax.numpy as jnp
from jax import lax
from jax.experimental import pallas as pl
from jax.experimental.pallas import tpu as pltpu
from jax.sharding import PartitionSpec as P

STEPS = 2

BETA_ONE = 0.6
BETA_TWO = 0.9
LEARN_RATE = 0.4
EPSILON = 1e-08

ROWS = ("row", "cores")
STRIPS = 16
SIDE = 8
EDGE = 4
PLANES = 7
VMEM = pl.BlockSpec(memory_space=pltpu.VMEM)
HBM = pl.BlockSpec(memory_space=pltpu.HBM)
F32 = jnp.float32
BF16 = jnp.bfloat16


def row_place():
    cores = lax.axis_size("cores")
    return lax.axis_index("row") * cores + lax.axis_index("cores")


def pairs(count, parity):
    chosen = []
    for low in range(parity, count - 1, 2):
        chosen += [(low, low + 1), (low + 1, low)]
    return chosen


def swap(block, axes, parity):
    return lax.ppermute(block, axes, pairs(lax.axis_size(axes), parity))


def swap_near(block):
    return swap(block, ROWS, 0)


def swap_far(block):
    rows, cols, cores = (lax.axis_size(name) for name in ("row", "col", "cores"))
    count = rows * cores

    def index(place, col):
        return (place // cores * cols + col) * cores + place % cores

    chosen = []
    for col in range(cols):
        chosen += [(index(a, col), index(b, col)) for a, b in pairs(count, 1)]
    for place in (0, count - 1):
        chosen += [(index(place, a), index(place, b)) for a, b in pairs(cols, 0)]
    return lax.ppermute(block, ("row", "col", "cores"), sorted(chosen))


def far_there():
    place, count = row_place(), lax.axis_size("row") * lax.axis_size("cores")
    odd = lax.rem(place, 2) == 1
    return jnp.where(odd, place < count - 1, place > 0).astype(F32)


def call(kernel, out_shape, in_specs, out_specs, scratch, cost, name, aliases=None, limit=24 << 20):
    return pl.pallas_call(
        kernel,
        out_shape=out_shape,
        in_specs=in_specs,
        out_specs=out_specs,
        scratch_shapes=scratch,
        compiler_params=pltpu.CompilerParams(vmem_limit_bytes=limit),
        cost_estimate=pl.CostEstimate(flops=cost[0], bytes_accessed=cost[1], transcendentals=0),
        input_output_aliases=aliases or {},
        name=name,
    )


def in_hbm(array):
    return pltpu.with_memory_space_constraint(array, pltpu.HBM)


def shape(dims, dtype):
    return jax.ShapeDtypeStruct(dims, dtype)


def pick_row(index, height):
    odd = lax.rem(row_place(), 2) == 1
    return jnp.where(odd, height - 1 - index, index)


def pick_partner_row(index, height):
    odd = lax.rem(row_place(), 2) == 1
    return jnp.where(odd, index, height - 1 - index)


def piece_counts(height):
    return height, height + 2, height * EDGE // SIDE


def pack_columns(sides, latent, first, second, target, mask, *rest):
    outs, rest = rest[:sides], rest[sides:]
    turned, ends, aim, known, planes, flat, sem = rest
    height, breadth = latent.shape[0], latent.shape[1]
    early = [
        pltpu.make_async_copy(target, aim, sem.at[3, 0]),
        pltpu.make_async_copy(mask, known, sem.at[3, 1]),
    ]
    copies = [
        pltpu.make_async_copy(
            source.at[:, pl.ds(start, SIDE)], ends.at[number, end], sem.at[number, end]
        )
        for number, source in enumerate((latent, first, second))
        for end, start in enumerate((0, breadth - SIDE))
    ]
    for copy in early + copies:
        copy.start()
    planes[...] = jnp.zeros_like(planes)
    for copy in early:
        copy.wait()
    keep = known[...].astype(F32)
    for color in range(3):
        wanted = keep * aim[color]
        high = wanted.astype(BF16).astype(F32)
        planes[pl.ds(color, height, stride=PLANES), :] = high
        planes[pl.ds(color + 3, height, stride=PLANES), :] = wanted - high
    planes[pl.ds(6, height, stride=PLANES), :] = keep
    swapped = planes[...].T
    turned[...] = swapped.astype(BF16)
    for copy in copies:
        copy.wait()
    col_even = lax.rem(lax.axis_index("col"), 2) == 0
    _, at_low, step = piece_counts(height)
    for side, out in enumerate(outs):
        right = col_even if side == 0 else jnp.logical_not(col_even)
        flat[height] = jnp.where(right, swapped[breadth - SIDE :], swapped[:SIDE])
        flat[height + 1] = jnp.zeros(flat.shape[1:], F32)
        for row in range(height):
            source = pick_row(row, height)
            own = [jnp.where(right, ends[n, 1, source], ends[n, 0, source]) for n in range(3)]
            flat[row] = own[0]
            own[0] = own[0] - own[0].astype(BF16).astype(F32)
            for number, piece in enumerate(own):
                near = jnp.where(right, piece[SIDE - EDGE :], piece[:EDGE])
                at = EDGE * row
                flat[at_low + number * step + at // SIDE, at % SIDE : at % SIDE + EDGE] = near
        out[...] = flat[...].astype(BF16)


def pack_weights(one, two, rgb, bias_one, bias_two, *refs):
    given, loaded, refs = refs[:3], refs[10:13], refs[3:10] + refs[13:]
    ahead_one, ahead_two, back_one, back_two, colors, spread, bias, held, sem = refs
    copies = [
        pltpu.make_async_copy(source, dest, sem.at[number])
        for number, (source, dest) in enumerate(zip(given, loaded))
    ]
    for copy in copies:
        copy.start()
    size = one.shape[2]
    half = jnp.asarray(0.5, BF16)
    odd = lax.rem(row_place(), 2) == 1
    for kernel, ahead, back in ((one, ahead_one, back_one), (two, ahead_two, back_two)):
        for row in range(4):
            for col in range(3):
                at = (row * 3 + col) * size
                for out in range(2):
                    tap = row - out
                    if 0 <= tap <= 2:
                        front = kernel[jnp.where(odd, 2 - tap, tap), col] * half
                        rear = kernel[jnp.where(odd, tap, 2 - tap), 2 - col]
                        rear = rear.astype(F32).T.astype(BF16)
                        if kernel is two:
                            rear = rear * half
                    else:
                        front = rear = jnp.zeros((size, size), BF16)
                    ahead[at : at + size, out * size : (out + 1) * size] = front
                    back[at : at + size, out * size : (out + 1) * size] = rear
    held[...] = jnp.zeros_like(held)
    for at in (0, size):
        held[at : at + 3, at : at + size] = rgb[...].astype(F32)
        held[at + 3 : at + 6, at : at + size] = rgb[...].astype(F32)
    colors[...] = held[...].astype(BF16)
    spread[...] = (0.5 * held[...]).astype(BF16)
    for number, given in enumerate((bias_one, bias_two)):
        for at in (0, size):
            bias[number, :, at : at + size] = jnp.broadcast_to(0.5 * given[...], (8, size))
    for copy in copies:
        copy.wait()


def put(dest, row, value, strip, keep=None):
    low, high = value[:STRIPS], value[(strip - 1) * STRIPS :]
    value = value.astype(BF16)
    if keep is not None:
        value = value * keep
        low = low * keep[:STRIPS].astype(F32)
        high = high * keep[(strip - 1) * STRIPS :].astype(F32)
    dest[row, 1 : strip + 1] = value.reshape(strip, STRIPS, -1)
    dest[row, 0] = pltpu.roll(high, 1, 0).astype(BF16)
    dest[row, strip + 1] = pltpu.roll(low, STRIPS - 1, 0).astype(BF16)


def widen(dest, source, strip, there=None):
    for row in range(EDGE):
        value, low, high = source[row], source[row, 0].astype(F32), source[row, strip - 1].astype(F32)
        if there is not None:
            value, low, high = value * there.astype(BF16), low * there, high * there
        dest[row, 1 : strip + 1] = value
        dest[row, 0] = pltpu.roll(high, 1, 0).astype(BF16)
        dest[row, strip + 1] = pltpu.roll(low, STRIPS - 1, 0).astype(BF16)


def strips_of(source, row, strip):
    return jnp.concatenate(
        [source[row, pl.ds(j, STRIPS, stride=strip), :] for j in range(strip)], axis=0
    )


def fill_sides(sides, held, pieces, spread, rows):
    breadth = held.shape[1] - 2 * SIDE
    col_even = lax.rem(lax.axis_index("col"), 2) == 0
    for side in range(2):
        right = col_even if side == 0 else jnp.logical_not(col_even)
        spot = pl.ds(pl.multiple_of(jnp.where(right, SIDE + breadth, 0), SIDE), SIDE)
        for row in range(rows):
            if side < sides:
                held[row, spot] = spread(pieces[side], row, right)
            else:
                held[row, spot] = jnp.zeros((SIDE, held.shape[2]), F32)


def nearest(pieces, number, height, row, right):
    _, at_low, step = piece_counts(height)
    at = EDGE * row
    piece = pieces[at_low + number * step + at // SIDE].astype(F32)
    piece = piece[at % SIDE : at % SIDE + EDGE]
    blank = jnp.zeros((SIDE - EDGE, piece.shape[1]), F32)
    return jnp.where(
        right,
        jnp.concatenate([piece, blank], axis=0),
        jnp.concatenate([blank, piece], axis=0),
    )


def pack_rows(sides, latent, turned, *rest):
    pieces, rest = rest[:sides], rest[sides:]
    own, lines, near, far, spots, inside, held, turn = rest
    height, breadth, size = latent.shape
    strip = own.shape[1] - 2
    for row in range(height):
        held[row, SIDE : SIDE + breadth] = latent[pick_row(row, height)]
    fill_sides(
        sides,
        held,
        pieces,
        lambda piece, row, right: piece[row].astype(F32) + nearest(piece, 0, height, row, right),
        height,
    )
    turn[0, SIDE : SIDE + breadth] = turned[...].astype(F32)
    fill_sides(sides, turn, pieces, lambda piece, row, right: piece[height].astype(F32), 1)
    spot = strips_of(turn, 0, strip).astype(BF16).reshape(strip, STRIPS, size)
    spots[...] = spot
    near[EDGE] = spot
    far[EDGE] = spot
    for row in range(height):
        line = strips_of(held, row, strip)
        lines[row] = line
        put(own, row, line, strip)
        short = line.astype(BF16).reshape(strip, STRIPS, size)
        if row < EDGE:
            far[EDGE - 1 - row] = short
        if row >= height - EDGE:
            near[height - 1 - row] = short
    col = lax.axis_index("col")
    base = col * breadth - SIDE
    total = lax.axis_size("col") * breadth
    for j in range(strip):
        at = lax.broadcasted_iota(jnp.int32, (STRIPS, size), 0) * strip + (j + base)
        inside[j * STRIPS : (j + 1) * STRIPS] = ((at >= 0) & (at < total)).astype(F32)


def aim_rows(aims, known, spots):
    size = aims.shape[2] // 2
    lane_in = lax.broadcasted_iota(jnp.int32, (size, 2 * size), 0)
    lane_out = lax.broadcasted_iota(jnp.int32, (size, 2 * size), 1)
    color = lax.rem(lane_out, 3)
    aimed = (lane_out < 6) & ((lane_in == color) | (lane_in == color + 3))
    masked = (lane_out >= size) & (lane_out < size + 6) & (lane_in == 6)
    chosen = (aimed | masked).astype(F32).astype(BF16)

    def aim(row, spot, source):
        value = pltpu.roll(spot, lax.rem(size - PLANES * source, size), 1)
        both = jnp.dot(value.astype(BF16), chosen, preferred_element_type=F32)
        lanes = slice(row % 2 * size, (row % 2 + 1) * size)
        aims[row // 2, :, lanes] = both[:, :size]
        known[row // 2, :, lanes] = both[:, size:]

    return [functools.partial(aim, row, *spot) for row, spot in enumerate(spots)]


def conv_pair(rows, first, weights, strip):
    taps = []
    for down in range(4):
        source, at = rows[first + down]
        for across in range(3):
            taps.append(source[at, across : across + strip].reshape(strip * STRIPS, -1))
    half = weights.shape[0] // 2
    parts = [
        jnp.dot(
            jnp.concatenate(taps[6 * part : 6 * part + 6], axis=1),
            weights[half * part : half * (part + 1)],
            preferred_element_type=F32,
        )
        for part in range(2)
    ]
    return parts[0] + parts[1]


def sigma_of(value):
    return 0.5 * jnp.tanh(0.5 * value) + 0.5


def gradient(order, rows, weights, aims, known, inside, emit, beside=(), parts=True):
    wide, hidden, slope, grad_two, grad_one = rows
    ahead_one, ahead_two, back_one, back_two, colors, spread, bias = weights
    pixels, size = inside.shape
    strip = pixels // STRIPS
    there = far_there()
    low = min(first for stage, first in filter(None, order) if stage == 1)

    def keep_of(row):
        return (inside[...] * there if row < EDGE else inside[...]).astype(BF16)

    def half_of(both, half):
        return both[:, half * size : (half + 1) * size]

    def gate(both, number):
        value = both + bias[number, :1]
        twice = jnp.tanh(value) + 1.0
        hid = value * twice
        return hid, twice + hid * (2.0 - twice)

    def ahead_first(first):
        both = conv_pair(wide, first - 1, ahead_one, strip)
        yield
        hid, twice = gate(both, 0)
        for half in range(2):
            row = first + half
            put(*hidden[row], half_of(hid, half), strip, keep_of(row))
            if row in slope:
                held, at = slope[row]
                held[at] = half_of(twice, half)

    def ahead_second(first):
        number = (first - low) // 2
        both = conv_pair(hidden, first - 1, ahead_two, strip)
        yield
        hid, twice = gate(both, 1)
        color = lax.dot_general(
            hid.astype(BF16), colors[...], (((1,), (1,)), ((), ())), preferred_element_type=F32
        )
        if parts:
            yield
        residual = known[number] * color - aims[number]
        rest = residual - residual.astype(BF16).astype(F32)
        lane = lax.broadcasted_iota(jnp.int32, (pixels, 2 * size), 1)
        split = jnp.where(lax.rem(lane, size) < 3, residual, rest).astype(BF16)
        back = jnp.dot(split, spread[...], preferred_element_type=F32)
        if parts:
            yield
        result = back * twice
        for half in range(2):
            put(*grad_two[first + half], half_of(result, half), strip)

    def back_second(first):
        both = conv_pair(grad_two, first - 1, back_two, strip)
        yield
        for half in range(2):
            row = first + half
            held, at = slope[row]
            put(*grad_one[row], half_of(both, half) * held[at], strip, keep_of(row))

    def back_first(first):
        both = conv_pair(grad_one, first - 1, back_one, strip)
        yield
        for half in range(2):
            emit(first + half - EDGE, half_of(both, half))

    stages = (ahead_first, ahead_second, back_second, back_first)
    beside = list(beside)
    active = []
    slots = list(order)
    while slots or active:
        started = None
        if slots:
            item = slots.pop(0)
            if item is not None:
                started = stages[item[0]](item[1])
                next(started)
        if beside:
            beside.pop(0)()
        active = [task for task in active if next(task, active) is None]
        if started is not None:
            active.append(started)


def adam(current, first, second, grad):
    first = BETA_ONE * first + (1.0 - BETA_ONE) * grad
    second = BETA_TWO * second + (1.0 - BETA_TWO) * grad * grad
    root = second * lax.rsqrt(jnp.maximum(second, 1e-30))
    return current - (LEARN_RATE * first) / (root + EPSILON), first, second


def place_rows(*parts):
    rows = {}
    for first, last, held, at in parts:
        for row in range(first, last):
            rows[row] = (held, at + row - first)
    return rows


def near_order(height):
    firsts = [list(range(5 + n, height + 7 - n, 2)) for n in range(4)]
    delay = (2, 4, 2)
    done, order = {}, []
    while any(firsts):
        slot = len(order)
        for stage in (3, 2, 1, 0):
            if not firsts[stage]:
                continue
            first = firsts[stage][0]
            needs = [(stage - 1, first - 1), (stage - 1, first + 1)] if stage else []
            if all(done.get(need, slot) + delay[stage - 1] <= slot for need in needs):
                done[stage, first] = slot
                order.append((stage, firsts[stage].pop(0)))
                break
        else:
            order.append(None)
    return order


def far_order():
    return [(0, 3), (0, 1), (1, 4), (1, 2), (2, 5), (2, 3), (3, 6), (3, 4)]


def near_rows(height, own, halo, passed, scratch):
    hidden, slope, grad_two, grad_one = scratch
    hidden_out, slope_out, two_out, one_out = passed
    return (
        {**own, **place_rows((height + 4, height + 8, halo, 0))},
        place_rows((5, 7, hidden_out, 0), (7, height + 7, hidden, 0)),
        place_rows((5, 7, slope_out, 0), (7, height + 5, slope, 0)),
        place_rows((6, 8, two_out, 0), (8, height + 6, grad_two, 0)),
        place_rows((7, 9, one_out, 0), (9, height + 5, grad_one, 0)),
    )


def far_rows(own, halo, passed, scratch):
    hidden, slope, grad_two, grad_one = scratch
    hidden_in, slope_in, two_in, one_in = passed
    return (
        {**own, **place_rows((0, 4, halo, 0))},
        place_rows((1, 5, hidden, 0), (5, 7, hidden_in, 0)),
        place_rows((3, 5, slope, 0), (5, 7, slope_in, 0)),
        place_rows((2, 6, grad_two, 0), (6, 8, two_in, 0)),
        place_rows((3, 7, grad_one, 0), (7, 9, one_in, 0)),
    )


def pair_up(tasks):
    def both(one, two):
        one()
        two()

    return [functools.partial(both, *tasks[at : at + 2]) for at in range(0, len(tasks), 2)]


def flat_spot(spots):
    return spots[...].reshape(-1, spots.shape[-1]).astype(F32)


def first_near(sides, own, lines, moment_one, moment_two, near, spots, inside, *refs):
    pieces, refs = refs[:sides], refs[sides:]
    weights, refs = refs[:7], refs[7:]
    passed, refs = refs[:4], refs[4:]
    (new, near_out, z_out, m_out, v_out, m_rest, v_rest, aims, known), refs = refs[:9], refs[9:]
    halo, m_held, v_held, *scratch = refs
    height, breadth = moment_one.shape[:2]
    strip = own.shape[1] - 2
    widen(halo, near, strip)
    mine, theirs = flat_spot(spots), flat_spot(near.at[EDGE])
    tasks = aim_rows(
        aims,
        known,
        [(mine, pick_row(row, height)) for row in range(2, height)]
        + [(theirs, pick_partner_row(row, height)) for row in (height - 1, height - 2)],
    )
    for number, (held, moment) in enumerate(((m_held, moment_one), (v_held, moment_two))):
        for row in range(height):
            held[row, SIDE : SIDE + breadth] = moment[pick_row(row, height)]
        fill_sides(
            sides,
            held,
            pieces,
            lambda piece, row, right: nearest(piece, number + 1, height, row, right),
            height,
        )
    for row in range(EDGE):
        m_rest[row] = strips_of(m_held, row, strip)
        v_rest[row] = strips_of(v_held, row, strip)

    def emit(row, grad):
        current, first, second = adam(
            lines[row], strips_of(m_held, row, strip), strips_of(v_held, row, strip), grad
        )
        current = current * inside[...]
        at = row - EDGE
        z_out[at] = current
        m_out[at] = first
        v_out[at] = second
        put(new, at, current, strip)
        if row >= height - EDGE:
            near_out[height - 1 - row] = current.astype(BF16).reshape(near_out.shape[1:])

    rows = near_rows(height, place_rows((4, height + 4, own, 0)), halo, passed, scratch)
    gradient(near_order(height), rows, weights, aims, known, inside, emit, pair_up(tasks))


def first_far(own, lines, m_rest, v_rest, far, spots, inside, *refs):
    passed, refs = refs[:4], refs[4:]
    weights, refs = refs[:7], refs[7:]
    (new, far_out, z_out, m_out, v_out, aims, known), refs = refs[:7], refs[7:]
    halo, *scratch = refs
    height = own.shape[0]
    strip = own.shape[1] - 2
    widen(halo, far, strip, far_there())
    mine, theirs = flat_spot(spots), flat_spot(far.at[EDGE]) * far_there()
    tasks = aim_rows(
        aims,
        known,
        [(theirs, pick_partner_row(row, height)) for row in (1, 0)]
        + [(mine, pick_row(row, height)) for row in range(2)],
    )

    def emit(row, grad):
        current, first, second = adam(lines[row], m_rest[row], v_rest[row], grad)
        current = current * inside[...]
        z_out[row] = current
        m_out[row] = first
        v_out[row] = second
        put(new, row, current, strip)
        far_out[EDGE - 1 - row] = current.astype(BF16).reshape(far_out.shape[1:])

    rows = far_rows(place_rows((4, 8, own, 0)), halo, passed, scratch)
    gradient(far_order(), rows, weights, aims, known, inside, emit, pair_up(tasks), False)


def keep_row(held, at, value, strip):
    for j in range(strip):
        held[at, pl.ds(j, STRIPS, stride=strip), :] = value[j * STRIPS : (j + 1) * STRIPS]


def last_near(low, high, near, z_in, m_in, v_in, aims, known, inside, *refs):
    weights, refs = refs[:7], refs[7:]
    passed, refs = refs[:4], refs[4:]
    helds, refs = refs[:3], refs[3:]
    halo, *scratch = refs
    height = EDGE + high.shape[0]
    strip = low.shape[1] - 2
    widen(halo, near, strip)

    def emit(row, grad):
        at = row - EDGE
        for held, value in zip(helds, adam(z_in[at], m_in[at], v_in[at], grad)):
            keep_row(held, at, value, strip)

    own = place_rows((4, 8, low, 0), (8, height + 4, high, 0))
    rows = near_rows(height, own, halo, passed, scratch)
    gradient(near_order(height), rows, weights, aims, known, inside, emit)


def last_far(low, far, z_in, m_in, v_in, aims, known, inside, *refs):
    passed, refs = refs[:4], refs[4:]
    weights, refs = refs[:7], refs[7:]
    ready, outs, helds, refs = refs[:3], refs[3:6], refs[6:9], refs[9:]
    halo, *scratch, sem = refs
    height, breadth = outs[0].shape[:2]
    strip = low.shape[1] - 2
    copies = []

    def send(row, number, held, at):
        copy = pltpu.make_async_copy(
            held.at[at, pl.ds(SIDE, breadth)],
            outs[number].at[pick_row(row, height)],
            sem.at[number, row],
        )
        copy.start()
        copies.append(copy)

    for row in range(EDGE, height):
        for number in range(3):
            send(row, number, ready[number], row - EDGE)
    widen(halo, far, strip, far_there())

    def emit(row, grad):
        for number, value in enumerate(adam(z_in[row], m_in[row], v_in[row], grad)):
            keep_row(helds[number], row, value, strip)
            send(row, number, helds[number], row)

    rows = far_rows(place_rows((4, 8, low, 0)), halo, passed, scratch)
    gradient(far_order(), rows, weights, aims, known, inside, emit, (), False)
    for copy in copies:
        copy.wait()


def body(
    latent,
    moment_one,
    moment_two,
    hole_mask,
    target_rgb,
    kernel_one,
    bias_one,
    kernel_two,
    bias_two,
    rgb_weight,
):
    height, breadth, size = latent.shape
    strip = (breadth + 2 * SIDE) // STRIPS
    assert strip * STRIPS == breadth + 2 * SIDE and height % 2 == 0 and height >= 8
    assert height * PLANES <= size and breadth == size and lax.axis_size("cores") == 2
    pixels = strip * STRIPS
    sides = 1 if lax.axis_size("col") == 2 else 2
    dma = pltpu.SemaphoreType.DMA
    _, at_low, step = piece_counts(height)
    block = (at_low + 3 * step, SIDE, size)
    tall = lambda rows: shape((rows, strip + 2, STRIPS, size), BF16)
    short = lambda rows: shape((rows, strip, STRIPS, size), BF16)
    lines_of = lambda rows: shape((rows, pixels, size), F32)
    aims_of = lambda rows: shape((rows // 2, pixels, 2 * size), F32)
    vmem = lambda like: pltpu.VMEM(like.shape, like.dtype)
    work = 2 * 12 * 2 * pixels * size * size

    given = tuple(map(in_hbm, (latent, moment_one, moment_two)))
    *columns, turned = call(
        functools.partial(pack_columns, sides),
        [shape(block, BF16)] * sides
        + [shape((breadth, size), BF16)],
        [HBM] * 5,
        [VMEM] * (sides + 1),
        [
            pltpu.VMEM((3, 2, height, SIDE, size), F32),
            pltpu.VMEM(target_rgb.shape, F32),
            pltpu.VMEM(hole_mask.shape, jnp.int32),
            pltpu.VMEM((size, breadth), F32),
            pltpu.VMEM(block, F32),
            dma((4, 2)),
        ],
        (10**6, 10**6),
        "pack_columns",
    )(*given, in_hbm(target_rgb), in_hbm(hole_mask))
    columns = [swap(piece, "col", side) for side, piece in enumerate(columns)]

    matrix = shape((12 * size, 2 * size), BF16)
    *weights, latent, moment_one, moment_two = call(
        pack_weights,
        [matrix] * 4 + [shape((2 * size, 2 * size), BF16)] * 2 + [shape((2, 8, 2 * size), F32)]
        + [shape(latent.shape, F32)] * 3,
        [VMEM] * 5 + [HBM] * 3,
        [VMEM] * 10,
        [pltpu.VMEM((2 * size, 2 * size), F32), dma((3,))],
        (10**6, 4 * 10**6),
        "pack_weights",
    )(kernel_one, kernel_two, rgb_weight, bias_one[None], bias_two[None], *given)

    columns, weights = lax.optimization_barrier((columns, weights))
    own, lines, near, far, spots, inside = call(
        functools.partial(pack_rows, sides),
        [tall(height), lines_of(height), short(EDGE + 1), short(EDGE + 1)]
        + [shape((strip, STRIPS, size), BF16), shape((pixels, size), F32)],
        [VMEM] * (2 + sides),
        [VMEM] * 6,
        [vmem(lines_of(height)), vmem(lines_of(1))],
        (10**6, 4 * 10**6),
        "pack_rows",
    )(latent, turned, *columns)
    near = swap_near(near)
    far = swap_far(far)

    passed = [tall(2), lines_of(2), tall(2), tall(2)]
    near_scratch = [
        vmem(tall(height)),
        vmem(lines_of(height - 2)),
        vmem(tall(height - 2)),
        vmem(tall(height - 4)),
    ]
    far_scratch = [vmem(tall(4)), vmem(lines_of(2)), vmem(tall(4)), vmem(tall(4))]
    near_work = (2 * (height - 1) + 0) * work, 10**7
    far_work = 8 * work, 10**7
    rest, some = height - EDGE, EDGE

    *results, near_next, z_high, m_high, v_high, m_rest, v_rest, aims_near, known_near = call(
        functools.partial(first_near, sides),
        passed
        + [tall(rest), short(EDGE), lines_of(rest), lines_of(rest), lines_of(rest)]
        + [lines_of(some), lines_of(some), aims_of(height), aims_of(height)],
        [VMEM] * (7 + sides + 7),
        [VMEM] * 13,
        [vmem(tall(EDGE)), vmem(lines_of(height)), vmem(lines_of(height))] + near_scratch,
        near_work,
        "first_near",
    )(own, lines, moment_one, moment_two, near, spots, inside, *columns, *weights)
    *handed, high = results
    near_next = swap_near(near_next)

    low, far_next, z_low, m_low, v_low, aims_far, known_far = call(
        first_far,
        [tall(some), short(EDGE), lines_of(some), lines_of(some), lines_of(some)]
        + [aims_of(4), aims_of(4)],
        [VMEM] * (7 + 4 + 7),
        [VMEM] * 7,
        [vmem(tall(EDGE))] + far_scratch,
        far_work,
        "first_far",
    )(own, lines, m_rest, v_rest, far, spots, inside, *handed, *weights)
    far_next = swap_far(far_next)

    out = shape(latent.shape, F32)
    results = call(
        last_near,
        passed + [lines_of(rest)] * 3,
        [VMEM] * (9 + 7),
        [VMEM] * 7,
        [vmem(tall(EDGE))] + near_scratch,
        near_work,
        "last_near",
    )(low, high, near_next, z_high, m_high, v_high, aims_near, known_near, inside, *weights)
    handed, ready = results[:4], results[4:]
    return call(
        last_far,
        [out] * 3,
        [VMEM] * (8 + 4 + 7 + 3),
        [HBM] * 3,
        [vmem(lines_of(some))] * 3 + [vmem(tall(EDGE))] + far_scratch + [dma((3, height))],
        far_work,
        "last_far",
    )(low, far_next, z_low, m_low, v_low, aims_far, known_far, inside, *handed, *weights, *ready)


def solution(mesh):
    tile = P(("parts", "row", "cores"), "col", None)
    return jax.shard_map(
        body,
        mesh=mesh,
        in_specs=(
            tile,
            tile,
            tile,
            P(("parts", "row", "cores"), "col"),
            P(None, ("parts", "row", "cores"), "col"),
            P(),
            P(),
            P(),
            P(),
            P(),
        ),
        out_specs=(tile, tile, tile),
        check_vma=False,
    )
```

```python
import functools
import math

import jax
import jax.numpy as jnp
from jax import lax
from jax.experimental import pallas as pl
from jax.experimental.pallas import tpu as pltpu
from jax.sharding import PartitionSpec as P

STEPS = 2

BETA_ONE = 0.6
BETA_TWO = 0.9
LEARN_RATE = 0.4
EPSILON = 1e-08

ROWS = ("row", "cores")
STRIPS = 16
SIDE = 8
EDGE = 4
PLANES = 7
VMEM = pl.BlockSpec(memory_space=pltpu.VMEM)
HBM = pl.BlockSpec(memory_space=pltpu.HBM)
F32 = jnp.float32
BF16 = jnp.bfloat16


def row_place():
    cores = lax.axis_size("cores")
    return lax.axis_index("row") * cores + lax.axis_index("cores")


def pairs(count, parity):
    chosen = []
    for low in range(parity, count - 1, 2):
        chosen += [(low, low + 1), (low + 1, low)]
    return chosen


def swap(block, axes, parity):
    return lax.ppermute(block, axes, pairs(lax.axis_size(axes), parity))


def swap_near(block):
    return swap(block, ROWS, 0)


def swap_far(block):
    rows, cols, cores = (lax.axis_size(name) for name in ("row", "col", "cores"))
    count = rows * cores

    def index(place, col):
        return (place // cores * cols + col) * cores + place % cores

    chosen = []
    for col in range(cols):
        chosen += [(index(a, col), index(b, col)) for a, b in pairs(count, 1)]
    for place in (0, count - 1):
        chosen += [(index(place, a), index(place, b)) for a, b in pairs(cols, 0)]
    return lax.ppermute(block, ("row", "col", "cores"), sorted(chosen))


def far_there():
    place, count = row_place(), lax.axis_size("row") * lax.axis_size("cores")
    odd = lax.rem(place, 2) == 1
    return jnp.where(odd, place < count - 1, place > 0).astype(F32)


def call(kernel, out_shape, in_specs, out_specs, scratch, cost, name, aliases=None, limit=24 << 20):
    return pl.pallas_call(
        kernel,
        out_shape=out_shape,
        in_specs=in_specs,
        out_specs=out_specs,
        scratch_shapes=scratch,
        compiler_params=pltpu.CompilerParams(vmem_limit_bytes=limit),
        cost_estimate=pl.CostEstimate(flops=cost[0], bytes_accessed=cost[1], transcendentals=0),
        input_output_aliases=aliases or {},
        name=name,
    )


def in_hbm(array):
    return pltpu.with_memory_space_constraint(array, pltpu.HBM)


def shape(dims, dtype):
    return jax.ShapeDtypeStruct(dims, dtype)


def pick_row(index, height):
    odd = lax.rem(row_place(), 2) == 1
    return jnp.where(odd, height - 1 - index, index)


def pick_partner_row(index, height):
    odd = lax.rem(row_place(), 2) == 1
    return jnp.where(odd, index, height - 1 - index)


def piece_counts(height):
    return height, height + 2, height * EDGE // SIDE


def pack_columns(sides, latent, first, second, target, mask, *rest):
    outs, rest = rest[:sides], rest[sides:]
    turned, ends, aim, known, planes, flat, sem = rest
    height, breadth = latent.shape[0], latent.shape[1]
    early = [
        pltpu.make_async_copy(target, aim, sem.at[3, 0]),
        pltpu.make_async_copy(mask, known, sem.at[3, 1]),
    ]
    copies = [
        pltpu.make_async_copy(
            source.at[:, pl.ds(start, SIDE)], ends.at[number, end], sem.at[number, end]
        )
        for number, source in enumerate((latent, first, second))
        for end, start in enumerate((0, breadth - SIDE))
    ]
    for copy in early + copies:
        copy.start()
    planes[...] = jnp.zeros_like(planes)
    for copy in early:
        copy.wait()
    keep = known[...].astype(F32)
    for color in range(3):
        wanted = keep * aim[color]
        high = wanted.astype(BF16).astype(F32)
        planes[pl.ds(color, height, stride=PLANES), :] = high
        planes[pl.ds(color + 3, height, stride=PLANES), :] = wanted - high
    planes[pl.ds(6, height, stride=PLANES), :] = keep
    swapped = planes[...].T
    turned[...] = swapped.astype(BF16)
    for copy in copies:
        copy.wait()
    col_even = lax.rem(lax.axis_index("col"), 2) == 0
    _, at_low, step = piece_counts(height)
    for side, out in enumerate(outs):
        right = col_even if side == 0 else jnp.logical_not(col_even)
        flat[height] = jnp.where(right, swapped[breadth - SIDE :], swapped[:SIDE])
        flat[height + 1] = jnp.zeros(flat.shape[1:], F32)
        for row in range(height):
            source = pick_row(row, height)
            own = [jnp.where(right, ends[n, 1, source], ends[n, 0, source]) for n in range(3)]
            flat[row] = own[0]
            own[0] = own[0] - own[0].astype(BF16).astype(F32)
            for number, piece in enumerate(own):
                near = jnp.where(right, piece[SIDE - EDGE :], piece[:EDGE])
                at = EDGE * row
                flat[at_low + number * step + at // SIDE, at % SIDE : at % SIDE + EDGE] = near
        out[...] = flat[...].astype(BF16)


def pack_weights(one, two, rgb, bias_one, bias_two, *refs):
    given, refs = refs[:1], refs[1:]
    matrices, loaded, refs = refs[:7], refs[7 : 7 + 1], refs[7 + 1 :]
    ahead_one, ahead_two, back_one, back_two, colors, spread, bias = matrices
    held, *small, sem = refs
    copies = [
        pltpu.make_async_copy(source, dest, sem.at[number])
        for number, (source, dest) in enumerate(
            zip((rgb, bias_one, bias_two, *given), (*small, *loaded))
        )
    ]
    rgb, bias_one, bias_two = small
    for copy in copies:
        copy.start()
    size = one.shape[2]
    half = jnp.asarray(0.5, BF16)
    odd = lax.rem(row_place(), 2) == 1
    for kernel, ahead, back in ((one, ahead_one, back_one), (two, ahead_two, back_two)):
        for row in range(4):
            for col in range(3):
                at = (row * 3 + col) * size
                for out in range(2):
                    tap = row - out
                    if 0 <= tap <= 2:
                        front = kernel[jnp.where(odd, 2 - tap, tap), col] * half
                        rear = kernel[jnp.where(odd, tap, 2 - tap), 2 - col]
                        rear = rear.astype(F32).T.astype(BF16)
                        if kernel is two:
                            rear = rear * half
                    else:
                        front = rear = jnp.zeros((size, size), BF16)
                    ahead[at : at + size, out * size : (out + 1) * size] = front
                    back[at : at + size, out * size : (out + 1) * size] = rear
    held[...] = jnp.zeros_like(held)
    for copy in copies[:3]:
        copy.wait()
    for at in (0, size):
        held[at : at + 3, at : at + size] = rgb[...].astype(F32)
        held[at + 3 : at + 6, at : at + size] = rgb[...].astype(F32)
    colors[...] = held[...].astype(BF16)
    spread[...] = (0.5 * held[...]).astype(BF16)
    for number, given in enumerate((bias_one, bias_two)):
        for at in (0, size):
            bias[number, :, at : at + size] = jnp.broadcast_to(0.5 * given[...], (8, size))
    for copy in copies[3:]:
        copy.wait()


def put(dest, row, value, strip, keep=None):
    low, high = value[:STRIPS], value[(strip - 1) * STRIPS :]
    value = value.astype(BF16)
    if keep is not None:
        value = value * keep
        low = low * keep[:STRIPS].astype(F32)
        high = high * keep[(strip - 1) * STRIPS :].astype(F32)
    dest[row, 1 : strip + 1] = value.reshape(strip, STRIPS, -1)
    dest[row, 0] = pltpu.roll(high, 1, 0).astype(BF16)
    dest[row, strip + 1] = pltpu.roll(low, STRIPS - 1, 0).astype(BF16)


def widen(dest, source, strip, there=None):
    for row in range(EDGE):
        value, low, high = source[row], source[row, 0].astype(F32), source[row, strip - 1].astype(F32)
        if there is not None:
            value, low, high = value * there.astype(BF16), low * there, high * there
        dest[row, 1 : strip + 1] = value
        dest[row, 0] = pltpu.roll(high, 1, 0).astype(BF16)
        dest[row, strip + 1] = pltpu.roll(low, STRIPS - 1, 0).astype(BF16)


def strips_of(source, row, strip):
    return jnp.concatenate(
        [source[row, pl.ds(j, STRIPS, stride=strip), :] for j in range(strip)], axis=0
    )


def fill_sides(sides, held, pieces, spread, rows):
    breadth = held.shape[1] - 2 * SIDE
    col_even = lax.rem(lax.axis_index("col"), 2) == 0
    for side in range(2):
        right = col_even if side == 0 else jnp.logical_not(col_even)
        spot = pl.ds(pl.multiple_of(jnp.where(right, SIDE + breadth, 0), SIDE), SIDE)
        for row in range(rows):
            if side < sides:
                held[row, spot] = spread(pieces[side], row, right)
            else:
                held[row, spot] = jnp.zeros((SIDE, held.shape[2]), F32)


def nearest(pieces, number, height, row, right):
    _, at_low, step = piece_counts(height)
    at = EDGE * row
    piece = pieces[at_low + number * step + at // SIDE].astype(F32)
    piece = piece[at % SIDE : at % SIDE + EDGE]
    blank = jnp.zeros((SIDE - EDGE, piece.shape[1]), F32)
    return jnp.where(
        right,
        jnp.concatenate([piece, blank], axis=0),
        jnp.concatenate([blank, piece], axis=0),
    )


def pack_rows(sides, latent, turned, *rest):
    pieces, rest = rest[:sides], rest[sides:]
    own, lines, near, far, spots, inside, held, turn = rest
    height, breadth, size = latent.shape
    strip = own.shape[1] - 2
    for row in range(height):
        held[row, SIDE : SIDE + breadth] = latent[pick_row(row, height)]
    fill_sides(
        sides,
        held,
        pieces,
        lambda piece, row, right: piece[row].astype(F32) + nearest(piece, 0, height, row, right),
        height,
    )
    turn[0, SIDE : SIDE + breadth] = turned[...].astype(F32)
    fill_sides(sides, turn, pieces, lambda piece, row, right: piece[height].astype(F32), 1)
    spot = strips_of(turn, 0, strip).astype(BF16).reshape(strip, STRIPS, size)
    spots[...] = spot
    near[EDGE] = spot
    far[EDGE] = spot
    for row in range(height):
        line = strips_of(held, row, strip)
        lines[row] = line
        put(own, row, line, strip)
        short = line.astype(BF16).reshape(strip, STRIPS, size)
        if row < EDGE:
            far[EDGE - 1 - row] = short
        if row >= height - EDGE:
            near[height - 1 - row] = short
    col = lax.axis_index("col")
    base = col * breadth - SIDE
    total = lax.axis_size("col") * breadth
    for j in range(strip):
        at = lax.broadcasted_iota(jnp.int32, (STRIPS, size), 0) * strip + (j + base)
        inside[j * STRIPS : (j + 1) * STRIPS] = ((at >= 0) & (at < total)).astype(F32)


def aim_rows(aims, known, spots):
    size = aims.shape[2] // 2
    lane_in = lax.broadcasted_iota(jnp.int32, (size, 2 * size), 0)
    lane_out = lax.broadcasted_iota(jnp.int32, (size, 2 * size), 1)
    color = lax.rem(lane_out, 3)
    aimed = (lane_out < 6) & ((lane_in == color) | (lane_in == color + 3))
    masked = (lane_out >= size) & (lane_out < size + 6) & (lane_in == 6)
    chosen = (aimed | masked).astype(F32).astype(BF16)

    def aim(row, spot, source):
        value = pltpu.roll(spot, lax.rem(size - PLANES * source, size), 1)
        both = jnp.dot(value.astype(BF16), chosen, preferred_element_type=F32)
        lanes = slice(row % 2 * size, (row % 2 + 1) * size)
        aims[row // 2, :, lanes] = both[:, :size]
        known[row // 2, :, lanes] = both[:, size:]

    return [functools.partial(aim, row, *spot) for row, spot in enumerate(spots)]


def conv_pairs(rows, firsts, weights, strip, count):
    taps = []
    for down in range(4):
        for across in range(3):
            parts = []
            for first in firsts:
                source, at = rows[first - 1 + down]
                parts.append(source[at, across : across + strip].reshape(strip * STRIPS, -1))
            taps.append(jnp.concatenate(parts, axis=0) if len(parts) > 1 else parts[0])
    size = weights.shape[0] // count
    parts = [
        jnp.dot(
            jnp.concatenate(taps[len(taps) // count * part : len(taps) // count * (part + 1)], axis=1),
            weights[size * part : size * (part + 1)],
            preferred_element_type=F32,
        )
        for part in range(count)
    ]
    total = parts[0]
    for part in parts[1:]:
        total = total + part
    pixels = strip * STRIPS
    return [total[at * pixels : (at + 1) * pixels] for at in range(len(firsts))]


def gradient(order, rows, weights, aims, known, inside, emit, beside=(), parts=False, cuts=1):
    wide, hidden, slope, grad_two, grad_one = rows
    ahead_one, ahead_two, back_one, back_two, colors, spread, bias = weights
    pixels, size = inside.shape
    strip = pixels // STRIPS
    there = far_there()
    low = min(min(firsts) for stage, firsts in filter(None, order) if stage == 1)

    def keep_of(row):
        return (inside[...] * there if row < EDGE else inside[...]).astype(BF16)

    def half_of(both, half):
        return both[:, half * size : (half + 1) * size]

    def gate(both, number):
        value = both + bias[number, :1]
        twice = jnp.tanh(value) + 1.0
        hid = value * twice
        return hid, twice + hid * (2.0 - twice)

    def ahead_first(firsts):
        results = conv_pairs(wide, firsts, ahead_one, strip, cuts)
        yield
        for first, both in zip(firsts, results):
            hid, twice = gate(both, 0)
            for half in range(2):
                row = first + half
                put(*hidden[row], half_of(hid, half), strip, keep_of(row))
                if row in slope:
                    held, at = slope[row]
                    held[at] = half_of(twice, half)

    lane = lax.rem(lax.broadcasted_iota(jnp.int32, (pixels, 2 * size), 1), size)

    def ahead_second(firsts):
        results = conv_pairs(hidden, firsts, ahead_two, strip, cuts)
        yield
        for first, both in zip(firsts, results):
            number = (first - low) // 2
            hid, twice = gate(both, 1)
            color = lax.dot_general(
                hid.astype(BF16), colors[...], (((1,), (1,)), ((), ())), preferred_element_type=F32
            )
            if parts:
                yield
            residual = known[number] * color - aims[number]
            rest = residual - residual.astype(BF16).astype(F32)
            split = jnp.where(lane < 3, residual, rest).astype(BF16)
            back = jnp.dot(split, spread[...], preferred_element_type=F32)
            if parts:
                yield
            result = back * twice
            for half in range(2):
                put(*grad_two[first + half], half_of(result, half), strip)

    def back_second(firsts):
        results = conv_pairs(grad_two, firsts, back_two, strip, cuts)
        yield
        for first, both in zip(firsts, results):
            for half in range(2):
                row = first + half
                held, at = slope[row]
                put(*grad_one[row], half_of(both, half) * held[at], strip, keep_of(row))

    def back_first(firsts):
        results = conv_pairs(grad_one, firsts, back_one, strip, cuts)
        yield
        for first, both in zip(firsts, results):
            for half in range(2):
                emit(first + half - EDGE, half_of(both, half))

    stages = (ahead_first, ahead_second, back_second, back_first)
    beside = list(beside)
    active = []
    slots = list(order)
    while slots or active:
        started = None
        if slots:
            item = slots.pop(0)
            if item is not None:
                started = stages[item[0]](item[1])
                next(started)
        if beside:
            beside.pop(0)()
        active = [task for task in active if next(task, active) is None]
        if started is not None:
            active.append(started)


def adam(current, first, second, grad):
    first = BETA_ONE * first + (1.0 - BETA_ONE) * grad
    second = BETA_TWO * second + ((1.0 - BETA_TWO) * grad) * grad
    root = second * lax.rsqrt(second)
    return current - (LEARN_RATE * first) / (root + EPSILON), first, second


def floored(second):
    return jnp.maximum(second, 1e-30)


def place_rows(*parts):
    rows = {}
    for first, last, held, at in parts:
        for row in range(first, last):
            rows[row] = (held, at + row - first)
    return rows


def first_near_order(height):
    return [(0, (5, 7)), (0, (9, 11)), (0, (13,)), (1, (6, 8)), (1, (10, 12)), None, (2, (7, 9)), (2, (11,)), (3, (8,)), (3, (10,))]


def last_near_order(height):
    return [(0, (5, 7, 9)), (0, (11, 13)), (1, (6,)), (1, (8,)), (1, (10,)), (1, (12,)), (2, (7,)), (2, (9,)), (2, (11,)), (3, (8,)), (3, (10,))]


def first_far_order(height):
    return [(0, (3,)), (0, (1,)), (1, (4,)), (1, (2,)), (2, (5,)), (2, (3,)), (3, (6,)), (3, (4,))]


def last_far_order(height):
    return [(0, (3,)), (0, (1,)), (1, (4,)), (1, (2,)), (2, (5,)), (2, (3,)), (3, (6,)), (3, (4,))]


def near_rows(height, own, halo, passed, scratch):
    hidden, slope, grad_two, grad_one = scratch
    hidden_out, slope_out, two_out, one_out = passed
    return (
        {**own, **place_rows((height + 4, height + 8, halo, 0))},
        place_rows((5, 7, hidden_out, 0), (7, height + 7, hidden, 0)),
        place_rows((5, 7, slope_out, 0), (7, height + 5, slope, 0)),
        place_rows((6, 8, two_out, 0), (8, height + 6, grad_two, 0)),
        place_rows((7, 9, one_out, 0), (9, height + 5, grad_one, 0)),
    )


def far_rows(own, halo, passed, scratch):
    hidden, slope, grad_two, grad_one = scratch
    hidden_in, slope_in, two_in, one_in = passed
    return (
        {**own, **place_rows((0, 4, halo, 0))},
        place_rows((1, 5, hidden, 0), (5, 7, hidden_in, 0)),
        place_rows((3, 5, slope, 0), (5, 7, slope_in, 0)),
        place_rows((2, 6, grad_two, 0), (6, 8, two_in, 0)),
        place_rows((3, 7, grad_one, 0), (7, 9, one_in, 0)),
    )


def pair_up(tasks):
    def both(one, two):
        one()
        two()

    return [functools.partial(both, *tasks[at : at + 2]) for at in range(0, len(tasks), 2)]


def flat_spot(spots):
    return spots[...].reshape(-1, spots.shape[-1]).astype(F32)


def first_near(sides, own, lines, moment_one, moment_two, near, spots, inside, *refs):
    pieces, refs = refs[:sides], refs[sides:]
    weights, refs = refs[:7], refs[7:]
    passed, refs = refs[:4], refs[4:]
    (new, near_out, z_out, m_out, v_out, m_rest, v_rest, aims, known), refs = refs[:9], refs[9:]
    halo, m_held, v_held, *scratch = refs
    height, breadth = moment_one.shape[:2]
    strip = own.shape[1] - 2
    widen(halo, near, strip)
    mine, theirs = flat_spot(spots), flat_spot(near.at[EDGE])
    tasks = aim_rows(
        aims,
        known,
        [(mine, pick_row(row, height)) for row in range(2, height)]
        + [(theirs, pick_partner_row(row, height)) for row in (height - 1, height - 2)],
    )
    for number, (held, moment) in enumerate(((m_held, moment_one), (v_held, moment_two))):
        for row in range(height):
            held[row, SIDE : SIDE + breadth] = moment[pick_row(row, height)]
        fill_sides(
            sides,
            held,
            pieces,
            lambda piece, row, right: nearest(piece, number + 1, height, row, right),
            height,
        )
    for row in range(EDGE):
        m_rest[row] = strips_of(m_held, row, strip)
        v_rest[row] = floored(strips_of(v_held, row, strip))

    def emit(row, grad):
        current, first, second = adam(
            lines[row], strips_of(m_held, row, strip), floored(strips_of(v_held, row, strip)), grad
        )
        current = current * inside[...]
        at = row - EDGE
        z_out[at] = current
        m_out[at] = first
        v_out[at] = second
        put(new, at, current, strip)
        if row >= height - EDGE:
            near_out[height - 1 - row] = current.astype(BF16).reshape(near_out.shape[1:])

    rows = near_rows(height, place_rows((4, height + 4, own, 0)), halo, passed, scratch)
    gradient(first_near_order(height), rows, weights, aims, known, inside, emit, pair_up(tasks), False, 2)


def first_far(own, lines, m_rest, v_rest, far, spots, inside, *refs):
    passed, refs = refs[:4], refs[4:]
    weights, refs = refs[:7], refs[7:]
    (new, far_out, z_out, m_out, v_out, aims, known), refs = refs[:7], refs[7:]
    halo, *scratch = refs
    height = own.shape[0]
    strip = own.shape[1] - 2
    widen(halo, far, strip, far_there())
    mine, theirs = flat_spot(spots), flat_spot(far.at[EDGE]) * far_there()
    tasks = aim_rows(
        aims,
        known,
        [(theirs, pick_partner_row(row, height)) for row in (1, 0)]
        + [(mine, pick_row(row, height)) for row in range(2)],
    )

    def emit(row, grad):
        current, first, second = adam(lines[row], m_rest[row], v_rest[row], grad)
        current = current * inside[...]
        z_out[row] = current
        m_out[row] = first
        v_out[row] = second
        put(new, row, current, strip)
        far_out[EDGE - 1 - row] = current.astype(BF16).reshape(far_out.shape[1:])

    rows = far_rows(place_rows((4, 8, own, 0)), halo, passed, scratch)
    gradient(first_far_order(height), rows, weights, aims, known, inside, emit, pair_up(tasks), False, 2)


def keep_row(held, at, value, strip):
    for j in range(strip):
        held[at, pl.ds(j, STRIPS, stride=strip), :] = value[j * STRIPS : (j + 1) * STRIPS]


def last_near(low, high, near, z_in, m_in, v_in, aims, known, inside, *refs):
    weights, refs = refs[:7], refs[7:]
    passed, refs = refs[:4], refs[4:]
    helds, refs = refs[:3], refs[3:]
    halo, *scratch = refs
    height = EDGE + high.shape[0]
    strip = low.shape[1] - 2
    widen(halo, near, strip)

    def emit(row, grad):
        at = row - EDGE
        for held, value in zip(helds, adam(z_in[at], m_in[at], v_in[at], grad)):
            keep_row(held, at, value, strip)

    own = place_rows((4, 8, low, 0), (8, height + 4, high, 0))
    rows = near_rows(height, own, halo, passed, scratch)
    gradient(last_near_order(height), rows, weights, aims, known, inside, emit, (), False, 2)


def last_far(low, far, z_in, m_in, v_in, aims, known, inside, *refs):
    passed, refs = refs[:4], refs[4:]
    weights, refs = refs[:7], refs[7:]
    ready, outs, helds, refs = refs[:3], refs[3:6], refs[6:9], refs[9:]
    halo, *scratch, sem = refs
    height, breadth = outs[0].shape[:2]
    strip = low.shape[1] - 2
    copies = []

    def send(row, number, held, at):
        copy = pltpu.make_async_copy(
            held.at[at, pl.ds(SIDE, breadth)],
            outs[number].at[pick_row(row, height)],
            sem.at[number, row],
        )
        copy.start()
        copies.append(copy)

    for row in range(EDGE, height):
        for number in range(3):
            send(row, number, ready[number], row - EDGE)
    widen(halo, far, strip, far_there())

    def emit(row, grad):
        for number, value in enumerate(adam(z_in[row], m_in[row], v_in[row], grad)):
            keep_row(helds[number], row, value, strip)
            send(row, number, helds[number], row)

    rows = far_rows(place_rows((4, 8, low, 0)), halo, passed, scratch)
    gradient(last_far_order(height), rows, weights, aims, known, inside, emit, (), False, 2)
    for copy in copies:
        copy.wait()


def body(
    latent,
    moment_one,
    moment_two,
    hole_mask,
    target_rgb,
    kernel_one,
    bias_one,
    kernel_two,
    bias_two,
    rgb_weight,
):
    height, breadth, size = latent.shape
    strip = (breadth + 2 * SIDE) // STRIPS
    assert strip * STRIPS == breadth + 2 * SIDE and height % 2 == 0 and height >= 8
    assert height * PLANES <= size and breadth == size and lax.axis_size("cores") == 2
    pixels = strip * STRIPS
    sides = 1 if lax.axis_size("col") == 2 else 2
    dma = pltpu.SemaphoreType.DMA
    _, at_low, step = piece_counts(height)
    block = (at_low + 3 * step, SIDE, size)
    tall = lambda rows: shape((rows, strip + 2, STRIPS, size), BF16)
    short = lambda rows: shape((rows, strip, STRIPS, size), BF16)
    lines_of = lambda rows: shape((rows, pixels, size), F32)
    aims_of = lambda rows: shape((rows // 2, pixels, 2 * size), F32)
    vmem = lambda like: pltpu.VMEM(like.shape, like.dtype)
    work = 2 * 12 * 2 * pixels * size * size

    given = tuple(map(in_hbm, (latent, moment_one, moment_two)))
    *columns, turned = call(
        functools.partial(pack_columns, sides),
        [shape(block, BF16)] * sides
        + [shape((breadth, size), BF16)],
        [HBM] * 5,
        [VMEM] * (sides + 1),
        [
            pltpu.VMEM((3, 2, height, SIDE, size), F32),
            pltpu.VMEM(target_rgb.shape, F32),
            pltpu.VMEM(hole_mask.shape, jnp.int32),
            pltpu.VMEM((size, breadth), F32),
            pltpu.VMEM(block, F32),
            dma((4, 2)),
        ],
        (10**6, 10**6),
        "pack_columns",
    )(*given, in_hbm(target_rgb), in_hbm(hole_mask))
    columns = [swap(piece, "col", side) for side, piece in enumerate(columns)]

    matrix = shape((12 * size, 2 * size), BF16)
    *weights, latent = call(
        pack_weights,
        [matrix] * 4 + [shape((2 * size, 2 * size), BF16)] * 2 + [shape((2, 8, 2 * size), F32)]
        + [shape(latent.shape, F32)],
        [VMEM] * 2 + [HBM] * 4,
        [VMEM] * 8,
        [
            pltpu.VMEM((2 * size, 2 * size), F32),
            pltpu.VMEM(rgb_weight.shape, BF16),
            pltpu.VMEM((1, size), F32),
            pltpu.VMEM((1, size), F32),
            dma((4,)),
        ],
        (10**6, 4 * 10**6),
        "pack_weights",
    )(
        kernel_one,
        kernel_two,
        *map(in_hbm, (rgb_weight, bias_one[None], bias_two[None])),
        given[0],
    )

    columns, weights = lax.optimization_barrier((columns, weights))
    own, lines, near, far, spots, inside = call(
        functools.partial(pack_rows, sides),
        [tall(height), lines_of(height), short(EDGE + 1), short(EDGE + 1)]
        + [shape((strip, STRIPS, size), BF16), shape((pixels, size), F32)],
        [VMEM] * (2 + sides),
        [VMEM] * 6,
        [vmem(lines_of(height)), vmem(lines_of(1))],
        (10**6, 4 * 10**6),
        "pack_rows",
    )(latent, turned, *columns)
    near = swap_near(near)
    far = swap_far(far)

    passed = [tall(2), lines_of(2), tall(2), tall(2)]
    near_scratch = [
        vmem(tall(height)),
        vmem(lines_of(height - 2)),
        vmem(tall(height - 2)),
        vmem(tall(height - 4)),
    ]
    far_scratch = [vmem(tall(4)), vmem(lines_of(2)), vmem(tall(4)), vmem(tall(4))]
    near_work = (2 * (height - 1) + 0) * work, 10**7
    far_work = 8 * work, 10**7
    rest, some = height - EDGE, EDGE

    *results, near_next, z_high, m_high, v_high, m_rest, v_rest, aims_near, known_near = call(
        functools.partial(first_near, sides),
        passed
        + [tall(rest), short(EDGE), lines_of(rest), lines_of(rest), lines_of(rest)]
        + [lines_of(some), lines_of(some), aims_of(height), aims_of(height)],
        [VMEM] * (7 + sides + 7),
        [VMEM] * 13,
        [vmem(tall(EDGE)), vmem(lines_of(height)), vmem(lines_of(height))] + near_scratch,
        near_work,
        "first_near",
    )(own, lines, moment_one, moment_two, near, spots, inside, *columns, *weights)
    *handed, high = results
    near_next = swap_near(near_next)

    low, far_next, z_low, m_low, v_low, aims_far, known_far = call(
        first_far,
        [tall(some), short(EDGE), lines_of(some), lines_of(some), lines_of(some)]
        + [aims_of(4), aims_of(4)],
        [VMEM] * (7 + 4 + 7),
        [VMEM] * 7,
        [vmem(tall(EDGE))] + far_scratch,
        far_work,
        "first_far",
    )(own, lines, m_rest, v_rest, far, spots, inside, *handed, *weights)
    far_next = swap_far(far_next)

    out = shape(latent.shape, F32)
    results = call(
        last_near,
        passed + [lines_of(rest)] * 3,
        [VMEM] * (9 + 7),
        [VMEM] * 7,
        [vmem(tall(EDGE))] + near_scratch,
        near_work,
        "last_near",
    )(low, high, near_next, z_high, m_high, v_high, aims_near, known_near, inside, *weights)
    handed, ready = results[:4], results[4:]
    return call(
        last_far,
        [out] * 3,
        [VMEM] * (8 + 4 + 7 + 3),
        [HBM] * 3,
        [vmem(lines_of(some))] * 3 + [vmem(tall(EDGE))] + far_scratch + [dma((3, height))],
        far_work,
        "last_far",
    )(low, far_next, z_low, m_low, v_low, aims_far, known_far, inside, *handed, *weights, *ready)


def solution(mesh):
    tile = P(("parts", "row", "cores"), "col", None)
    return jax.shard_map(
        body,
        mesh=mesh,
        in_specs=(
            tile,
            tile,
            tile,
            P(("parts", "row", "cores"), "col"),
            P(None, ("parts", "row", "cores"), "col"),
            P(),
            P(),
            P(),
            P(),
            P(),
        ),
        out_specs=(tile, tile, tile),
        check_vma=False,
    )
```

```python
import functools
import math

import jax
import jax.numpy as jnp
from jax import lax
from jax.experimental import pallas as pl
from jax.experimental.pallas import tpu as pltpu
from jax.sharding import PartitionSpec as P

STEPS = 2

BETA_ONE = 0.6
BETA_TWO = 0.9
LEARN_RATE = 0.4
EPSILON = 1e-08

ROWS = ("row", "cores")
STRIPS = 16
SIDE = 8
EDGE = 4
PLANES = 7
VMEM = pl.BlockSpec(memory_space=pltpu.VMEM)
HBM = pl.BlockSpec(memory_space=pltpu.HBM)
F32 = jnp.float32
BF16 = jnp.bfloat16


def row_place():
    cores = lax.axis_size("cores")
    return lax.axis_index("row") * cores + lax.axis_index("cores")


def pairs(count, parity):
    chosen = []
    for low in range(parity, count - 1, 2):
        chosen += [(low, low + 1), (low + 1, low)]
    return chosen


def swap(block, axes, parity):
    return lax.ppermute(block, axes, pairs(lax.axis_size(axes), parity))


def swap_near(block):
    return swap(block, ROWS, 0)


def swap_far(block):
    rows, cols, cores = (lax.axis_size(name) for name in ("row", "col", "cores"))
    count = rows * cores

    def index(place, col):
        return (place // cores * cols + col) * cores + place % cores

    chosen = []
    for col in range(cols):
        chosen += [(index(a, col), index(b, col)) for a, b in pairs(count, 1)]
    for place in (0, count - 1):
        chosen += [(index(place, a), index(place, b)) for a, b in pairs(cols, 0)]
    return lax.ppermute(block, ("row", "col", "cores"), sorted(chosen))


def far_there():
    place, count = row_place(), lax.axis_size("row") * lax.axis_size("cores")
    odd = lax.rem(place, 2) == 1
    return jnp.where(odd, place < count - 1, place > 0).astype(F32)


def call(kernel, out_shape, in_specs, out_specs, scratch, cost, name, aliases=None, limit=24 << 20):
    return pl.pallas_call(
        kernel,
        out_shape=out_shape,
        in_specs=in_specs,
        out_specs=out_specs,
        scratch_shapes=scratch,
        compiler_params=pltpu.CompilerParams(vmem_limit_bytes=limit),
        cost_estimate=pl.CostEstimate(flops=cost[0], bytes_accessed=cost[1], transcendentals=0),
        input_output_aliases=aliases or {},
        name=name,
    )


def in_hbm(array):
    return pltpu.with_memory_space_constraint(array, pltpu.HBM)


def shape(dims, dtype):
    return jax.ShapeDtypeStruct(dims, dtype)


def pick_row(index, height):
    odd = lax.rem(row_place(), 2) == 1
    return jnp.where(odd, height - 1 - index, index)


def pick_partner_row(index, height):
    odd = lax.rem(row_place(), 2) == 1
    return jnp.where(odd, index, height - 1 - index)


def piece_counts(height):
    return height, height + 2, height * EDGE // SIDE


def pack_columns(sides, latent, first, second, target, mask, *rest):
    outs, rest = rest[:sides], rest[sides:]
    turned, close, away, ends, aim, known, planes, flat, sem = rest
    height, breadth = latent.shape[0], latent.shape[1]
    early = [
        pltpu.make_async_copy(target, aim, sem.at[3, 0]),
        pltpu.make_async_copy(mask, known, sem.at[3, 1]),
    ]
    copies = [
        pltpu.make_async_copy(
            source.at[:, pl.ds(start, SIDE)], ends.at[number, end], sem.at[number, end]
        )
        for number, source in enumerate((latent, first, second))
        for end, start in enumerate((0, breadth - SIDE))
    ]
    for copy in early + copies:
        copy.start()
    planes[...] = jnp.zeros_like(planes)
    for copy in early:
        copy.wait()
    keep = known[...].astype(F32)
    for color in range(3):
        wanted = keep * aim[color]
        high = wanted.astype(BF16).astype(F32)
        planes[pl.ds(color, height, stride=PLANES), :] = high
        planes[pl.ds(color + 3, height, stride=PLANES), :] = wanted - high
    planes[pl.ds(6, height, stride=PLANES), :] = keep
    swapped = planes[...].T
    turned[...] = swapped.astype(BF16)
    odd = lax.rem(row_place(), 2) == 1
    start = (height - 2) * PLANES
    low, high = planes[:STRIPS], planes[start : start + STRIPS]
    close[...] = jnp.where(odd, low, high).astype(BF16)
    away[...] = jnp.where(odd, high, low).astype(BF16)
    for copy in copies:
        copy.wait()
    col_even = lax.rem(lax.axis_index("col"), 2) == 0
    _, at_low, step = piece_counts(height)
    for side, out in enumerate(outs):
        right = col_even if side == 0 else jnp.logical_not(col_even)
        flat[height] = jnp.where(right, swapped[breadth - SIDE :], swapped[:SIDE])
        flat[height + 1] = jnp.zeros(flat.shape[1:], F32)
        for row in range(height):
            source = pick_row(row, height)
            own = [jnp.where(right, ends[n, 1, source], ends[n, 0, source]) for n in range(3)]
            flat[row] = own[0]
            for number, piece in enumerate(own[1:]):
                near = jnp.where(right, piece[SIDE - EDGE :], piece[:EDGE])
                at = EDGE * row
                flat[at_low + number * step + at // SIDE, at % SIDE : at % SIDE + EDGE] = near
        out[...] = flat[...].astype(BF16)


def pack_weights(one, two, rgb, bias_one, bias_two, *refs):
    given, refs = refs[:1], refs[1:]
    matrices, loaded, refs = refs[:7], refs[7 : 7 + 1], refs[7 + 1 :]
    ahead_one, ahead_two, back_one, back_two, colors, spread, bias = matrices
    held, *small, sem = refs
    copies = [
        pltpu.make_async_copy(source, dest, sem.at[number])
        for number, (source, dest) in enumerate(
            zip((rgb, bias_one, bias_two, *given), (*small, *loaded))
        )
    ]
    rgb, bias_one, bias_two = small
    for copy in copies:
        copy.start()
    size = one.shape[2]
    half = jnp.asarray(0.5, BF16)
    odd = lax.rem(row_place(), 2) == 1
    for kernel, ahead, back in ((one, ahead_one, back_one), (two, ahead_two, back_two)):
        for row in range(4):
            for col in range(3):
                at = (row * 3 + col) * size
                for out in range(2):
                    tap = row - out
                    if 0 <= tap <= 2:
                        front = kernel[jnp.where(odd, 2 - tap, tap), col] * half
                        rear = kernel[jnp.where(odd, tap, 2 - tap), 2 - col]
                        rear = rear.astype(F32).T.astype(BF16)
                        if kernel is two:
                            rear = rear * half
                    else:
                        front = rear = jnp.zeros((size, size), BF16)
                    ahead[at : at + size, out * size : (out + 1) * size] = front
                    back[at : at + size, out * size : (out + 1) * size] = rear
    held[...] = jnp.zeros_like(held)
    for copy in copies[:3]:
        copy.wait()
    for at in (0, size):
        held[at : at + 3, at : at + size] = rgb[...].astype(F32)
        held[at + 3 : at + 6, at : at + size] = rgb[...].astype(F32)
    colors[...] = held[...].astype(BF16)
    spread[...] = (0.5 * held[...]).astype(BF16)
    for number, given in enumerate((bias_one, bias_two)):
        for at in (0, size):
            bias[number, :, at : at + size] = jnp.broadcast_to(0.5 * given[...], (8, size))
    for copy in copies[3:]:
        copy.wait()


def put(dest, row, value, strip, keep=None):
    low, high = value[:STRIPS], value[(strip - 1) * STRIPS :]
    value = value.astype(BF16)
    if keep is not None:
        value = value * keep
        low = low * keep[:STRIPS].astype(F32)
        high = high * keep[(strip - 1) * STRIPS :].astype(F32)
    dest[row, 1 : strip + 1] = value.reshape(strip, STRIPS, -1)
    dest[row, 0] = pltpu.roll(high, 1, 0).astype(BF16)
    dest[row, strip + 1] = pltpu.roll(low, STRIPS - 1, 0).astype(BF16)


def widen(dest, source, strip, there=None):
    for row in range(EDGE):
        at = row * strip
        value = source[at : at + strip]
        low, high = source[at].astype(F32), source[at + strip - 1].astype(F32)
        if there is not None:
            value, low, high = value * there.astype(BF16), low * there, high * there
        dest[row, 1 : strip + 1] = value
        dest[row, 0] = pltpu.roll(high, 1, 0).astype(BF16)
        dest[row, strip + 1] = pltpu.roll(low, STRIPS - 1, 0).astype(BF16)


def strips_of(source, row, strip):
    return jnp.concatenate(
        [source[row, pl.ds(j, STRIPS, stride=strip), :] for j in range(strip)], axis=0
    )


def fill_sides(sides, held, pieces, spread, rows):
    breadth = held.shape[1] - 2 * SIDE
    col_even = lax.rem(lax.axis_index("col"), 2) == 0
    for side in range(2):
        right = col_even if side == 0 else jnp.logical_not(col_even)
        spot = pl.ds(pl.multiple_of(jnp.where(right, SIDE + breadth, 0), SIDE), SIDE)
        for row in range(rows):
            if side < sides:
                held[row, spot] = spread(pieces[side], row, right)
            else:
                held[row, spot] = jnp.zeros((SIDE, held.shape[2]), F32)


def nearest(pieces, number, height, row, right):
    _, at_low, step = piece_counts(height)
    at = EDGE * row
    piece = pieces[at_low + number * step + at // SIDE].astype(F32)
    piece = piece[at % SIDE : at % SIDE + EDGE]
    blank = jnp.zeros((SIDE - EDGE, piece.shape[1]), F32)
    return jnp.where(
        right,
        jnp.concatenate([piece, blank], axis=0),
        jnp.concatenate([blank, piece], axis=0),
    )


def pack_rows(sides, latent, turned, close, away, *rest):
    pieces, rest = rest[:sides], rest[sides:]
    own, lines, near, far, spots, inside, held, turn = rest
    height, breadth, size = latent.shape
    strip = own.shape[1] - 2
    for row in range(height):
        held[row, SIDE : SIDE + breadth] = latent[pick_row(row, height)]
    fill_sides(
        sides,
        held,
        pieces,
        lambda piece, row, right: piece[row].astype(F32),
        height,
    )
    turn[0, SIDE : SIDE + breadth] = turned[...].astype(F32)
    fill_sides(sides, turn, pieces, lambda piece, row, right: piece[height].astype(F32), 1)
    spots[...] = strips_of(turn, 0, strip).astype(BF16).reshape(strip, STRIPS, size)
    ends = jnp.concatenate([turn[0, :SIDE], turn[0, SIDE + breadth :]], axis=0).astype(BF16)
    near[EDGE * strip] = close[...]
    far[EDGE * strip] = away[...]
    near[EDGE * strip + 1] = ends
    far[EDGE * strip + 1] = ends
    for row in range(height):
        line = strips_of(held, row, strip)
        lines[row] = line
        put(own, row, line, strip)
        short = line.astype(BF16).reshape(strip, STRIPS, size)
        if row < EDGE:
            far[(EDGE - 1 - row) * strip : (EDGE - row) * strip] = short
        if row >= height - EDGE:
            near[(height - 1 - row) * strip : (height - row) * strip] = short
    col = lax.axis_index("col")
    base = col * breadth - SIDE
    total = lax.axis_size("col") * breadth
    for j in range(strip):
        at = lax.broadcasted_iota(jnp.int32, (STRIPS, size), 0) * strip + (j + base)
        inside[j * STRIPS : (j + 1) * STRIPS] = ((at >= 0) & (at < total)).astype(F32)


def aim_rows(aims, known, spots):
    size = aims.shape[2] // 2
    lane_in = lax.broadcasted_iota(jnp.int32, (size, 2 * size), 0)
    lane_out = lax.broadcasted_iota(jnp.int32, (size, 2 * size), 1)
    color = lax.rem(lane_out, 3)
    aimed = (lane_out < 6) & ((lane_in == color) | (lane_in == color + 3))
    masked = (lane_out >= size) & (lane_out < size + 6) & (lane_in == 6)
    chosen = (aimed | masked).astype(F32).astype(BF16)

    def aim(row, spot, source):
        spot = spot() if callable(spot) else spot
        value = pltpu.roll(spot, lax.rem(size - PLANES * source, size), 1)
        both = jnp.dot(value.astype(BF16), chosen, preferred_element_type=F32)
        lanes = slice(row % 2 * size, (row % 2 + 1) * size)
        aims[row // 2, :, lanes] = both[:, :size]
        known[row // 2, :, lanes] = both[:, size:]

    return [functools.partial(aim, row, *spot) for row, spot in enumerate(spots)]


def conv_pairs(rows, firsts, weights, strip, count):
    taps = []
    for down in range(4):
        for across in range(3):
            parts = []
            for first in firsts:
                source, at = rows[first - 1 + down]
                parts.append(source[at, across : across + strip].reshape(strip * STRIPS, -1))
            taps.append(jnp.concatenate(parts, axis=0) if len(parts) > 1 else parts[0])
    size = weights.shape[0] // count
    parts = [
        jnp.dot(
            jnp.concatenate(taps[len(taps) // count * part : len(taps) // count * (part + 1)], axis=1),
            weights[size * part : size * (part + 1)],
            preferred_element_type=F32,
        )
        for part in range(count)
    ]
    total = parts[0]
    for part in parts[1:]:
        total = total + part
    pixels = strip * STRIPS
    return [total[at * pixels : (at + 1) * pixels] for at in range(len(firsts))]


def gradient(order, rows, weights, aims, known, inside, emit, beside=(), parts=False, cuts=1):
    wide, hidden, slope, grad_two, grad_one = rows
    ahead_one, ahead_two, back_one, back_two, colors, spread, bias = weights
    pixels, size = inside.shape
    strip = pixels // STRIPS
    there = far_there()
    low = min(min(firsts) for stage, firsts in filter(None, order) if stage == 1)

    def keep_of(row):
        return (inside[...] * there if row < EDGE else inside[...]).astype(BF16)

    def half_of(both, half):
        return both[:, half * size : (half + 1) * size]

    def gate(both, number):
        value = both + bias[number, :1]
        twice = jnp.tanh(value) + 1.0
        hid = value * twice
        return hid, twice + hid * (2.0 - twice)

    def ahead_first(firsts):
        results = conv_pairs(wide, firsts, ahead_one, strip, cuts)
        yield
        for first, both in zip(firsts, results):
            hid, twice = gate(both, 0)
            for half in range(2):
                row = first + half
                put(*hidden[row], half_of(hid, half), strip, keep_of(row))
                if row in slope:
                    held, at = slope[row]
                    held[at] = half_of(twice, half)

    lane = lax.rem(lax.broadcasted_iota(jnp.int32, (pixels, 2 * size), 1), size)

    def ahead_second(firsts):
        results = conv_pairs(hidden, firsts, ahead_two, strip, cuts)
        yield
        for first, both in zip(firsts, results):
            number = (first - low) // 2
            hid, twice = gate(both, 1)
            color = lax.dot_general(
                hid.astype(BF16), colors[...], (((1,), (1,)), ((), ())), preferred_element_type=F32
            )
            if parts:
                yield
            residual = known[number] * color - aims[number]
            rest = residual - residual.astype(BF16).astype(F32)
            split = jnp.where(lane < 3, residual, rest).astype(BF16)
            back = jnp.dot(split, spread[...], preferred_element_type=F32)
            if parts:
                yield
            result = back * twice
            for half in range(2):
                put(*grad_two[first + half], half_of(result, half), strip)

    def back_second(firsts):
        results = conv_pairs(grad_two, firsts, back_two, strip, cuts)
        yield
        for first, both in zip(firsts, results):
            for half in range(2):
                row = first + half
                held, at = slope[row]
                put(*grad_one[row], half_of(both, half) * held[at], strip, keep_of(row))

    def back_first(firsts):
        results = conv_pairs(grad_one, firsts, back_one, strip, cuts)
        yield
        for first, both in zip(firsts, results):
            for half in range(2):
                emit(first + half - EDGE, half_of(both, half))

    stages = (ahead_first, ahead_second, back_second, back_first)
    beside = list(beside)
    active = []
    slots = list(order)
    while slots or active:
        started = None
        if slots:
            item = slots.pop(0)
            if item is not None:
                started = stages[item[0]](item[1])
                next(started)
        if beside:
            beside.pop(0)()
        active = [task for task in active if next(task, active) is None]
        if started is not None:
            active.append(started)


def adam(current, first, second, grad):
    first = BETA_ONE * first + (1.0 - BETA_ONE) * grad
    second = BETA_TWO * second + ((1.0 - BETA_TWO) * grad) * grad
    root = second * lax.rsqrt(second)
    return current - (LEARN_RATE * first) / (root + EPSILON), first, second


def floored(second):
    return jnp.maximum(second, 1e-30)


def place_rows(*parts):
    rows = {}
    for first, last, held, at in parts:
        for row in range(first, last):
            rows[row] = (held, at + row - first)
    return rows


def first_near_order(height):
    return [(0, (5, 7)), (0, (9, 11)), (0, (13,)), (1, (6, 8)), (1, (10, 12)), None, (2, (7, 9)), (2, (11,)), (3, (8,)), (3, (10,))]


def last_near_order(height):
    return [(0, (5, 7, 9)), (0, (11, 13)), (1, (6,)), (1, (8,)), (1, (10,)), (1, (12,)), (2, (7,)), (2, (9,)), (2, (11,)), (3, (8,)), (3, (10,))]


def first_far_order(height):
    return [(0, (3,)), (0, (1,)), (1, (4,)), (1, (2,)), (2, (5,)), (2, (3,)), (3, (6,)), (3, (4,))]


def last_far_order(height):
    return [(0, (3,)), (0, (1,)), (1, (4,)), (1, (2,)), (2, (5,)), (2, (3,)), (3, (6,)), (3, (4,))]


def near_rows(height, own, halo, passed, scratch):
    hidden, slope, grad_two, grad_one = scratch
    hidden_out, slope_out, two_out, one_out = passed
    return (
        {**own, **place_rows((height + 4, height + 8, halo, 0))},
        place_rows((5, 7, hidden_out, 0), (7, height + 7, hidden, 0)),
        place_rows((5, 7, slope_out, 0), (7, height + 5, slope, 0)),
        place_rows((6, 8, two_out, 0), (8, height + 6, grad_two, 0)),
        place_rows((7, 9, one_out, 0), (9, height + 5, grad_one, 0)),
    )


def far_rows(own, halo, passed, scratch):
    hidden, slope, grad_two, grad_one = scratch
    hidden_in, slope_in, two_in, one_in = passed
    return (
        {**own, **place_rows((0, 4, halo, 0))},
        place_rows((1, 5, hidden, 0), (5, 7, hidden_in, 0)),
        place_rows((3, 5, slope, 0), (5, 7, slope_in, 0)),
        place_rows((2, 6, grad_two, 0), (6, 8, two_in, 0)),
        place_rows((3, 7, grad_one, 0), (7, 9, one_in, 0)),
    )


def once(make):
    made = []

    def get():
        if not made:
            made.append(make())
        return made[0]

    return get


def pair_up(tasks):
    def both(one, two):
        one()
        two()

    return [functools.partial(both, *tasks[at : at + 2]) for at in range(0, len(tasks), 2)]


def spread_spot(sent, turn, strip, first):
    breadth = turn.shape[1] - 2 * SIDE
    size = turn.shape[2]
    middle = sent[EDGE * strip].astype(F32)
    rest = jnp.zeros((size - STRIPS, breadth), F32)
    turn[0, SIDE : SIDE + breadth] = jnp.concatenate([middle, rest], axis=0).T
    ends = pltpu.roll(sent[EDGE * strip + 1].astype(F32), lax.rem(size - PLANES * first, size), 1)
    turn[0, :SIDE] = ends[:SIDE]
    turn[0, SIDE + breadth :] = ends[SIDE:]
    return strips_of(turn, 0, strip)


def flat_spot(spots):
    return spots[...].reshape(-1, spots.shape[-1]).astype(F32)


def first_near(sides, own, lines, moment_one, moment_two, near, spots, inside, *refs):
    pieces, refs = refs[:sides], refs[sides:]
    weights, refs = refs[:7], refs[7:]
    passed, refs = refs[:4], refs[4:]
    (new, near_out, z_out, m_out, v_out, m_rest, v_rest, aims, known), refs = refs[:9], refs[9:]
    halo, turn, m_held, v_held, *scratch = refs
    height, breadth = moment_one.shape[:2]
    strip = own.shape[1] - 2
    widen(halo, near, strip)
    start = jnp.where(lax.rem(row_place(), 2) == 1, height - 2, 0)
    mine, theirs = flat_spot(spots), once(lambda: spread_spot(near, turn, strip, start))
    tasks = aim_rows(
        aims,
        known,
        [(mine, pick_row(row, height)) for row in range(2, height)]
        + [(theirs, pick_partner_row(row, height) - start) for row in (height - 1, height - 2)],
    )
    for number, (held, moment) in enumerate(((m_held, moment_one), (v_held, moment_two))):
        for row in range(height):
            held[row, SIDE : SIDE + breadth] = moment[pick_row(row, height)]
        fill_sides(
            sides,
            held,
            pieces,
            lambda piece, row, right: nearest(piece, number, height, row, right),
            height,
        )
    for row in range(EDGE):
        m_rest[row] = strips_of(m_held, row, strip)
        v_rest[row] = floored(strips_of(v_held, row, strip))

    def emit(row, grad):
        current, first, second = adam(
            lines[row], strips_of(m_held, row, strip), floored(strips_of(v_held, row, strip)), grad
        )
        current = current * inside[...]
        at = row - EDGE
        z_out[at] = current
        m_out[at] = first
        v_out[at] = second
        put(new, at, current, strip)
        if row >= height - EDGE:
            short = current.astype(BF16).reshape(strip, *near_out.shape[1:])
            near_out[(height - 1 - row) * strip : (height - row) * strip] = short

    rows = near_rows(height, place_rows((4, height + 4, own, 0)), halo, passed, scratch)
    gradient(first_near_order(height), rows, weights, aims, known, inside, emit, pair_up(tasks), False, 2)


def first_far(own, lines, m_rest, v_rest, far, spots, inside, *refs):
    passed, refs = refs[:4], refs[4:]
    weights, refs = refs[:7], refs[7:]
    (new, far_out, z_out, m_out, v_out, aims, known), refs = refs[:7], refs[7:]
    halo, turn, *scratch = refs
    height = own.shape[0]
    strip = own.shape[1] - 2
    widen(halo, far, strip, far_there())
    start = jnp.where(lax.rem(row_place(), 2) == 1, 0, height - 2)
    mine = flat_spot(spots)
    theirs = once(lambda: spread_spot(far, turn, strip, start) * far_there())
    tasks = aim_rows(
        aims,
        known,
        [(theirs, pick_partner_row(row, height) - start) for row in (1, 0)]
        + [(mine, pick_row(row, height)) for row in range(2)],
    )

    def emit(row, grad):
        current, first, second = adam(lines[row], m_rest[row], v_rest[row], grad)
        current = current * inside[...]
        z_out[row] = current
        m_out[row] = first
        v_out[row] = second
        put(new, row, current, strip)
        short = current.astype(BF16).reshape(strip, *far_out.shape[1:])
        far_out[(EDGE - 1 - row) * strip : (EDGE - row) * strip] = short

    rows = far_rows(place_rows((4, 8, own, 0)), halo, passed, scratch)
    gradient(first_far_order(height), rows, weights, aims, known, inside, emit, pair_up(tasks)[::-1], False, 2)


def keep_row(held, at, value, strip):
    for j in range(strip):
        held[at, pl.ds(j, STRIPS, stride=strip), :] = value[j * STRIPS : (j + 1) * STRIPS]


def last_near(low, high, near, z_in, m_in, v_in, aims, known, inside, *refs):
    weights, refs = refs[:7], refs[7:]
    passed, refs = refs[:4], refs[4:]
    helds, refs = refs[:3], refs[3:]
    halo, *scratch = refs
    height = EDGE + high.shape[0]
    strip = low.shape[1] - 2
    widen(halo, near, strip)

    def emit(row, grad):
        at = row - EDGE
        for held, value in zip(helds, adam(z_in[at], m_in[at], v_in[at], grad)):
            keep_row(held, at, value, strip)

    own = place_rows((4, 8, low, 0), (8, height + 4, high, 0))
    rows = near_rows(height, own, halo, passed, scratch)
    gradient(last_near_order(height), rows, weights, aims, known, inside, emit, (), False, 2)


def last_far(low, far, z_in, m_in, v_in, aims, known, inside, *refs):
    passed, refs = refs[:4], refs[4:]
    weights, refs = refs[:7], refs[7:]
    ready, outs, helds, refs = refs[:3], refs[3:6], refs[6:9], refs[9:]
    halo, *scratch, sem = refs
    height, breadth = outs[0].shape[:2]
    strip = low.shape[1] - 2
    copies = []

    def send(row, number, held, at):
        copy = pltpu.make_async_copy(
            held.at[at, pl.ds(SIDE, breadth)],
            outs[number].at[pick_row(row, height)],
            sem.at[number, row],
        )
        copy.start()
        copies.append(copy)

    for row in range(EDGE, height):
        for number in range(3):
            send(row, number, ready[number], row - EDGE)
    widen(halo, far, strip, far_there())

    def emit(row, grad):
        for number, value in enumerate(adam(z_in[row], m_in[row], v_in[row], grad)):
            keep_row(helds[number], row, value, strip)
            send(row, number, helds[number], row)

    rows = far_rows(place_rows((4, 8, low, 0)), halo, passed, scratch)
    gradient(last_far_order(height), rows, weights, aims, known, inside, emit, (), False, 2)
    for copy in copies:
        copy.wait()


def body(
    latent,
    moment_one,
    moment_two,
    hole_mask,
    target_rgb,
    kernel_one,
    bias_one,
    kernel_two,
    bias_two,
    rgb_weight,
):
    height, breadth, size = latent.shape
    strip = (breadth + 2 * SIDE) // STRIPS
    assert strip * STRIPS == breadth + 2 * SIDE and height % 2 == 0 and height >= 8
    assert height * PLANES <= size and breadth == size and lax.axis_size("cores") == 2
    pixels = strip * STRIPS
    sides = 1 if lax.axis_size("col") == 2 else 2
    dma = pltpu.SemaphoreType.DMA
    _, at_low, step = piece_counts(height)
    block = (at_low + 2 * step, SIDE, size)
    tall = lambda rows: shape((rows, strip + 2, STRIPS, size), BF16)
    short = lambda tiles: shape((EDGE * strip + tiles, STRIPS, size), BF16)
    lines_of = lambda rows: shape((rows, pixels, size), F32)
    aims_of = lambda rows: shape((rows // 2, pixels, 2 * size), F32)
    vmem = lambda like: pltpu.VMEM(like.shape, like.dtype)
    work = 2 * 12 * 2 * pixels * size * size

    given = tuple(map(in_hbm, (latent, moment_one, moment_two)))
    *columns, turned, close, away = call(
        functools.partial(pack_columns, sides),
        [shape(block, BF16)] * sides
        + [shape((breadth, size), BF16)]
        + [shape((STRIPS, breadth), BF16)] * 2,
        [HBM] * 5,
        [VMEM] * (sides + 3),
        [
            pltpu.VMEM((3, 2, height, SIDE, size), F32),
            pltpu.VMEM(target_rgb.shape, F32),
            pltpu.VMEM(hole_mask.shape, jnp.int32),
            pltpu.VMEM((size, breadth), F32),
            pltpu.VMEM(block, F32),
            dma((4, 2)),
        ],
        (10**6, 10**6),
        "pack_columns",
    )(*given, in_hbm(target_rgb), in_hbm(hole_mask))
    columns = [swap(piece, "col", side) for side, piece in enumerate(columns)]

    matrix = shape((12 * size, 2 * size), BF16)
    *weights, latent = call(
        pack_weights,
        [matrix] * 4 + [shape((2 * size, 2 * size), BF16)] * 2 + [shape((2, 8, 2 * size), F32)]
        + [shape(latent.shape, F32)],
        [VMEM] * 2 + [HBM] * 4,
        [VMEM] * 8,
        [
            pltpu.VMEM((2 * size, 2 * size), F32),
            pltpu.VMEM(rgb_weight.shape, BF16),
            pltpu.VMEM((1, size), F32),
            pltpu.VMEM((1, size), F32),
            dma((4,)),
        ],
        (10**6, 4 * 10**6),
        "pack_weights",
    )(
        kernel_one,
        kernel_two,
        *map(in_hbm, (rgb_weight, bias_one[None], bias_two[None])),
        given[0],
    )

    columns, weights = lax.optimization_barrier((columns, weights))
    own, lines, near, far, spots, inside = call(
        functools.partial(pack_rows, sides),
        [tall(height), lines_of(height), short(2), short(2)]
        + [shape((strip, STRIPS, size), BF16), shape((pixels, size), F32)],
        [VMEM] * (4 + sides),
        [VMEM] * 6,
        [vmem(lines_of(height)), vmem(lines_of(1))],
        (10**6, 4 * 10**6),
        "pack_rows",
    )(latent, turned, close, away, *columns)
    near = swap_near(near)
    far = swap_far(far)

    passed = [tall(2), lines_of(2), tall(2), tall(2)]
    near_scratch = [
        vmem(tall(height)),
        vmem(lines_of(height - 2)),
        vmem(tall(height - 2)),
        vmem(tall(height - 4)),
    ]
    far_scratch = [vmem(tall(4)), vmem(lines_of(2)), vmem(tall(4)), vmem(tall(4))]
    near_work = (2 * (height - 1) + 0) * work, 10**7
    far_work = 8 * work, 10**7
    rest, some = height - EDGE, EDGE

    *results, near_next, z_high, m_high, v_high, m_rest, v_rest, aims_near, known_near = call(
        functools.partial(first_near, sides),
        passed
        + [tall(rest), short(0), lines_of(rest), lines_of(rest), lines_of(rest)]
        + [lines_of(some), lines_of(some), aims_of(height), aims_of(height)],
        [VMEM] * (7 + sides + 7),
        [VMEM] * 13,
        [vmem(tall(EDGE)), vmem(lines_of(1)), vmem(lines_of(height)), vmem(lines_of(height))]
        + near_scratch,
        near_work,
        "first_near",
    )(own, lines, moment_one, moment_two, near, spots, inside, *columns, *weights)
    *handed, high = results
    near_next = swap_near(near_next)

    low, far_next, z_low, m_low, v_low, aims_far, known_far = call(
        first_far,
        [tall(some), short(0), lines_of(some), lines_of(some), lines_of(some)]
        + [aims_of(4), aims_of(4)],
        [VMEM] * (7 + 4 + 7),
        [VMEM] * 7,
        [vmem(tall(EDGE)), vmem(lines_of(1))] + far_scratch,
        far_work,
        "first_far",
    )(own, lines, m_rest, v_rest, far, spots, inside, *handed, *weights)
    far_next = swap_far(far_next)

    out = shape(latent.shape, F32)
    results = call(
        last_near,
        passed + [lines_of(rest)] * 3,
        [VMEM] * (9 + 7),
        [VMEM] * 7,
        [vmem(tall(EDGE))] + near_scratch,
        near_work,
        "last_near",
    )(low, high, near_next, z_high, m_high, v_high, aims_near, known_near, inside, *weights)
    handed, ready = results[:4], results[4:]
    return call(
        last_far,
        [out] * 3,
        [VMEM] * (8 + 4 + 7 + 3),
        [HBM] * 3,
        [vmem(lines_of(some))] * 3 + [vmem(tall(EDGE))] + far_scratch + [dma((3, height))],
        far_work,
        "last_far",
    )(low, far_next, z_low, m_low, v_low, aims_far, known_far, inside, *handed, *weights, *ready)


def solution(mesh):
    tile = P(("parts", "row", "cores"), "col", None)
    return jax.shard_map(
        body,
        mesh=mesh,
        in_specs=(
            tile,
            tile,
            tile,
            P(("parts", "row", "cores"), "col"),
            P(None, ("parts", "row", "cores"), "col"),
            P(),
            P(),
            P(),
            P(),
            P(),
        ),
        out_specs=(tile, tile, tile),
        check_vma=False,
    )
```

```python
import functools
import math

import jax
import jax.numpy as jnp
from jax import lax
from jax.experimental import pallas as pl
from jax.experimental.pallas import tpu as pltpu
from jax.sharding import PartitionSpec as P

STEPS = 2

BETA_ONE = 0.6
BETA_TWO = 0.9
LEARN_RATE = 0.4
EPSILON = 1e-08

ROWS = ("row", "cores")
STRIPS = 16
SIDE = 8
EDGE = 4
PLANES = 7
VMEM = pl.BlockSpec(memory_space=pltpu.VMEM)
HBM = pl.BlockSpec(memory_space=pltpu.HBM)
F32 = jnp.float32
BF16 = jnp.bfloat16


def row_place():
    cores = lax.axis_size("cores")
    return lax.axis_index("row") * cores + lax.axis_index("cores")


def pairs(count, parity):
    chosen = []
    for low in range(parity, count - 1, 2):
        chosen += [(low, low + 1), (low + 1, low)]
    return chosen


def swap(block, axes, parity):
    return lax.ppermute(block, axes, pairs(lax.axis_size(axes), parity))


def swap_near(block):
    return swap(block, ROWS, 0)


def swap_far(block):
    rows, cols, cores = (lax.axis_size(name) for name in ("row", "col", "cores"))
    count = rows * cores

    def index(place, col):
        return (place // cores * cols + col) * cores + place % cores

    chosen = []
    for col in range(cols):
        chosen += [(index(a, col), index(b, col)) for a, b in pairs(count, 1)]
    for place in (0, count - 1):
        chosen += [(index(place, a), index(place, b)) for a, b in pairs(cols, 0)]
    return lax.ppermute(block, ("row", "col", "cores"), sorted(chosen))


def far_there():
    place, count = row_place(), lax.axis_size("row") * lax.axis_size("cores")
    odd = lax.rem(place, 2) == 1
    return jnp.where(odd, place < count - 1, place > 0).astype(F32)


def call(kernel, out_shape, in_specs, out_specs, scratch, cost, name, aliases=None, limit=24 << 20):
    return pl.pallas_call(
        kernel,
        out_shape=out_shape,
        in_specs=in_specs,
        out_specs=out_specs,
        scratch_shapes=scratch,
        compiler_params=pltpu.CompilerParams(vmem_limit_bytes=limit),
        cost_estimate=pl.CostEstimate(flops=cost[0], bytes_accessed=cost[1], transcendentals=0),
        input_output_aliases=aliases or {},
        name=name,
    )


def in_hbm(array):
    return pltpu.with_memory_space_constraint(array, pltpu.HBM)


def shape(dims, dtype):
    return jax.ShapeDtypeStruct(dims, dtype)


def pick_row(index, height):
    odd = lax.rem(row_place(), 2) == 1
    return jnp.where(odd, height - 1 - index, index)


def pick_partner_row(index, height):
    odd = lax.rem(row_place(), 2) == 1
    return jnp.where(odd, index, height - 1 - index)


def piece_counts(height):
    return height, height + 2, height * EDGE // SIDE


def pack_columns(sides, latent, first, second, target, mask, *rest):
    outs, rest = rest[:sides], rest[sides:]
    turned, close, away, ends, aim, known, planes, flat, sem = rest
    height, breadth = latent.shape[0], latent.shape[1]
    col_even = lax.rem(lax.axis_index("col"), 2) == 0
    rights = (col_even, jnp.logical_not(col_even))[:sides]
    early = [
        pltpu.make_async_copy(target, aim, sem.at[3, 0]),
        pltpu.make_async_copy(mask, known, sem.at[3, 1]),
    ]
    copies = [
        pltpu.make_async_copy(
            source.at[:, pl.ds(pl.multiple_of(jnp.where(right, breadth - SIDE, 0), SIDE), SIDE)],
            ends.at[number, side],
            sem.at[number, side],
        )
        for number, source in enumerate((latent, first, second))
        for side, right in enumerate(rights)
    ]
    for copy in early + copies:
        copy.start()
    planes[...] = jnp.zeros_like(planes)
    for copy in early:
        copy.wait()
    keep = known[...].astype(F32)
    for color in range(3):
        wanted = keep * aim[color]
        high = wanted.astype(BF16).astype(F32)
        planes[pl.ds(color, height, stride=PLANES), :] = high
        planes[pl.ds(color + 3, height, stride=PLANES), :] = wanted - high
    planes[pl.ds(6, height, stride=PLANES), :] = keep
    swapped = planes[...].T
    turned[...] = swapped.astype(BF16)
    odd = lax.rem(row_place(), 2) == 1
    start = (height - 2) * PLANES
    low, high = planes[:STRIPS], planes[start : start + STRIPS]
    close[...] = jnp.where(odd, low, high).astype(BF16)
    away[...] = jnp.where(odd, high, low).astype(BF16)
    for copy in copies:
        copy.wait()
    _, at_low, step = piece_counts(height)
    for side, (out, right) in enumerate(zip(outs, rights)):
        flat[height] = jnp.where(right, swapped[breadth - SIDE :], swapped[:SIDE])
        flat[height + 1] = jnp.zeros(flat.shape[1:], F32)
        for row in range(height):
            source = pick_row(row, height)
            own = [ends[n, side, source] for n in range(3)]
            flat[row] = own[0]
            for number, piece in enumerate(own[1:]):
                near = jnp.where(right, piece[SIDE - EDGE :], piece[:EDGE])
                at = EDGE * row
                flat[at_low + number * step + at // SIDE, at % SIDE : at % SIDE + EDGE] = near
        out[...] = flat[...].astype(BF16)


def pack_weights(one, two, rgb, bias_one, bias_two, *refs):
    given, refs = refs[:1], refs[1:]
    matrices, loaded, refs = refs[:7], refs[7 : 7 + 1], refs[7 + 1 :]
    ahead_one, ahead_two, back_one, back_two, colors, spread, bias = matrices
    held, *small, sem = refs
    copies = [
        pltpu.make_async_copy(source, dest, sem.at[number])
        for number, (source, dest) in enumerate(
            zip((rgb, bias_one, bias_two, *given), (*small, *loaded))
        )
    ]
    rgb, bias_one, bias_two = small
    for copy in copies:
        copy.start()
    size = one.shape[2]
    half = jnp.asarray(0.5, BF16)
    odd = lax.rem(row_place(), 2) == 1
    for kernel, ahead, back in ((one, ahead_one, back_one), (two, ahead_two, back_two)):
        for row in range(4):
            for col in range(3):
                at = (row * 3 + col) * size
                for out in range(2):
                    tap = row - out
                    if 0 <= tap <= 2:
                        front = kernel[jnp.where(odd, 2 - tap, tap), col] * half
                        rear = kernel[jnp.where(odd, tap, 2 - tap), 2 - col]
                        rear = rear.astype(F32).T.astype(BF16)
                        if kernel is two:
                            rear = rear * half
                    else:
                        front = rear = jnp.zeros((size, size), BF16)
                    ahead[at : at + size, out * size : (out + 1) * size] = front
                    back[at : at + size, out * size : (out + 1) * size] = rear
    held[...] = jnp.zeros_like(held)
    for copy in copies[:3]:
        copy.wait()
    for at in (0, size):
        held[at : at + 3, at : at + size] = rgb[...].astype(F32)
        held[at + 3 : at + 6, at : at + size] = rgb[...].astype(F32)
    colors[...] = held[...].astype(BF16)
    spread[...] = (0.5 * held[...]).astype(BF16)
    for number, given in enumerate((bias_one, bias_two)):
        for at in (0, size):
            bias[number, :, at : at + size] = jnp.broadcast_to(0.5 * given[...], (8, size))
    for copy in copies[3:]:
        copy.wait()


def put(dest, row, value, strip, keep=None):
    low, high = value[:STRIPS], value[(strip - 1) * STRIPS :]
    value = value.astype(BF16)
    if keep is not None:
        value = value * keep
        low = low * keep[:STRIPS].astype(F32)
        high = high * keep[(strip - 1) * STRIPS :].astype(F32)
    dest[row, 1 : strip + 1] = value.reshape(strip, STRIPS, -1)
    dest[row, 0] = pltpu.roll(high, 1, 0).astype(BF16)
    dest[row, strip + 1] = pltpu.roll(low, STRIPS - 1, 0).astype(BF16)


def widen(dest, source, strip, there=None):
    for row in range(EDGE):
        at = row * strip
        value = source[at : at + strip]
        low, high = source[at].astype(F32), source[at + strip - 1].astype(F32)
        if there is not None:
            value, low, high = value * there.astype(BF16), low * there, high * there
        dest[row, 1 : strip + 1] = value
        dest[row, 0] = pltpu.roll(high, 1, 0).astype(BF16)
        dest[row, strip + 1] = pltpu.roll(low, STRIPS - 1, 0).astype(BF16)


def strips_of(source, row, strip):
    return jnp.concatenate(
        [source[row, pl.ds(j, STRIPS, stride=strip), :] for j in range(strip)], axis=0
    )


def fill_sides(sides, held, pieces, spread, rows):
    breadth = held.shape[1] - 2 * SIDE
    col_even = lax.rem(lax.axis_index("col"), 2) == 0
    for side in range(2):
        right = col_even if side == 0 else jnp.logical_not(col_even)
        spot = pl.ds(pl.multiple_of(jnp.where(right, SIDE + breadth, 0), SIDE), SIDE)
        for row in range(rows):
            if side < sides:
                held[row, spot] = spread(pieces[side], row, right)
            else:
                held[row, spot] = jnp.zeros((SIDE, held.shape[2]), F32)


def nearest(pieces, number, height, row, right):
    _, at_low, step = piece_counts(height)
    at = EDGE * row
    piece = pieces[at_low + number * step + at // SIDE].astype(F32)
    piece = piece[at % SIDE : at % SIDE + EDGE]
    blank = jnp.zeros((SIDE - EDGE, piece.shape[1]), F32)
    return jnp.where(
        right,
        jnp.concatenate([piece, blank], axis=0),
        jnp.concatenate([blank, piece], axis=0),
    )


def pack_rows(sides, latent, turned, close, away, *rest):
    pieces, rest = rest[:sides], rest[sides:]
    own, lines, near, far, spots, inside, held, turn = rest
    height, breadth, size = latent.shape
    strip = own.shape[1] - 2
    for row in range(height):
        held[row, SIDE : SIDE + breadth] = latent[pick_row(row, height)]
    fill_sides(
        sides,
        held,
        pieces,
        lambda piece, row, right: piece[row].astype(F32),
        height,
    )
    turn[0, SIDE : SIDE + breadth] = turned[...].astype(F32)
    fill_sides(sides, turn, pieces, lambda piece, row, right: piece[height].astype(F32), 1)
    spots[...] = strips_of(turn, 0, strip).astype(BF16).reshape(strip, STRIPS, size)
    ends = jnp.concatenate([turn[0, :SIDE], turn[0, SIDE + breadth :]], axis=0).astype(BF16)
    near[EDGE * strip] = close[...]
    far[EDGE * strip] = away[...]
    near[EDGE * strip + 1] = ends
    far[EDGE * strip + 1] = ends
    for row in range(height):
        line = strips_of(held, row, strip)
        lines[row] = line
        put(own, row, line, strip)
        short = line.astype(BF16).reshape(strip, STRIPS, size)
        if row < EDGE:
            far[(EDGE - 1 - row) * strip : (EDGE - row) * strip] = short
        if row >= height - EDGE:
            near[(height - 1 - row) * strip : (height - row) * strip] = short
    col = lax.axis_index("col")
    base = col * breadth - SIDE
    total = lax.axis_size("col") * breadth
    for j in range(strip):
        at = lax.broadcasted_iota(jnp.int32, (STRIPS, size), 0) * strip + (j + base)
        inside[j * STRIPS : (j + 1) * STRIPS] = ((at >= 0) & (at < total)).astype(F32)


def aim_rows(aims, known, spots):
    size = aims.shape[2] // 2
    lane_in = lax.broadcasted_iota(jnp.int32, (size, 2 * size), 0)
    lane_out = lax.broadcasted_iota(jnp.int32, (size, 2 * size), 1)
    color = lax.rem(lane_out, 3)
    aimed = (lane_out < 6) & ((lane_in == color) | (lane_in == color + 3))
    masked = (lane_out >= size) & (lane_out < size + 6) & (lane_in == 6)
    chosen = (aimed | masked).astype(F32).astype(BF16)

    def aim(row, spot, source):
        spot = spot() if callable(spot) else spot
        value = pltpu.roll(spot, lax.rem(size - PLANES * source, size), 1)
        both = jnp.dot(value.astype(BF16), chosen, preferred_element_type=F32)
        lanes = slice(row % 2 * size, (row % 2 + 1) * size)
        aims[row // 2, :, lanes] = both[:, :size]
        known[row // 2, :, lanes] = both[:, size:]

    return [functools.partial(aim, row, *spot) for row, spot in enumerate(spots)]


def conv_pairs(rows, firsts, weights, strip, count):
    taps = []
    for down in range(4):
        for across in range(3):
            parts = []
            for first in firsts:
                source, at = rows[first - 1 + down]
                parts.append(source[at, across : across + strip].reshape(strip * STRIPS, -1))
            taps.append(jnp.concatenate(parts, axis=0) if len(parts) > 1 else parts[0])
    size = weights.shape[0] // count
    parts = [
        jnp.dot(
            jnp.concatenate(taps[len(taps) // count * part : len(taps) // count * (part + 1)], axis=1),
            weights[size * part : size * (part + 1)],
            preferred_element_type=F32,
        )
        for part in range(count)
    ]
    total = parts[0]
    for part in parts[1:]:
        total = total + part
    pixels = strip * STRIPS
    return [total[at * pixels : (at + 1) * pixels] for at in range(len(firsts))]


def gradient(order, rows, weights, aims, known, inside, emit, beside=(), parts=False, cuts=1):
    wide, hidden, slope, grad_two, grad_one = rows
    ahead_one, ahead_two, back_one, back_two, colors, spread, bias = weights
    pixels, size = inside.shape
    strip = pixels // STRIPS
    there = far_there()
    low = min(min(firsts) for stage, firsts in filter(None, order) if stage == 1)

    def keep_of(row):
        return (inside[...] * there if row < EDGE else inside[...]).astype(BF16)

    def half_of(both, half):
        return both[:, half * size : (half + 1) * size]

    def gate(both, number):
        value = both + bias[number, :1]
        twice = jnp.tanh(value) + 1.0
        hid = value * twice
        return hid, twice + hid * (2.0 - twice)

    def ahead_first(firsts):
        results = conv_pairs(wide, firsts, ahead_one, strip, cuts)
        yield
        for first, both in zip(firsts, results):
            hid, twice = gate(both, 0)
            for half in range(2):
                row = first + half
                put(*hidden[row], half_of(hid, half), strip, keep_of(row))
                if row in slope:
                    held, at = slope[row]
                    held[at] = half_of(twice, half)

    lane = lax.rem(lax.broadcasted_iota(jnp.int32, (pixels, 2 * size), 1), size)

    def ahead_second(firsts):
        results = conv_pairs(hidden, firsts, ahead_two, strip, cuts)
        yield
        for first, both in zip(firsts, results):
            number = (first - low) // 2
            hid, twice = gate(both, 1)
            color = lax.dot_general(
                hid.astype(BF16), colors[...], (((1,), (1,)), ((), ())), preferred_element_type=F32
            )
            if parts:
                yield
            residual = known[number] * color - aims[number]
            rest = residual - residual.astype(BF16).astype(F32)
            split = jnp.where(lane < 3, residual, rest).astype(BF16)
            back = jnp.dot(split, spread[...], preferred_element_type=F32)
            if parts:
                yield
            result = back * twice
            for half in range(2):
                put(*grad_two[first + half], half_of(result, half), strip)

    def back_second(firsts):
        results = conv_pairs(grad_two, firsts, back_two, strip, cuts)
        yield
        for first, both in zip(firsts, results):
            for half in range(2):
                row = first + half
                held, at = slope[row]
                put(*grad_one[row], half_of(both, half) * held[at], strip, keep_of(row))

    def back_first(firsts):
        results = conv_pairs(grad_one, firsts, back_one, strip, cuts)
        yield
        for first, both in zip(firsts, results):
            for half in range(2):
                emit(first + half - EDGE, half_of(both, half))

    stages = (ahead_first, ahead_second, back_second, back_first)
    beside = list(beside)
    active = []
    slots = list(order)
    while slots or active:
        started = None
        if slots:
            item = slots.pop(0)
            if item is not None:
                started = stages[item[0]](item[1])
                next(started)
        if beside:
            beside.pop(0)()
        active = [task for task in active if next(task, active) is None]
        if started is not None:
            active.append(started)


def adam(current, first, second, grad):
    first = BETA_ONE * first + (1.0 - BETA_ONE) * grad
    second = BETA_TWO * second + ((1.0 - BETA_TWO) * grad) * grad
    root = second * lax.rsqrt(second)
    return current - (LEARN_RATE * first) / (root + EPSILON), first, second


def floored(second):
    return jnp.maximum(second, 1e-30)


def place_rows(*parts):
    rows = {}
    for first, last, held, at in parts:
        for row in range(first, last):
            rows[row] = (held, at + row - first)
    return rows


def first_near_order(height):
    return [(0, (5, 7)), (0, (9, 11)), (0, (13,)), (1, (6, 8)), (1, (10, 12)), None, (2, (7, 9)), (2, (11,)), (3, (8,)), (3, (10,))]


def last_near_order(height):
    return [(0, (5, 7, 9)), (0, (11, 13)), (1, (6,)), (1, (8,)), (1, (10,)), (1, (12,)), (2, (7,)), (2, (9,)), (2, (11,)), (3, (8,)), (3, (10,))]


def first_far_order(height):
    return [(0, (3,)), (0, (1,)), (1, (4,)), (1, (2,)), (2, (5,)), (2, (3,)), (3, (6,)), (3, (4,))]


def last_far_order(height):
    return [(0, (3,)), (0, (1,)), (1, (4,)), (1, (2,)), (2, (5,)), (2, (3,)), (3, (6,)), (3, (4,))]


def near_rows(height, own, halo, passed, scratch):
    hidden, slope, grad_two, grad_one = scratch
    hidden_out, slope_out, two_out, one_out = passed
    return (
        {**own, **place_rows((height + 4, height + 8, halo, 0))},
        place_rows((5, 7, hidden_out, 0), (7, height + 7, hidden, 0)),
        place_rows((5, 7, slope_out, 0), (7, height + 5, slope, 0)),
        place_rows((6, 8, two_out, 0), (8, height + 6, grad_two, 0)),
        place_rows((7, 9, one_out, 0), (9, height + 5, grad_one, 0)),
    )


def far_rows(own, halo, passed, scratch):
    hidden, slope, grad_two, grad_one = scratch
    hidden_in, slope_in, two_in, one_in = passed
    return (
        {**own, **place_rows((0, 4, halo, 0))},
        place_rows((1, 5, hidden, 0), (5, 7, hidden_in, 0)),
        place_rows((3, 5, slope, 0), (5, 7, slope_in, 0)),
        place_rows((2, 6, grad_two, 0), (6, 8, two_in, 0)),
        place_rows((3, 7, grad_one, 0), (7, 9, one_in, 0)),
    )


def once(make):
    made = []

    def get():
        if not made:
            made.append(make())
        return made[0]

    return get


def pair_up(tasks):
    def both(one, two):
        one()
        two()

    return [functools.partial(both, *tasks[at : at + 2]) for at in range(0, len(tasks), 2)]


def spread_spot(sent, turn, strip, first):
    breadth = turn.shape[1] - 2 * SIDE
    size = turn.shape[2]
    middle = sent[EDGE * strip].astype(F32)
    rest = jnp.zeros((size - STRIPS, breadth), F32)
    turn[0, SIDE : SIDE + breadth] = jnp.concatenate([middle, rest], axis=0).T
    ends = pltpu.roll(sent[EDGE * strip + 1].astype(F32), lax.rem(size - PLANES * first, size), 1)
    turn[0, :SIDE] = ends[:SIDE]
    turn[0, SIDE + breadth :] = ends[SIDE:]
    return strips_of(turn, 0, strip)


def flat_spot(spots):
    return spots[...].reshape(-1, spots.shape[-1]).astype(F32)


def first_near(sides, own, lines, moment_one, moment_two, near, spots, inside, *refs):
    pieces, refs = refs[:sides], refs[sides:]
    weights, refs = refs[:7], refs[7:]
    passed, refs = refs[:4], refs[4:]
    (new, near_out, z_out, m_out, v_out, m_rest, v_rest, aims, known), refs = refs[:9], refs[9:]
    halo, turn, m_held, v_held, *scratch = refs
    height, breadth = moment_one.shape[:2]
    strip = own.shape[1] - 2
    widen(halo, near, strip)
    start = jnp.where(lax.rem(row_place(), 2) == 1, height - 2, 0)
    mine, theirs = flat_spot(spots), once(lambda: spread_spot(near, turn, strip, start))
    tasks = aim_rows(
        aims,
        known,
        [(mine, pick_row(row, height)) for row in range(2, height)]
        + [(theirs, pick_partner_row(row, height) - start) for row in (height - 1, height - 2)],
    )
    for number, (held, moment) in enumerate(((m_held, moment_one), (v_held, moment_two))):
        for row in range(height):
            held[row, SIDE : SIDE + breadth] = moment[pick_row(row, height)]
        fill_sides(
            sides,
            held,
            pieces,
            lambda piece, row, right: nearest(piece, number, height, row, right),
            height,
        )
    for row in range(EDGE):
        m_rest[row] = strips_of(m_held, row, strip)
        v_rest[row] = floored(strips_of(v_held, row, strip))

    def emit(row, grad):
        current, first, second = adam(
            lines[row], strips_of(m_held, row, strip), floored(strips_of(v_held, row, strip)), grad
        )
        current = current * inside[...]
        at = row - EDGE
        z_out[at] = current
        m_out[at] = first
        v_out[at] = second
        put(new, at, current, strip)
        if row >= height - EDGE:
            short = current.astype(BF16).reshape(strip, *near_out.shape[1:])
            near_out[(height - 1 - row) * strip : (height - row) * strip] = short

    rows = near_rows(height, place_rows((4, height + 4, own, 0)), halo, passed, scratch)
    gradient(first_near_order(height), rows, weights, aims, known, inside, emit, pair_up(tasks), False, 2)


def first_far(own, lines, m_rest, v_rest, far, spots, inside, *refs):
    passed, refs = refs[:4], refs[4:]
    weights, refs = refs[:7], refs[7:]
    (new, far_out, z_out, m_out, v_out, aims, known), refs = refs[:7], refs[7:]
    halo, turn, *scratch = refs
    height = own.shape[0]
    strip = own.shape[1] - 2
    widen(halo, far, strip, far_there())
    start = jnp.where(lax.rem(row_place(), 2) == 1, 0, height - 2)
    mine = flat_spot(spots)
    theirs = once(lambda: spread_spot(far, turn, strip, start) * far_there())
    tasks = aim_rows(
        aims,
        known,
        [(theirs, pick_partner_row(row, height) - start) for row in (1, 0)]
        + [(mine, pick_row(row, height)) for row in range(2)],
    )

    def emit(row, grad):
        current, first, second = adam(lines[row], m_rest[row], v_rest[row], grad)
        current = current * inside[...]
        z_out[row] = current
        m_out[row] = first
        v_out[row] = second
        put(new, row, current, strip)
        short = current.astype(BF16).reshape(strip, *far_out.shape[1:])
        far_out[(EDGE - 1 - row) * strip : (EDGE - row) * strip] = short

    rows = far_rows(place_rows((4, 8, own, 0)), halo, passed, scratch)
    gradient(first_far_order(height), rows, weights, aims, known, inside, emit, pair_up(tasks)[::-1], False, 2)


def keep_row(held, at, value, strip):
    for j in range(strip):
        held[at, pl.ds(j, STRIPS, stride=strip), :] = value[j * STRIPS : (j + 1) * STRIPS]


def last_near(low, high, near, z_in, m_in, v_in, aims, known, inside, *refs):
    weights, refs = refs[:7], refs[7:]
    passed, refs = refs[:4], refs[4:]
    helds, refs = refs[:3], refs[3:]
    halo, *scratch = refs
    height = EDGE + high.shape[0]
    strip = low.shape[1] - 2
    widen(halo, near, strip)

    def emit(row, grad):
        at = row - EDGE
        for held, value in zip(helds, adam(z_in[at], m_in[at], v_in[at], grad)):
            keep_row(held, at, value, strip)

    own = place_rows((4, 8, low, 0), (8, height + 4, high, 0))
    rows = near_rows(height, own, halo, passed, scratch)
    gradient(last_near_order(height), rows, weights, aims, known, inside, emit, (), False, 2)


def last_far(low, far, z_in, m_in, v_in, aims, known, inside, *refs):
    passed, refs = refs[:4], refs[4:]
    weights, refs = refs[:7], refs[7:]
    ready, outs, helds, refs = refs[:3], refs[3:6], refs[6:9], refs[9:]
    halo, *scratch, sem = refs
    height, breadth = outs[0].shape[:2]
    strip = low.shape[1] - 2
    copies = []

    def send(row, number, held, at):
        copy = pltpu.make_async_copy(
            held.at[at, pl.ds(SIDE, breadth)],
            outs[number].at[pick_row(row, height)],
            sem.at[number, row],
        )
        copy.start()
        copies.append(copy)

    for row in range(EDGE, height):
        for number in range(3):
            send(row, number, ready[number], row - EDGE)
    widen(halo, far, strip, far_there())

    def emit(row, grad):
        for number, value in enumerate(adam(z_in[row], m_in[row], v_in[row], grad)):
            keep_row(helds[number], row, value, strip)
            send(row, number, helds[number], row)

    rows = far_rows(place_rows((4, 8, low, 0)), halo, passed, scratch)
    gradient(last_far_order(height), rows, weights, aims, known, inside, emit, (), False, 2)
    for copy in copies:
        copy.wait()


def body(
    latent,
    moment_one,
    moment_two,
    hole_mask,
    target_rgb,
    kernel_one,
    bias_one,
    kernel_two,
    bias_two,
    rgb_weight,
):
    height, breadth, size = latent.shape
    strip = (breadth + 2 * SIDE) // STRIPS
    assert strip * STRIPS == breadth + 2 * SIDE and height % 2 == 0 and height >= 8
    assert height * PLANES <= size and breadth == size and lax.axis_size("cores") == 2
    pixels = strip * STRIPS
    sides = 1 if lax.axis_size("col") == 2 else 2
    dma = pltpu.SemaphoreType.DMA
    _, at_low, step = piece_counts(height)
    block = (at_low + 2 * step, SIDE, size)
    tall = lambda rows: shape((rows, strip + 2, STRIPS, size), BF16)
    short = lambda tiles: shape((EDGE * strip + tiles, STRIPS, size), BF16)
    lines_of = lambda rows: shape((rows, pixels, size), F32)
    aims_of = lambda rows: shape((rows // 2, pixels, 2 * size), F32)
    vmem = lambda like: pltpu.VMEM(like.shape, like.dtype)
    work = 2 * 12 * 2 * pixels * size * size

    given = tuple(map(in_hbm, (latent, moment_one, moment_two)))
    *columns, turned, close, away = call(
        functools.partial(pack_columns, sides),
        [shape(block, BF16)] * sides
        + [shape((breadth, size), BF16)]
        + [shape((STRIPS, breadth), BF16)] * 2,
        [HBM] * 5,
        [VMEM] * (sides + 3),
        [
            pltpu.VMEM((3, sides, height, SIDE, size), F32),
            pltpu.VMEM(target_rgb.shape, F32),
            pltpu.VMEM(hole_mask.shape, jnp.int32),
            pltpu.VMEM((size, breadth), F32),
            pltpu.VMEM(block, F32),
            dma((4, 2)),
        ],
        (10**6, 10**6),
        "pack_columns",
    )(*given, in_hbm(target_rgb), in_hbm(hole_mask))
    columns = [swap(piece, "col", side) for side, piece in enumerate(columns)]

    matrix = shape((12 * size, 2 * size), BF16)
    *weights, latent = call(
        pack_weights,
        [matrix] * 4 + [shape((2 * size, 2 * size), BF16)] * 2 + [shape((2, 8, 2 * size), F32)]
        + [shape(latent.shape, F32)],
        [VMEM] * 2 + [HBM] * 4,
        [VMEM] * 8,
        [
            pltpu.VMEM((2 * size, 2 * size), F32),
            pltpu.VMEM(rgb_weight.shape, BF16),
            pltpu.VMEM((1, size), F32),
            pltpu.VMEM((1, size), F32),
            dma((4,)),
        ],
        (10**6, 4 * 10**6),
        "pack_weights",
    )(
        kernel_one,
        kernel_two,
        *map(in_hbm, (rgb_weight, bias_one[None], bias_two[None])),
        given[0],
    )

    columns, weights = lax.optimization_barrier((columns, weights))
    own, lines, near, far, spots, inside = call(
        functools.partial(pack_rows, sides),
        [tall(height), lines_of(height), short(2), short(2)]
        + [shape((strip, STRIPS, size), BF16), shape((pixels, size), F32)],
        [VMEM] * (4 + sides),
        [VMEM] * 6,
        [vmem(lines_of(height)), vmem(lines_of(1))],
        (10**6, 4 * 10**6),
        "pack_rows",
    )(latent, turned, close, away, *columns)
    near = swap_near(near)
    far = swap_far(far)

    passed = [tall(2), lines_of(2), tall(2), tall(2)]
    near_scratch = [
        vmem(tall(height)),
        vmem(lines_of(height - 2)),
        vmem(tall(height - 2)),
        vmem(tall(height - 4)),
    ]
    far_scratch = [vmem(tall(4)), vmem(lines_of(2)), vmem(tall(4)), vmem(tall(4))]
    near_work = (2 * (height - 1) + 0) * work, 10**7
    far_work = 8 * work, 10**7
    rest, some = height - EDGE, EDGE

    *results, near_next, z_high, m_high, v_high, m_rest, v_rest, aims_near, known_near = call(
        functools.partial(first_near, sides),
        passed
        + [tall(rest), short(0), lines_of(rest), lines_of(rest), lines_of(rest)]
        + [lines_of(some), lines_of(some), aims_of(height), aims_of(height)],
        [VMEM] * (7 + sides + 7),
        [VMEM] * 13,
        [vmem(tall(EDGE)), vmem(lines_of(1)), vmem(lines_of(height)), vmem(lines_of(height))]
        + near_scratch,
        near_work,
        "first_near",
    )(own, lines, moment_one, moment_two, near, spots, inside, *columns, *weights)
    *handed, high = results
    near_next = swap_near(near_next)

    low, far_next, z_low, m_low, v_low, aims_far, known_far = call(
        first_far,
        [tall(some), short(0), lines_of(some), lines_of(some), lines_of(some)]
        + [aims_of(4), aims_of(4)],
        [VMEM] * (7 + 4 + 7),
        [VMEM] * 7,
        [vmem(tall(EDGE)), vmem(lines_of(1))] + far_scratch,
        far_work,
        "first_far",
    )(own, lines, m_rest, v_rest, far, spots, inside, *handed, *weights)
    far_next = swap_far(far_next)

    out = shape(latent.shape, F32)
    results = call(
        last_near,
        passed + [lines_of(rest)] * 3,
        [VMEM] * (9 + 7),
        [VMEM] * 7,
        [vmem(tall(EDGE))] + near_scratch,
        near_work,
        "last_near",
    )(low, high, near_next, z_high, m_high, v_high, aims_near, known_near, inside, *weights)
    handed, ready = results[:4], results[4:]
    return call(
        last_far,
        [out] * 3,
        [VMEM] * (8 + 4 + 7 + 3),
        [HBM] * 3,
        [vmem(lines_of(some))] * 3 + [vmem(tall(EDGE))] + far_scratch + [dma((3, height))],
        far_work,
        "last_far",
    )(low, far_next, z_low, m_low, v_low, aims_far, known_far, inside, *handed, *weights, *ready)


def solution(mesh):
    tile = P(("parts", "row", "cores"), "col", None)
    return jax.shard_map(
        body,
        mesh=mesh,
        in_specs=(
            tile,
            tile,
            tile,
            P(("parts", "row", "cores"), "col"),
            P(None, ("parts", "row", "cores"), "col"),
            P(),
            P(),
            P(),
            P(),
            P(),
        ),
        out_specs=(tile, tile, tile),
        check_vma=False,
    )
```

```python
import functools
import math

import jax
import jax.numpy as jnp
from jax import lax
from jax.experimental import pallas as pl
from jax.experimental.pallas import tpu as pltpu
from jax.sharding import PartitionSpec as P

STEPS = 2

BETA_ONE = 0.6
BETA_TWO = 0.9
LEARN_RATE = 0.4
EPSILON = 1e-08

ROWS = ("row", "cores")
STRIPS = 16
SIDE = 8
EDGE = 4
PLANES = 7
VMEM = pl.BlockSpec(memory_space=pltpu.VMEM)
HBM = pl.BlockSpec(memory_space=pltpu.HBM)
F32 = jnp.float32
BF16 = jnp.bfloat16


def row_place():
    cores = lax.axis_size("cores")
    return lax.axis_index("row") * cores + lax.axis_index("cores")


def pairs(count, parity):
    chosen = []
    for low in range(parity, count - 1, 2):
        chosen += [(low, low + 1), (low + 1, low)]
    return chosen


def swap(block, axes, parity):
    return lax.ppermute(block, axes, pairs(lax.axis_size(axes), parity))


def swap_near(block):
    return swap(block, ROWS, 0)


def swap_far(block):
    rows, cols, cores = (lax.axis_size(name) for name in ("row", "col", "cores"))
    count = rows * cores

    def index(place, col):
        return (place // cores * cols + col) * cores + place % cores

    chosen = []
    for col in range(cols):
        chosen += [(index(a, col), index(b, col)) for a, b in pairs(count, 1)]
    for place in (0, count - 1):
        chosen += [(index(place, a), index(place, b)) for a, b in pairs(cols, 0)]
    return lax.ppermute(block, ("row", "col", "cores"), sorted(chosen))


def far_there():
    place, count = row_place(), lax.axis_size("row") * lax.axis_size("cores")
    odd = lax.rem(place, 2) == 1
    return jnp.where(odd, place < count - 1, place > 0).astype(F32)


def call(kernel, out_shape, in_specs, out_specs, scratch, cost, name, aliases=None, limit=24 << 20):
    return pl.pallas_call(
        kernel,
        out_shape=out_shape,
        in_specs=in_specs,
        out_specs=out_specs,
        scratch_shapes=scratch,
        compiler_params=pltpu.CompilerParams(vmem_limit_bytes=limit),
        cost_estimate=pl.CostEstimate(flops=cost[0], bytes_accessed=cost[1], transcendentals=0),
        input_output_aliases=aliases or {},
        name=name,
    )


def in_hbm(array):
    return pltpu.with_memory_space_constraint(array, pltpu.HBM)


def shape(dims, dtype):
    return jax.ShapeDtypeStruct(dims, dtype)


def pick_row(index, height):
    odd = lax.rem(row_place(), 2) == 1
    return jnp.where(odd, height - 1 - index, index)


def pick_partner_row(index, height):
    odd = lax.rem(row_place(), 2) == 1
    return jnp.where(odd, index, height - 1 - index)


def piece_counts(height):
    return height, height + 2, height * EDGE // SIDE


def pack_columns(sides, latent, first, second, target, mask, *rest):
    outs, rest = rest[:sides], rest[sides:]
    turned, close, away, ends, aim, known, planes, flat, sem = rest
    height, breadth = latent.shape[0], latent.shape[1]
    col_even = lax.rem(lax.axis_index("col"), 2) == 0
    rights = (col_even, jnp.logical_not(col_even))[:sides]
    early = [
        pltpu.make_async_copy(target, aim, sem.at[3, 0]),
        pltpu.make_async_copy(mask, known, sem.at[3, 1]),
    ]
    copies = [
        pltpu.make_async_copy(
            source.at[:, pl.ds(pl.multiple_of(jnp.where(right, breadth - SIDE, 0), SIDE), SIDE)],
            ends.at[number, side],
            sem.at[number, side],
        )
        for number, source in enumerate((latent, first, second))
        for side, right in enumerate(rights)
    ]
    for copy in early + copies:
        copy.start()
    planes[...] = jnp.zeros_like(planes)
    for copy in early:
        copy.wait()
    keep = known[...].astype(F32)
    for color in range(3):
        wanted = keep * aim[color]
        high = wanted.astype(BF16).astype(F32)
        planes[pl.ds(color, height, stride=PLANES), :] = high
        planes[pl.ds(color + 3, height, stride=PLANES), :] = wanted - high
    planes[pl.ds(6, height, stride=PLANES), :] = keep
    swapped = planes[...].T
    turned[...] = swapped.astype(BF16)
    odd = lax.rem(row_place(), 2) == 1
    start = (height - 2) * PLANES
    low, high = planes[:STRIPS], planes[start : start + STRIPS]
    close[...] = jnp.where(odd, low, high).astype(BF16)
    away[...] = jnp.where(odd, high, low).astype(BF16)
    for copy in copies:
        copy.wait()
    _, at_low, step = piece_counts(height)
    for side, (out, right) in enumerate(zip(outs, rights)):
        flat[height] = jnp.where(right, swapped[breadth - SIDE :], swapped[:SIDE])
        flat[height + 1] = jnp.zeros(flat.shape[1:], F32)
        for row in range(height):
            source = pick_row(row, height)
            own = [ends[n, side, source] for n in range(3)]
            flat[row] = own[0]
            for number, piece in enumerate(own[1:]):
                near = jnp.where(right, piece[SIDE - EDGE :], piece[:EDGE])
                at = EDGE * row
                flat[at_low + number * step + at // SIDE, at % SIDE : at % SIDE + EDGE] = near
        out[...] = flat[...].astype(BF16)


def pack_weights(one, two, rgb, bias_one, bias_two, *refs):
    given, refs = refs[:1], refs[1:]
    matrices, loaded, refs = refs[:7], refs[7 : 7 + 1], refs[7 + 1 :]
    ahead_one, ahead_two, back_one, back_two, colors, spread, bias = matrices
    held, *small, sem = refs
    copies = [
        pltpu.make_async_copy(source, dest, sem.at[number])
        for number, (source, dest) in enumerate(
            zip((rgb, bias_one, bias_two, *given), (*small, *loaded))
        )
    ]
    rgb, bias_one, bias_two = small
    for copy in copies:
        copy.start()
    size = one.shape[2]
    half = jnp.asarray(0.5, BF16)
    odd = lax.rem(row_place(), 2) == 1
    for kernel, ahead, back in ((one, ahead_one, back_one), (two, ahead_two, back_two)):
        for row in range(4):
            for col in range(3):
                at = (row * 3 + col) * size
                for out in range(2):
                    tap = row - out
                    if 0 <= tap <= 2:
                        front = kernel[jnp.where(odd, 2 - tap, tap), col] * half
                        rear = kernel[jnp.where(odd, tap, 2 - tap), 2 - col]
                        rear = rear.astype(F32).T.astype(BF16)
                        if kernel is two:
                            rear = rear * half
                    else:
                        front = rear = jnp.zeros((size, size), BF16)
                    ahead[at : at + size, out * size : (out + 1) * size] = front
                    back[at : at + size, out * size : (out + 1) * size] = rear
    held[...] = jnp.zeros_like(held)
    for copy in copies[:3]:
        copy.wait()
    for at in (0, size):
        held[at : at + 3, at : at + size] = rgb[...].astype(F32)
        held[at + 3 : at + 6, at : at + size] = rgb[...].astype(F32)
    colors[...] = held[...].astype(BF16)
    spread[...] = (0.5 * held[...]).astype(BF16)
    for number, given in enumerate((bias_one, bias_two)):
        for at in (0, size):
            bias[number, :, at : at + size] = jnp.broadcast_to(0.5 * given[...], (8, size))
    for copy in copies[3:]:
        copy.wait()


def put(dest, row, value, strip, keep=None):
    low, high = value[:STRIPS], value[(strip - 1) * STRIPS :]
    value = value.astype(BF16)
    if keep is not None:
        value = value * keep
        low = low * keep[:STRIPS].astype(F32)
        high = high * keep[(strip - 1) * STRIPS :].astype(F32)
    dest[row, 1 : strip + 1] = value.reshape(strip, STRIPS, -1)
    dest[row, 0] = pltpu.roll(high, 1, 0).astype(BF16)
    dest[row, strip + 1] = pltpu.roll(low, STRIPS - 1, 0).astype(BF16)


def widen(dest, source, strip, there=None):
    for row in range(EDGE):
        at = row * strip
        value = source[at : at + strip]
        low, high = source[at].astype(F32), source[at + strip - 1].astype(F32)
        if there is not None:
            value, low, high = value * there.astype(BF16), low * there, high * there
        dest[row, 1 : strip + 1] = value
        dest[row, 0] = pltpu.roll(high, 1, 0).astype(BF16)
        dest[row, strip + 1] = pltpu.roll(low, STRIPS - 1, 0).astype(BF16)


def strips_of(source, row, strip):
    return jnp.concatenate(
        [source[row, pl.ds(j, STRIPS, stride=strip), :] for j in range(strip)], axis=0
    )


def fill_sides(sides, held, pieces, spread, rows):
    breadth = held.shape[1] - 2 * SIDE
    col_even = lax.rem(lax.axis_index("col"), 2) == 0
    for side in range(2):
        right = col_even if side == 0 else jnp.logical_not(col_even)
        spot = pl.ds(pl.multiple_of(jnp.where(right, SIDE + breadth, 0), SIDE), SIDE)
        for row in range(rows):
            if side < sides:
                held[row, spot] = spread(pieces[side], row, right)
            else:
                held[row, spot] = jnp.zeros((SIDE, held.shape[2]), F32)


def nearest(pieces, number, height, row, right):
    _, at_low, step = piece_counts(height)
    at = EDGE * row
    piece = pieces[at_low + number * step + at // SIDE].astype(F32)
    piece = piece[at % SIDE : at % SIDE + EDGE]
    blank = jnp.zeros((SIDE - EDGE, piece.shape[1]), F32)
    return jnp.where(
        right,
        jnp.concatenate([piece, blank], axis=0),
        jnp.concatenate([blank, piece], axis=0),
    )


def pack_rows(sides, latent, turned, close, away, *rest):
    pieces, rest = rest[:sides], rest[sides:]
    own, lines, near, far, spots, inside, held, turn = rest
    height, breadth, size = latent.shape
    strip = own.shape[1] - 2
    for row in range(height):
        held[row, SIDE : SIDE + breadth] = latent[pick_row(row, height)]
    fill_sides(
        sides,
        held,
        pieces,
        lambda piece, row, right: piece[row].astype(F32),
        height,
    )
    turn[0, SIDE : SIDE + breadth] = turned[...].astype(F32)
    fill_sides(sides, turn, pieces, lambda piece, row, right: piece[height].astype(F32), 1)
    spots[...] = strips_of(turn, 0, strip).astype(BF16).reshape(strip, STRIPS, size)
    ends = jnp.concatenate([turn[0, :SIDE], turn[0, SIDE + breadth :]], axis=0).astype(BF16)
    near[EDGE * strip] = close[...]
    far[EDGE * strip] = away[...]
    near[EDGE * strip + 1] = ends
    far[EDGE * strip + 1] = ends
    for row in range(height):
        line = strips_of(held, row, strip)
        lines[row] = line
        put(own, row, line, strip)
        short = line.astype(BF16).reshape(strip, STRIPS, size)
        if row < EDGE:
            far[(EDGE - 1 - row) * strip : (EDGE - row) * strip] = short
        if row >= height - EDGE:
            near[(height - 1 - row) * strip : (height - row) * strip] = short
    col = lax.axis_index("col")
    base = col * breadth - SIDE
    total = lax.axis_size("col") * breadth
    for j in range(strip):
        at = lax.broadcasted_iota(jnp.int32, (STRIPS, size), 0) * strip + (j + base)
        inside[j * STRIPS : (j + 1) * STRIPS] = ((at >= 0) & (at < total)).astype(F32)


def aim_rows(aims, known, spots):
    size = aims.shape[2] // 2
    lane_in = lax.broadcasted_iota(jnp.int32, (size, 2 * size), 0)
    lane_out = lax.broadcasted_iota(jnp.int32, (size, 2 * size), 1)
    color = lax.rem(lane_out, 3)
    aimed = (lane_out < 6) & ((lane_in == color) | (lane_in == color + 3))
    masked = (lane_out >= size) & (lane_out < size + 6) & (lane_in == 6)
    chosen = (aimed | masked).astype(F32).astype(BF16)

    def aim(row, spot, source):
        spot = spot() if callable(spot) else spot
        value = pltpu.roll(spot, lax.rem(size - PLANES * source, size), 1)
        both = jnp.dot(value.astype(BF16), chosen, preferred_element_type=F32)
        lanes = slice(row % 2 * size, (row % 2 + 1) * size)
        aims[row // 2, :, lanes] = both[:, :size]
        known[row // 2, :, lanes] = both[:, size:]

    return [functools.partial(aim, row, *spot) for row, spot in enumerate(spots)]


def conv_pairs(rows, firsts, weights, strip, count):
    taps = []
    for down in range(4):
        for across in range(3):
            parts = []
            for first in firsts:
                source, at = rows[first - 1 + down]
                parts.append(source[at, across : across + strip].reshape(strip * STRIPS, -1))
            taps.append(jnp.concatenate(parts, axis=0) if len(parts) > 1 else parts[0])
    size = weights.shape[0] // count
    parts = [
        jnp.dot(
            jnp.concatenate(taps[len(taps) // count * part : len(taps) // count * (part + 1)], axis=1),
            weights[size * part : size * (part + 1)],
            preferred_element_type=F32,
        )
        for part in range(count)
    ]
    total = parts[0]
    for part in parts[1:]:
        total = total + part
    pixels = strip * STRIPS
    return [total[at * pixels : (at + 1) * pixels] for at in range(len(firsts))]


def gradient(order, rows, weights, aims, known, inside, emit, beside=(), parts=False, cuts=1):
    wide, hidden, slope, grad_two, grad_one = rows
    ahead_one, ahead_two, back_one, back_two, colors, spread, bias = weights
    pixels, size = inside.shape
    strip = pixels // STRIPS
    there = far_there()
    low = min(min(firsts) for stage, firsts in filter(None, order) if stage == 1)

    def keep_of(row):
        return (inside[...] * there if row < EDGE else inside[...]).astype(BF16)

    def half_of(both, half):
        return both[:, half * size : (half + 1) * size]

    def gate(both, number):
        value = both + bias[number, :1]
        twice = jnp.tanh(value) + 1.0
        hid = value * twice
        return hid, twice + hid * (2.0 - twice)

    def ahead_first(firsts):
        results = conv_pairs(wide, firsts, ahead_one, strip, cuts)
        yield
        for first, both in zip(firsts, results):
            hid, twice = gate(both, 0)
            for half in range(2):
                row = first + half
                put(*hidden[row], half_of(hid, half), strip, keep_of(row))
                if row in slope:
                    held, at = slope[row]
                    held[at] = half_of(twice, half)

    lane = lax.rem(lax.broadcasted_iota(jnp.int32, (pixels, 2 * size), 1), size)

    def ahead_second(firsts):
        results = conv_pairs(hidden, firsts, ahead_two, strip, cuts)
        yield
        for first, both in zip(firsts, results):
            number = (first - low) // 2
            hid, twice = gate(both, 1)
            color = lax.dot_general(
                hid.astype(BF16), colors[...], (((1,), (1,)), ((), ())), preferred_element_type=F32
            )
            if parts:
                yield
            residual = known[number] * color - aims[number]
            rest = residual - residual.astype(BF16).astype(F32)
            split = jnp.where(lane < 3, residual, rest).astype(BF16)
            back = jnp.dot(split, spread[...], preferred_element_type=F32)
            if parts:
                yield
            result = back * twice
            for half in range(2):
                put(*grad_two[first + half], half_of(result, half), strip)

    def back_second(firsts):
        results = conv_pairs(grad_two, firsts, back_two, strip, cuts)
        yield
        for first, both in zip(firsts, results):
            for half in range(2):
                row = first + half
                held, at = slope[row]
                put(*grad_one[row], half_of(both, half) * held[at], strip, keep_of(row))

    def back_first(firsts):
        results = conv_pairs(grad_one, firsts, back_one, strip, cuts)
        yield
        for first, both in zip(firsts, results):
            for half in range(2):
                emit(first + half - EDGE, half_of(both, half))

    stages = (ahead_first, ahead_second, back_second, back_first)
    beside = list(beside)
    active = []
    slots = list(order)
    while slots or active:
        started = None
        if slots:
            item = slots.pop(0)
            if item is not None:
                started = stages[item[0]](item[1])
                next(started)
        if beside:
            beside.pop(0)()
        active = [task for task in active if next(task, active) is None]
        if started is not None:
            active.append(started)


def adam(current, first, second, grad):
    first = BETA_ONE * first + (1.0 - BETA_ONE) * grad
    second = BETA_TWO * second + ((1.0 - BETA_TWO) * grad) * grad
    root = second * lax.rsqrt(second)
    return current - (LEARN_RATE * first) / (root + EPSILON), first, second


def floored(second):
    return jnp.maximum(second, 1e-30)


def place_rows(*parts):
    rows = {}
    for first, last, held, at in parts:
        for row in range(first, last):
            rows[row] = (held, at + row - first)
    return rows


def first_near_order(height):
    return [(0, (5, 7)), (0, (9, 11)), (0, (13,)), (1, (6, 8)), (1, (10, 12)), None, (2, (7, 9)), (2, (11,)), (3, (8,)), (3, (10,))]


def last_near_order(height):
    return [(0, (5, 7, 9)), (0, (11, 13)), (1, (6,)), (1, (8,)), (1, (10,)), (1, (12,)), (2, (7,)), (2, (9,)), (2, (11,)), (3, (8,)), (3, (10,))]


def first_far_order(height):
    return [(0, (3,)), (0, (1,)), (1, (4,)), (1, (2,)), (2, (5,)), (2, (3,)), (3, (6,)), (3, (4,))]


def last_far_order(height):
    return [(0, (3,)), (0, (1,)), (1, (4,)), (1, (2,)), (2, (5,)), (2, (3,)), (3, (6,)), (3, (4,))]


def near_rows(height, own, halo, passed, scratch):
    hidden, slope, grad_two, grad_one = scratch
    hidden_out, slope_out, two_out, one_out = passed
    return (
        {**own, **place_rows((height + 4, height + 8, halo, 0))},
        place_rows((5, 7, hidden_out, 0), (7, height + 7, hidden, 0)),
        place_rows((5, 7, slope_out, 0), (7, height + 5, slope, 0)),
        place_rows((6, 8, two_out, 0), (8, height + 6, grad_two, 0)),
        place_rows((7, 9, one_out, 0), (9, height + 5, grad_one, 0)),
    )


def far_rows(own, halo, passed, scratch):
    hidden, slope, grad_two, grad_one = scratch
    hidden_in, slope_in, two_in, one_in = passed
    return (
        {**own, **place_rows((0, 4, halo, 0))},
        place_rows((1, 5, hidden, 0), (5, 7, hidden_in, 0)),
        place_rows((3, 5, slope, 0), (5, 7, slope_in, 0)),
        place_rows((2, 6, grad_two, 0), (6, 8, two_in, 0)),
        place_rows((3, 7, grad_one, 0), (7, 9, one_in, 0)),
    )


def once(make):
    made = []

    def get():
        if not made:
            made.append(make())
        return made[0]

    return get


def pair_up(tasks):
    def both(one, two):
        one()
        two()

    return [functools.partial(both, *tasks[at : at + 2]) for at in range(0, len(tasks), 2)]


def spread_spot(sent, turn, strip, first):
    breadth = turn.shape[1] - 2 * SIDE
    size = turn.shape[2]
    middle = sent[EDGE * strip].astype(F32)
    rest = jnp.zeros((size - STRIPS, breadth), F32)
    turn[0, SIDE : SIDE + breadth] = jnp.concatenate([middle, rest], axis=0).T
    ends = pltpu.roll(sent[EDGE * strip + 1].astype(F32), lax.rem(size - PLANES * first, size), 1)
    turn[0, :SIDE] = ends[:SIDE]
    turn[0, SIDE + breadth :] = ends[SIDE:]
    return strips_of(turn, 0, strip)


def flat_spot(spots):
    return spots[...].reshape(-1, spots.shape[-1]).astype(F32)


def first_near(sides, own, lines, moment_one, moment_two, near, spots, inside, *refs):
    pieces, refs = refs[:sides], refs[sides:]
    weights, refs = refs[:7], refs[7:]
    passed, refs = refs[:4], refs[4:]
    (new, near_out, z_out, m_out, v_out, m_rest, v_rest, aims, known), refs = refs[:9], refs[9:]
    halo, turn, m_held, v_held, *scratch = refs
    height, breadth = moment_one.shape[:2]
    strip = own.shape[1] - 2
    widen(halo, near, strip)
    start = jnp.where(lax.rem(row_place(), 2) == 1, height - 2, 0)
    mine, theirs = flat_spot(spots), once(lambda: spread_spot(near, turn, strip, start))
    tasks = aim_rows(
        aims,
        known,
        [(mine, pick_row(row, height)) for row in range(2, height)]
        + [(theirs, pick_partner_row(row, height) - start) for row in (height - 1, height - 2)],
    )
    for number, (held, moment) in enumerate(((m_held, moment_one), (v_held, moment_two))):
        for row in range(height):
            held[row, SIDE : SIDE + breadth] = moment[pick_row(row, height)]
        fill_sides(
            sides,
            held,
            pieces,
            lambda piece, row, right: nearest(piece, number, height, row, right),
            height,
        )
    for row in range(EDGE):
        m_rest[row] = strips_of(m_held, row, strip)
        v_rest[row] = floored(strips_of(v_held, row, strip))

    def emit(row, grad):
        current, first, second = adam(
            lines[row], strips_of(m_held, row, strip), floored(strips_of(v_held, row, strip)), grad
        )
        current = current * inside[...]
        at = row - EDGE
        z_out[at] = current
        m_out[at] = first
        v_out[at] = second
        put(new, at, current, strip)
        if row >= height - EDGE:
            short = current.astype(BF16).reshape(strip, *near_out.shape[1:])
            near_out[(height - 1 - row) * strip : (height - row) * strip] = short

    rows = near_rows(height, place_rows((4, height + 4, own, 0)), halo, passed, scratch)
    gradient(first_near_order(height), rows, weights, aims, known, inside, emit, pair_up(tasks), False, 3)


def first_far(own, lines, m_rest, v_rest, far, spots, inside, *refs):
    passed, refs = refs[:4], refs[4:]
    weights, refs = refs[:7], refs[7:]
    (new, far_out, z_out, m_out, v_out, aims, known), refs = refs[:7], refs[7:]
    halo, turn, *scratch = refs
    height = own.shape[0]
    strip = own.shape[1] - 2
    widen(halo, far, strip, far_there())
    start = jnp.where(lax.rem(row_place(), 2) == 1, 0, height - 2)
    mine = flat_spot(spots)
    theirs = once(lambda: spread_spot(far, turn, strip, start) * far_there())
    tasks = aim_rows(
        aims,
        known,
        [(theirs, pick_partner_row(row, height) - start) for row in (1, 0)]
        + [(mine, pick_row(row, height)) for row in range(2)],
    )

    def emit(row, grad):
        current, first, second = adam(lines[row], m_rest[row], v_rest[row], grad)
        current = current * inside[...]
        z_out[row] = current
        m_out[row] = first
        v_out[row] = second
        put(new, row, current, strip)
        short = current.astype(BF16).reshape(strip, *far_out.shape[1:])
        far_out[(EDGE - 1 - row) * strip : (EDGE - row) * strip] = short

    rows = far_rows(place_rows((4, 8, own, 0)), halo, passed, scratch)
    gradient(first_far_order(height), rows, weights, aims, known, inside, emit, pair_up(tasks)[::-1], False, 2)


def keep_row(held, at, value, strip):
    for j in range(strip):
        held[at, pl.ds(j, STRIPS, stride=strip), :] = value[j * STRIPS : (j + 1) * STRIPS]


def last_near(low, high, near, z_in, m_in, v_in, aims, known, inside, *refs):
    weights, refs = refs[:7], refs[7:]
    passed, refs = refs[:4], refs[4:]
    helds, refs = refs[:3], refs[3:]
    halo, *scratch = refs
    height = EDGE + high.shape[0]
    strip = low.shape[1] - 2
    widen(halo, near, strip)

    def emit(row, grad):
        at = row - EDGE
        for held, value in zip(helds, adam(z_in[at], m_in[at], v_in[at], grad)):
            keep_row(held, at, value, strip)

    own = place_rows((4, 8, low, 0), (8, height + 4, high, 0))
    rows = near_rows(height, own, halo, passed, scratch)
    gradient(last_near_order(height), rows, weights, aims, known, inside, emit, (), False, 3)


def last_far(low, far, z_in, m_in, v_in, aims, known, inside, *refs):
    passed, refs = refs[:4], refs[4:]
    weights, refs = refs[:7], refs[7:]
    ready, outs, helds, refs = refs[:3], refs[3:6], refs[6:9], refs[9:]
    halo, *scratch, sem = refs
    height, breadth = outs[0].shape[:2]
    strip = low.shape[1] - 2
    copies = []

    def send(row, number, held, at):
        copy = pltpu.make_async_copy(
            held.at[at, pl.ds(SIDE, breadth)],
            outs[number].at[pick_row(row, height)],
            sem.at[number, row],
        )
        copy.start()
        copies.append(copy)

    for row in range(EDGE, height):
        for number in range(3):
            send(row, number, ready[number], row - EDGE)
    widen(halo, far, strip, far_there())

    def emit(row, grad):
        for number, value in enumerate(adam(z_in[row], m_in[row], v_in[row], grad)):
            keep_row(helds[number], row, value, strip)
            send(row, number, helds[number], row)

    rows = far_rows(place_rows((4, 8, low, 0)), halo, passed, scratch)
    gradient(last_far_order(height), rows, weights, aims, known, inside, emit, (), False, 2)
    for copy in copies:
        copy.wait()


def body(
    latent,
    moment_one,
    moment_two,
    hole_mask,
    target_rgb,
    kernel_one,
    bias_one,
    kernel_two,
    bias_two,
    rgb_weight,
):
    height, breadth, size = latent.shape
    strip = (breadth + 2 * SIDE) // STRIPS
    assert strip * STRIPS == breadth + 2 * SIDE and height % 2 == 0 and height >= 8
    assert height * PLANES <= size and breadth == size and lax.axis_size("cores") == 2
    pixels = strip * STRIPS
    sides = 1 if lax.axis_size("col") == 2 else 2
    dma = pltpu.SemaphoreType.DMA
    _, at_low, step = piece_counts(height)
    block = (at_low + 2 * step, SIDE, size)
    tall = lambda rows: shape((rows, strip + 2, STRIPS, size), BF16)
    short = lambda tiles: shape((EDGE * strip + tiles, STRIPS, size), BF16)
    lines_of = lambda rows: shape((rows, pixels, size), F32)
    aims_of = lambda rows: shape((rows // 2, pixels, 2 * size), F32)
    vmem = lambda like: pltpu.VMEM(like.shape, like.dtype)
    work = 2 * 12 * 2 * pixels * size * size

    given = tuple(map(in_hbm, (latent, moment_one, moment_two)))
    *columns, turned, close, away = call(
        functools.partial(pack_columns, sides),
        [shape(block, BF16)] * sides
        + [shape((breadth, size), BF16)]
        + [shape((STRIPS, breadth), BF16)] * 2,
        [HBM] * 5,
        [VMEM] * (sides + 3),
        [
            pltpu.VMEM((3, sides, height, SIDE, size), F32),
            pltpu.VMEM(target_rgb.shape, F32),
            pltpu.VMEM(hole_mask.shape, jnp.int32),
            pltpu.VMEM((size, breadth), F32),
            pltpu.VMEM(block, F32),
            dma((4, 2)),
        ],
        (10**6, 10**6),
        "pack_columns",
    )(*given, in_hbm(target_rgb), in_hbm(hole_mask))
    columns = [swap(piece, "col", side) for side, piece in enumerate(columns)]

    matrix = shape((12 * size, 2 * size), BF16)
    *weights, latent = call(
        pack_weights,
        [matrix] * 4 + [shape((2 * size, 2 * size), BF16)] * 2 + [shape((2, 8, 2 * size), F32)]
        + [shape(latent.shape, F32)],
        [VMEM] * 2 + [HBM] * 4,
        [VMEM] * 8,
        [
            pltpu.VMEM((2 * size, 2 * size), F32),
            pltpu.VMEM(rgb_weight.shape, BF16),
            pltpu.VMEM((1, size), F32),
            pltpu.VMEM((1, size), F32),
            dma((4,)),
        ],
        (10**6, 4 * 10**6),
        "pack_weights",
    )(
        kernel_one,
        kernel_two,
        *map(in_hbm, (rgb_weight, bias_one[None], bias_two[None])),
        given[0],
    )

    columns, weights = lax.optimization_barrier((columns, weights))
    own, lines, near, far, spots, inside = call(
        functools.partial(pack_rows, sides),
        [tall(height), lines_of(height), short(2), short(2)]
        + [shape((strip, STRIPS, size), BF16), shape((pixels, size), F32)],
        [VMEM] * (4 + sides),
        [VMEM] * 6,
        [vmem(lines_of(height)), vmem(lines_of(1))],
        (10**6, 4 * 10**6),
        "pack_rows",
    )(latent, turned, close, away, *columns)
    near = swap_near(near)
    far = swap_far(far)

    passed = [tall(2), lines_of(2), tall(2), tall(2)]
    near_scratch = [
        vmem(tall(height)),
        vmem(lines_of(height - 2)),
        vmem(tall(height - 2)),
        vmem(tall(height - 4)),
    ]
    far_scratch = [vmem(tall(4)), vmem(lines_of(2)), vmem(tall(4)), vmem(tall(4))]
    near_work = (2 * (height - 1) + 0) * work, 10**7
    far_work = 8 * work, 10**7
    rest, some = height - EDGE, EDGE

    *results, near_next, z_high, m_high, v_high, m_rest, v_rest, aims_near, known_near = call(
        functools.partial(first_near, sides),
        passed
        + [tall(rest), short(0), lines_of(rest), lines_of(rest), lines_of(rest)]
        + [lines_of(some), lines_of(some), aims_of(height), aims_of(height)],
        [VMEM] * (7 + sides + 7),
        [VMEM] * 13,
        [vmem(tall(EDGE)), vmem(lines_of(1)), vmem(lines_of(height)), vmem(lines_of(height))]
        + near_scratch,
        near_work,
        "first_near",
    )(own, lines, moment_one, moment_two, near, spots, inside, *columns, *weights)
    *handed, high = results
    near_next = swap_near(near_next)

    low, far_next, z_low, m_low, v_low, aims_far, known_far = call(
        first_far,
        [tall(some), short(0), lines_of(some), lines_of(some), lines_of(some)]
        + [aims_of(4), aims_of(4)],
        [VMEM] * (7 + 4 + 7),
        [VMEM] * 7,
        [vmem(tall(EDGE)), vmem(lines_of(1))] + far_scratch,
        far_work,
        "first_far",
    )(own, lines, m_rest, v_rest, far, spots, inside, *handed, *weights)
    far_next = swap_far(far_next)

    out = shape(latent.shape, F32)
    results = call(
        last_near,
        passed + [lines_of(rest)] * 3,
        [VMEM] * (9 + 7),
        [VMEM] * 7,
        [vmem(tall(EDGE))] + near_scratch,
        near_work,
        "last_near",
    )(low, high, near_next, z_high, m_high, v_high, aims_near, known_near, inside, *weights)
    handed, ready = results[:4], results[4:]
    return call(
        last_far,
        [out] * 3,
        [VMEM] * (8 + 4 + 7 + 3),
        [HBM] * 3,
        [vmem(lines_of(some))] * 3 + [vmem(tall(EDGE))] + far_scratch + [dma((3, height))],
        far_work,
        "last_far",
    )(low, far_next, z_low, m_low, v_low, aims_far, known_far, inside, *handed, *weights, *ready)


def solution(mesh):
    tile = P(("parts", "row", "cores"), "col", None)
    return jax.shard_map(
        body,
        mesh=mesh,
        in_specs=(
            tile,
            tile,
            tile,
            P(("parts", "row", "cores"), "col"),
            P(None, ("parts", "row", "cores"), "col"),
            P(),
            P(),
            P(),
            P(),
            P(),
        ),
        out_specs=(tile, tile, tile),
        check_vma=False,
    )
```
